32 devices in a mesh: dp: 16 (over z, y, x), tensor: 2 (over core).
Axes of the slice: x: 2, y: 2, z: 4, core: 2. Of those that a mesh axis runs over, the one named last changes fastest.
Arguments:
- normed: bfloat16 [3072, 8192], P('dp', 'tensor'), may hold values from -6 to 6
- stored_queries: bfloat16 [3072, 4096], P('dp', 'tensor'), may hold values from -170 to 170
- stored_keys: bfloat16 [3072, 1024], P('dp', 'tensor'), may hold values from -7 to 7
- stored_values: bfloat16 [3072, 1024], P('dp', 'tensor'), may hold values from -6 to 6
- head_output_grad: bfloat16 [3072, 4096], P('dp', 'tensor'), may hold values from -6 to 6
- document_index: int32 [16, 192], P('dp'), may hold values from 0 to 7, never falling along the last dimension, each value on 1 to 72 neighbouring positions
- query_projection_weight: bfloat16 [8192, 4096], P('dp', 'tensor'), may hold values from -0.0625 to 0.0625
- key_projection_weight: bfloat16 [8192, 1024], P('dp', 'tensor'), may hold values from -0.0625 to 0.0625
- value_projection_weight: bfloat16 [8192, 1024], P('dp', 'tensor'), may hold values from -0.0625 to 0.0625
- adapter_down_maps: bfloat16 [8192, 192], P('tensor'), may hold values from -0.0625 to 0.0625
- query_up_map: bfloat16 [64, 4096], P(None, 'tensor'), may hold values from -0.75 to 0.75
- key_value_up_maps: bfloat16 [2, 64, 1024], P(None, None, 'tensor'), may hold values from -0.75 to 0.75
Outputs:
- normed_input_grad: bfloat16 [3072, 8192], P('dp', 'tensor')
- down_grad: float32 [8192, 192], P('tensor')
- query_up_grad: float32 [64, 4096], P(None, 'tensor')
- key_value_up_grad: float32 [2, 64, 1024], P(None, None, 'tensor')
The draws below stay inside these ranges and needn't reach their ends.
All inputs are finite; a program needn't handle non-finite values.
Results may differ from the reference program's by a relative error of at most 0.0095.
Values may be sent and summed in bfloat16 or wider, within the bound.
No kernel may reach another device: no remote copies, remote signals or barrier semaphores. Data moves between devices by JAX's collectives and lax.ppermute only.
A program may use at most 192 MiB of HBM per device.

```python
import math
import jax
import jax.numpy as jnp
import numpy as np
from jax import lax

MODEL_WIDTH = 8192
QUERY_HEADS = 32
KEY_HEADS = 8
HEAD_SIZE = 128
ADAPTER_RANK = 64
ROW_TOKENS = 192
DOCS = 8
MOST = 72
ROWS = 16
TOKEN_TOTAL = 3072
QUERY_WIDTH = 4096
KVW = 1024
N_TENSOR = 2


def paired_draw(key):
    base_keys = jnp.clip(jax.random.normal(jax.random.fold_in(key, 11), (TOKEN_TOTAL, KVW), jnp.float32), -6.0, 6.0)
    base_queries = jnp.clip(jax.random.normal(jax.random.fold_in(key, 12), (TOKEN_TOTAL, QUERY_WIDTH), jnp.float32), -6.0, 6.0)
    return (base_queries, base_keys)


def draw_stored_queries(key, part):
    return paired_draw(key)[0].astype(jnp.bfloat16)


def draw_stored_keys(key, part):
    return paired_draw(key)[1].astype(jnp.bfloat16)


def levels(own_key, shape, cuts, smallest, high):
    def one(position, parts):
        draws = jax.random.uniform(jax.random.fold_in(jax.random.fold_in(own_key, 6), position), (parts,), jnp.float32, smallest / len(cuts), high / len(cuts))
        return jnp.repeat(jnp.exp(draws), shape[position] // parts).reshape((-1,) + (1,) * (len(shape) - position - 1))

    level = one(*cuts[0])
    for cut in cuts[1:]:
        level = level * one(*cut)
    return level


def profile(number_of, total, reach, skew):
    weights = [(1 << 20) // math.isqrt(grade ** skew) + 1 for grade in range(2, number_of + 1)]
    rest, holding = total - reach - (number_of - 1), [1] * (number_of - 1)
    while rest > 0:
        movable = [i for i in range(number_of - 1) if holding[i] < reach]
        pool, budget = sum([weights[i] for i in movable]), rest
        for i in movable:
            addition = min(reach - holding[i], max(1, budget * weights[i] // pool), rest)
            holding[i] = holding[i] + addition
            rest = rest - addition
    return np.array([reach] + holding)


def uneven_parts(stream_key, number_of, total, most, lean):
    if number_of == 2:
        one = jax.random.randint(stream_key, (), max(1, total - most), min(most, total - 1) + 1)
        return jnp.stack([one, total - one])
    lengths = jnp.asarray(profile(number_of, total, most, lean), jnp.int32)
    twos = (number_of - 1) // 2
    donor, receiver = lengths[1:1 + 2 * twos:2], lengths[2:2 + 2 * twos:2]
    room = jnp.minimum(donor - 1, most - receiver)
    moved = jax.random.randint(jax.random.fold_in(stream_key, 1), (twos,), 0, 1 << 20) % (room + 1)
    lengths = lengths.at[1:1 + 2 * twos:2].set(donor - moved).at[2:2 + 2 * twos:2].set(receiver + moved)
    return lengths[jax.random.permutation(jax.random.fold_in(stream_key, 2), number_of)]


def bell_draw(key, shape, deviation, limit, split=(), kind=jnp.bfloat16):
    factor_of = levels(key, shape, split, -0.22, 0.18) if split else 1.0
    result = jax.random.normal(key, shape, jnp.float32) * deviation * factor_of
    return jnp.minimum(jnp.maximum(result, -limit), limit).astype(kind)


def setup_inputs(seed: int = 0) -> dict:
    arg_keys = jax.random.split(jax.random.key(seed), 13)
    normed = bell_draw(arg_keys[0], (TOKEN_TOTAL, MODEL_WIDTH), 1.0, 6.0, ((0, 16), (1, 2)))
    stored_queries = draw_stored_queries(jax.random.fold_in(arg_keys[12], 71), 0)
    stored_keys = draw_stored_keys(jax.random.fold_in(arg_keys[12], 71), 0)
    stored_values = bell_draw(arg_keys[3], (TOKEN_TOTAL, KVW), 1.0, 6.0, ((0, 16), (1, 2)))
    head_output_grad = bell_draw(arg_keys[4], (TOKEN_TOTAL, QUERY_WIDTH), 1.0, 6.0, ((0, 16), (1, 2)))
    document_index = jax.vmap(lambda own: jnp.searchsorted(jnp.cumsum(uneven_parts(own, DOCS, ROW_TOKENS, MOST, 2)), jnp.arange(ROW_TOKENS), side="right"))(jax.random.split(arg_keys[5], ROWS)).reshape((ROWS, ROW_TOKENS)).astype(jnp.int32)
    query_projection_weight = bell_draw(arg_keys[6], (MODEL_WIDTH, QUERY_WIDTH), MODEL_WIDTH ** -0.5, 0.0625, ((0, 16), (1, 2)))
    key_projection_weight = bell_draw(arg_keys[7], (MODEL_WIDTH, KVW), MODEL_WIDTH ** -0.5, 0.0625, ((0, 16), (1, 2)))
    value_projection_weight = bell_draw(arg_keys[8], (MODEL_WIDTH, KVW), MODEL_WIDTH ** -0.5, 0.0625, ((0, 16), (1, 2)))
    adapter_down_maps = bell_draw(arg_keys[9], (MODEL_WIDTH, 3 * ADAPTER_RANK), MODEL_WIDTH ** -0.5, 0.0625, ((0, 2),))
    query_up_map = bell_draw(arg_keys[10], (ADAPTER_RANK, QUERY_WIDTH), ADAPTER_RANK ** -0.5, 0.75, ((1, 2),))
    key_value_up_maps = bell_draw(arg_keys[11], (2, ADAPTER_RANK, KVW), ADAPTER_RANK ** -0.5, 0.75, ((2, 2),))
    return dict(normed=normed, stored_queries=stored_queries, stored_keys=stored_keys, stored_values=stored_values, head_output_grad=head_output_grad, document_index=document_index, query_projection_weight=query_projection_weight, key_projection_weight=key_projection_weight, value_projection_weight=value_projection_weight, adapter_down_maps=adapter_down_maps, query_up_map=query_up_map, key_value_up_maps=key_value_up_maps)


adapter_scale = 0.5

def row_backward(packed):
    query_slice, key_row_slice, value_row_slice, output_gradient, ids = packed
    query_group = QUERY_HEADS // KEY_HEADS
    scale = 1.0 / math.sqrt(HEAD_SIZE)
    query_float = query_slice.astype(jnp.float32).reshape(ROW_TOKENS, KEY_HEADS, query_group, HEAD_SIZE)
    key_float = key_row_slice.astype(jnp.float32).reshape(ROW_TOKENS, KEY_HEADS, HEAD_SIZE)
    value_float = value_row_slice.astype(jnp.float32).reshape(ROW_TOKENS, KEY_HEADS, HEAD_SIZE)
    output_float = output_gradient.astype(jnp.float32).reshape(ROW_TOKENS, KEY_HEADS, query_group, HEAD_SIZE)
    same = ids[:, None] == ids[None, :]
    scores = jnp.einsum('bmav,wmv->mabw', query_float, key_float) * scale
    scores = jnp.where(same[None, None], scores, -1e+30)
    probs = jax.nn.softmax(scores, axis=-1)
    probs_half = probs.astype(jnp.bfloat16).astype(jnp.float32)
    value_gradient = jnp.einsum('kgtu,tkgd->ukd', probs_half, output_float).astype(jnp.bfloat16)
    probability_grad = jnp.einsum('bmav,wmv->mabw', output_float, value_float)
    row_dots = lax.optimization_barrier(jnp.sum(probs * probability_grad, axis=-1, keepdims=True))
    score_grad = (probs * (probability_grad - row_dots) * scale).astype(jnp.bfloat16).astype(jnp.float32)
    query_gradient = jnp.einsum('kgtu,ukd->tkgd', score_grad, key_float).astype(jnp.bfloat16)
    key_gradient = jnp.einsum('kgtu,tkgd->ukd', score_grad, query_float).astype(jnp.bfloat16)
    return (query_gradient.reshape(ROW_TOKENS, QUERY_WIDTH), key_gradient.reshape(ROW_TOKENS, KVW), value_gradient.reshape(ROW_TOKENS, KVW))

def reference(normed, stored_queries, stored_keys, stored_values, head_output_grad, document_index, query_projection_weight, key_projection_weight, value_projection_weight, adapter_down_maps, query_up_map, key_value_up_maps):
    packed = (stored_queries.reshape(ROWS, ROW_TOKENS, QUERY_WIDTH), stored_keys.reshape(ROWS, ROW_TOKENS, KVW), stored_values.reshape(ROWS, ROW_TOKENS, KVW), head_output_grad.reshape(ROWS, ROW_TOKENS, QUERY_WIDTH), document_index)
    query_gradient, key_gradient, value_gradient = lax.map(row_backward, packed)
    query_gradient = query_gradient.reshape(TOKEN_TOTAL, QUERY_WIDTH)
    key_gradient = key_gradient.reshape(TOKEN_TOTAL, KVW)
    value_gradient = value_gradient.reshape(TOKEN_TOTAL, KVW)
    adapter_middle = jnp.dot(normed, adapter_down_maps, preferred_element_type=jnp.float32).astype(jnp.bfloat16)
    middle_gradient = jnp.concatenate([adapter_scale * jnp.dot(query_gradient, query_up_map.T, preferred_element_type=jnp.float32), adapter_scale * jnp.dot(key_gradient, key_value_up_maps[0].T, preferred_element_type=jnp.float32), adapter_scale * jnp.dot(value_gradient, key_value_up_maps[1].T, preferred_element_type=jnp.float32)], axis=1).astype(jnp.bfloat16)
    query_cols = QUERY_WIDTH // N_TENSOR
    key_cols = KVW // N_TENSOR
    base_offset = jnp.zeros((TOKEN_TOTAL, MODEL_WIDTH), jnp.float32)
    for shard in range(N_TENSOR):
        qpart = slice(shard * query_cols, (shard + 1) * query_cols)
        kpart = slice(shard * key_cols, (shard + 1) * key_cols)
        term = jnp.dot(query_gradient[:, qpart], query_projection_weight[:, qpart].T, preferred_element_type=jnp.float32)
        term = term + jnp.dot(key_gradient[:, kpart], key_projection_weight[:, kpart].T, preferred_element_type=jnp.float32)
        term = term + jnp.dot(value_gradient[:, kpart], value_projection_weight[:, kpart].T, preferred_element_type=jnp.float32)
        rounded = lax.optimization_barrier(term.astype(jnp.bfloat16))
        base_offset = base_offset + rounded.astype(jnp.float32)
    normed_input_grad = (base_offset + jnp.dot(middle_gradient, adapter_down_maps.T, preferred_element_type=jnp.float32)).astype(jnp.bfloat16)
    down_grad = jnp.dot(normed.T, middle_gradient, preferred_element_type=jnp.float32)
    query_up_grad = adapter_scale * jnp.dot(adapter_middle[:, 0:ADAPTER_RANK].T, query_gradient, preferred_element_type=jnp.float32)
    key_value_up_grad = jnp.stack([adapter_scale * jnp.dot(adapter_middle[:, ADAPTER_RANK:2 * ADAPTER_RANK].T, key_gradient, preferred_element_type=jnp.float32), adapter_scale * jnp.dot(adapter_middle[:, 2 * ADAPTER_RANK:3 * ADAPTER_RANK].T, value_gradient, preferred_element_type=jnp.float32)])
    return (normed_input_grad, down_grad, query_up_grad, key_value_up_grad)
```

```python
import math

import jax
import jax.numpy as jnp
from jax import lax
from jax.sharding import Mesh
from jax.sharding import PartitionSpec as P

QUERY_HEADS = 32
KEY_HEADS = 8
HEAD_SIZE = 128
ADAPTER_RANK = 64


adapter_scale = 0.5


def attention_backward(queries, keyrows, value_row_block, output_gradient, ids):
    token_count = queries.shape[0]
    key_value_heads = keyrows.shape[1] // HEAD_SIZE
    query_group = QUERY_HEADS // KEY_HEADS
    scale = 1.0 / math.sqrt(HEAD_SIZE)
    qmat = queries.reshape(token_count, key_value_heads, query_group, HEAD_SIZE)
    kmat = keyrows.reshape(token_count, key_value_heads, HEAD_SIZE)
    value_matrix = value_row_block.reshape(token_count, key_value_heads, HEAD_SIZE)
    output_matrix = output_gradient.reshape(token_count, key_value_heads, query_group, HEAD_SIZE)
    same = ids[:, None] == ids[None, :]
    scores = jnp.einsum("bmav,wmv->mabw", qmat, kmat, preferred_element_type=jnp.float32) * scale
    scores = jnp.where(same[None, None], scores, -1e30)
    probs = jax.nn.softmax(scores, axis=-1)
    probs_half = probs.astype(jnp.bfloat16)
    value_gradient = jnp.einsum(
        "kgtu,tkgd->ukd", probs_half, output_matrix, preferred_element_type=jnp.float32
    ).astype(jnp.bfloat16)
    probability_grad = jnp.einsum(
        "bmav,wmv->mabw", output_matrix, value_matrix, preferred_element_type=jnp.float32
    )
    row_dots = jnp.sum(probs * probability_grad, axis=-1, keepdims=True)
    score_grad = (probs * (probability_grad - row_dots) * scale).astype(jnp.bfloat16)
    query_gradient = jnp.einsum(
        "kgtu,ukd->tkgd", score_grad, kmat, preferred_element_type=jnp.float32
    ).astype(jnp.bfloat16)
    key_gradient = jnp.einsum(
        "kgtu,tkgd->ukd", score_grad, qmat, preferred_element_type=jnp.float32
    ).astype(jnp.bfloat16)
    return (
        query_gradient.reshape(token_count, -1),
        key_gradient.reshape(token_count, -1),
        value_gradient.reshape(token_count, -1),
    )


def rows_product(left, piece):
    return lax.dot_general(
        left, piece, (((1,), (1,)), ((), ())), preferred_element_type=jnp.float32
    )


def up_gradients(adapter_middle, query_gradient, key_gradient, value_gradient):
    rank = ADAPTER_RANK
    parts = []
    for place, gradient in enumerate((query_gradient, key_gradient, value_gradient)):
        parts.append(
            adapter_scale
            * lax.dot_general(
                adapter_middle[:, place * rank : (place + 1) * rank],
                gradient,
                (((0,), (0,)), ((), ())),
                preferred_element_type=jnp.float32,
            )
        )
    return parts


def make_shards(outer, inner, tensor):
    every = ("hi", "lo")

    def shards(
        normed,
        stored_queries,
        stored_keys,
        stored_values,
        head_output_grad,
        document_index,
        query_projection_weight,
        key_projection_weight,
        value_projection_weight,
        adapter_down_maps,
        query_up_map,
        key_value_up_maps,
    ):
        weights = lax.all_gather(
            jnp.concatenate(
                [query_projection_weight, key_projection_weight, value_projection_weight], axis=1
            ),
            "lo",
            axis=0,
            tiled=True,
        )
        query_gradient, key_gradient, value_gradient = attention_backward(
            stored_queries, stored_keys, stored_values, head_output_grad, document_index[0]
        )
        own = jnp.concatenate([query_gradient, key_gradient, value_gradient], axis=1)
        gathered = lax.all_gather(own, "hi", axis=0, tiled=True)
        local_middle = jnp.dot(normed, adapter_down_maps, preferred_element_type=jnp.float32)
        grad_local = jnp.concatenate(
            [
                adapter_scale * rows_product(query_gradient, query_up_map),
                adapter_scale * rows_product(key_gradient, key_value_up_maps[0]),
                adapter_scale * rows_product(value_gradient, key_value_up_maps[1]),
            ],
            axis=1,
        )
        middle_total, grad_sum = (
            lax.psum(local_middle.astype(jnp.bfloat16), "tensor").astype(jnp.float32),
            lax.psum(grad_local.astype(jnp.bfloat16), "tensor").astype(jnp.float32),
        )
        adapter_middle = middle_total.astype(jnp.bfloat16)
        middle_gradient = grad_sum.astype(jnp.bfloat16)

        down_local = lax.dot_general(
            normed, middle_gradient, (((0,), (0,)), ((), ())), preferred_element_type=jnp.float32
        )
        ups = up_gradients(adapter_middle, query_gradient, key_gradient, value_gradient)
        up_local = jnp.concatenate(ups, axis=1)
        down_piece = lax.psum_scatter(down_local, every, scatter_dimension=0, tiled=True)
        up_piece = lax.psum_scatter(up_local, every, scatter_dimension=1, tiled=True)
        down_total = lax.all_gather(down_piece, every, axis=0, tiled=True)
        up_total = lax.all_gather(up_piece, every, axis=1, tiled=True)
        q_width = query_gradient.shape[1]
        k_width = key_gradient.shape[1]
        query_total = up_total[:, :q_width]
        key_value_total = jnp.stack(
            [up_total[:, q_width : q_width + k_width], up_total[:, q_width + k_width :]]
        )

        term = rows_product(gathered, weights).astype(jnp.bfloat16)
        tokens = own.shape[0]
        block = weights.shape[0]
        summed = lax.psum_scatter(term, "tensor", scatter_dimension=1, tiled=True)
        piece = block // tensor
        moved = lax.all_to_all(
            summed.reshape(outer, tokens, piece), "hi", split_axis=0, concat_axis=0, tiled=True
        )
        moved = moved.reshape(tensor, outer // tensor, tokens, piece)
        moved = lax.all_to_all(moved, "tensor", split_axis=0, concat_axis=0, tiled=True)
        base = moved.transpose(2, 1, 0, 3).reshape(tokens, -1).astype(jnp.float32)
        normed_input_grad = (base + rows_product(middle_gradient, adapter_down_maps)).astype(
            jnp.bfloat16
        )
        return (normed_input_grad, down_total, query_total, key_value_total)

    return shards


def solution(mesh):
    ranks = mesh.shape["dp"]
    tensor = mesh.shape["tensor"]
    inner = math.gcd(ranks, 4)
    outer = ranks // inner
    split = Mesh(mesh.devices.reshape(outer, inner, tensor), ("hi", "lo", "tensor"))
    rows = ("hi", "lo")
    in_specs = (
        P(rows, "tensor"),
        P(rows, "tensor"),
        P(rows, "tensor"),
        P(rows, "tensor"),
        P(rows, "tensor"),
        P(rows, None),
        P(rows, "tensor"),
        P(rows, "tensor"),
        P(rows, "tensor"),
        P("tensor", None),
        P(None, "tensor"),
        P(None, None, "tensor"),
    )
    out_specs = (P(rows, "tensor"), P("tensor", None), P(None, "tensor"), P(None, None, "tensor"))
    return jax.shard_map(
        make_shards(outer, inner, tensor),
        mesh=split,
        in_specs=in_specs,
        out_specs=out_specs,
        check_vma=False,
    )
```

```python
import math

import jax
import jax.numpy as jnp
from jax import lax
from jax.experimental import pallas as pl
from jax.experimental.pallas import tpu as pltpu
from jax.sharding import Mesh
from jax.sharding import PartitionSpec as P

QUERY_HEADS = 32
KEY_HEADS = 8
HEAD_SIZE = 128
ADAPTER_RANK = 64


adapter_scale = 0.5


def attention_backward(queries, keyrows, value_row_block, output_gradient, ids):
    token_count = queries.shape[0]
    key_value_heads = keyrows.shape[1] // HEAD_SIZE
    query_group = QUERY_HEADS // KEY_HEADS
    scale = 1.0 / math.sqrt(HEAD_SIZE)
    qmat = queries.reshape(token_count, key_value_heads, query_group, HEAD_SIZE)
    kmat = keyrows.reshape(token_count, key_value_heads, HEAD_SIZE)
    value_matrix = value_row_block.reshape(token_count, key_value_heads, HEAD_SIZE)
    output_matrix = output_gradient.reshape(token_count, key_value_heads, query_group, HEAD_SIZE)
    same = ids[:, None] == ids[None, :]
    scores = jnp.einsum("bmav,wmv->mabw", qmat, kmat, preferred_element_type=jnp.float32) * scale
    scores = jnp.where(same[None, None], scores, -1e30)
    probs = jax.nn.softmax(scores, axis=-1)
    probs_half = probs.astype(jnp.bfloat16)
    value_gradient = jnp.einsum(
        "kgtu,tkgd->ukd", probs_half, output_matrix, preferred_element_type=jnp.float32
    ).astype(jnp.bfloat16)
    probability_grad = jnp.einsum(
        "bmav,wmv->mabw", output_matrix, value_matrix, preferred_element_type=jnp.float32
    )
    row_dots = jnp.sum(probs * probability_grad, axis=-1, keepdims=True)
    score_grad = (probs * (probability_grad - row_dots) * scale).astype(jnp.bfloat16)
    query_gradient = jnp.einsum(
        "kgtu,ukd->tkgd", score_grad, kmat, preferred_element_type=jnp.float32
    ).astype(jnp.bfloat16)
    key_gradient = jnp.einsum(
        "kgtu,tkgd->ukd", score_grad, qmat, preferred_element_type=jnp.float32
    ).astype(jnp.bfloat16)
    return (
        query_gradient.reshape(token_count, -1),
        key_gradient.reshape(token_count, -1),
        value_gradient.reshape(token_count, -1),
    )


def rows_product(left, piece):
    return lax.dot_general(
        left, piece, (((1,), (1,)), ((), ())), preferred_element_type=jnp.float32
    )


def up_gradients(adapter_middle, query_gradient, key_gradient, value_gradient):
    rank = ADAPTER_RANK
    parts = []
    for place, gradient in enumerate((query_gradient, key_gradient, value_gradient)):
        parts.append(
            adapter_scale
            * lax.dot_general(
                adapter_middle[:, place * rank : (place + 1) * rank],
                gradient,
                (((0,), (0,)), ((), ())),
                preferred_element_type=jnp.float32,
            )
        )
    return parts


def general_shards(outer, inner, tensor):
    every = ("hi", "lo")

    def shards(
        normed,
        stored_queries,
        stored_keys,
        stored_values,
        head_output_grad,
        document_index,
        query_projection_weight,
        key_projection_weight,
        value_projection_weight,
        adapter_down_maps,
        query_up_map,
        key_value_up_maps,
    ):
        weights = lax.all_gather(
            jnp.concatenate(
                [query_projection_weight, key_projection_weight, value_projection_weight], axis=1
            ),
            "lo",
            axis=0,
            tiled=True,
        )
        query_gradient, key_gradient, value_gradient = attention_backward(
            stored_queries, stored_keys, stored_values, head_output_grad, document_index[0]
        )
        own = jnp.concatenate([query_gradient, key_gradient, value_gradient], axis=1)
        gathered = lax.all_gather(own, "hi", axis=0, tiled=True)
        local_middle = jnp.dot(normed, adapter_down_maps, preferred_element_type=jnp.float32)
        grad_local = jnp.concatenate(
            [
                adapter_scale * rows_product(query_gradient, query_up_map),
                adapter_scale * rows_product(key_gradient, key_value_up_maps[0]),
                adapter_scale * rows_product(value_gradient, key_value_up_maps[1]),
            ],
            axis=1,
        )
        middle_total, grad_sum = (
            lax.psum(local_middle.astype(jnp.bfloat16), "tensor").astype(jnp.float32),
            lax.psum(grad_local.astype(jnp.bfloat16), "tensor").astype(jnp.float32),
        )
        adapter_middle = middle_total.astype(jnp.bfloat16)
        middle_gradient = grad_sum.astype(jnp.bfloat16)

        down_local = lax.dot_general(
            normed, middle_gradient, (((0,), (0,)), ((), ())), preferred_element_type=jnp.float32
        )
        ups = up_gradients(adapter_middle, query_gradient, key_gradient, value_gradient)
        up_local = jnp.concatenate(ups, axis=1)
        down_piece = lax.psum_scatter(down_local, every, scatter_dimension=0, tiled=True)
        up_piece = lax.psum_scatter(up_local, every, scatter_dimension=1, tiled=True)
        down_total = lax.all_gather(down_piece, every, axis=0, tiled=True)
        up_total = lax.all_gather(up_piece, every, axis=1, tiled=True)
        q_width = query_gradient.shape[1]
        k_width = key_gradient.shape[1]
        query_total = up_total[:, :q_width]
        key_value_total = jnp.stack(
            [up_total[:, q_width : q_width + k_width], up_total[:, q_width + k_width :]]
        )

        term = rows_product(gathered, weights).astype(jnp.bfloat16)
        tokens = own.shape[0]
        block = weights.shape[0]
        summed = lax.psum_scatter(term, "tensor", scatter_dimension=1, tiled=True)
        piece = block // tensor
        moved = lax.all_to_all(
            summed.reshape(outer, tokens, piece), "hi", split_axis=0, concat_axis=0, tiled=True
        )
        moved = moved.reshape(tensor, outer // tensor, tokens, piece)
        moved = lax.all_to_all(moved, "tensor", split_axis=0, concat_axis=0, tiled=True)
        base = moved.transpose(2, 1, 0, 3).reshape(tokens, -1).astype(jnp.float32)
        normed_input_grad = (base + rows_product(middle_gradient, adapter_down_maps)).astype(
            jnp.bfloat16
        )
        return (normed_input_grad, down_total, query_total, key_value_total)

    return shards


SIZES = (4, 4, 2)
AXES = ("hi", "lo", "tensor")


def send(value, target):
    pairs = []
    for rank in range(32):
        hi, lo, core = rank // 8, rank // 2 % 4, rank % 2
        there = target(hi, lo, core)
        if there is not None:
            pairs.append((rank, there[0] * 8 + there[1] * 2 + there[2]))
    return lax.ppermute(value, AXES, pairs)


def swap_lo(value, bit):
    return send(value, lambda hi, lo, core: (hi, lo ^ bit, core))


def swap_core(value):
    return send(value, lambda hi, lo, core: (hi, lo, 1 - core))


def turn_hi(value, step):
    return send(value, lambda hi, lo, core: ((hi + step) % 4, lo, core))


def move_hi(value, step, first, last):
    return send(
        value,
        lambda hi, lo, core: (hi + step, lo, core) if first <= hi <= last else None,
    )


def pick(value, index, axis):
    return lax.dynamic_index_in_dim(value, index, axis, keepdims=False)


def term_kernel(turn_ref, a0, a1, a2, a3, right_ref, out_ref, left, arrived):
    del turn_ref
    tokens = a0.shape[0]

    @pl.when(pl.program_id(0) == 0)
    def _():
        copies = [
            pltpu.make_async_copy(a, left.at[pl.ds(n * tokens, tokens), :], arrived.at[n])
            for n, a in enumerate((a0, a1, a2, a3))
        ]
        for copy in copies:
            copy.start()
        for copy in copies:
            copy.wait()

    out_ref[...] = lax.dot_general(
        left[...],
        right_ref[...],
        (((1,), (1,)), ((), ())),
        preferred_element_type=jnp.float32,
    ).astype(jnp.bfloat16)[None]


def term_halves(slots, weights, core):
    tokens, depth = slots[0].shape
    rows = weights.shape[0] // 2
    return pl.pallas_call(
        term_kernel,
        out_shape=jax.ShapeDtypeStruct((2, 4 * tokens, rows), jnp.bfloat16),
        grid_spec=pltpu.PrefetchScalarGridSpec(
            num_scalar_prefetch=1,
            grid=(2,),
            in_specs=[pl.BlockSpec(memory_space=pl.ANY)] * 4
            + [pl.BlockSpec((rows, depth), lambda i, turn: (lax.rem(turn[0] + 1 - i, 2), 0))],
            out_specs=pl.BlockSpec((1, 4 * tokens, rows), lambda i, turn: (1 - i, 0, 0)),
            scratch_shapes=[
                pltpu.VMEM((4 * tokens, depth), jnp.bfloat16),
                pltpu.SemaphoreType.DMA((4,)),
            ],
        ),
        compiler_params=pltpu.CompilerParams(vmem_limit_bytes=40 << 20),
        cost_estimate=pl.CostEstimate(
            flops=16 * tokens * depth * rows,
            bytes_accessed=8 * tokens * depth + 4 * rows * depth + 16 * tokens * rows,
            transcendentals=0,
        ),
        name="term",
    )(core[None], *slots, weights)


def finish_kernel(order_ref, piece_ref, middle_ref, down_ref, out_ref):
    del order_ref
    added = lax.dot_general(
        middle_ref[...],
        down_ref[...],
        (((1,), (1,)), ((), ())),
        preferred_element_type=jnp.float32,
    )
    out_ref[...] = (piece_ref[0].astype(jnp.float32) + added).astype(jnp.bfloat16)


def finish(pieces, order, middle_gradient, down_maps, width):
    tokens = pieces.shape[1]
    columns = down_maps.shape[0]
    rank = middle_gradient.shape[1]
    each = pieces.shape[2] // width
    return pl.pallas_call(
        finish_kernel,
        out_shape=jax.ShapeDtypeStruct((tokens, columns), jnp.bfloat16),
        grid_spec=pltpu.PrefetchScalarGridSpec(
            num_scalar_prefetch=1,
            grid=(columns // width,),
            in_specs=[
                pl.BlockSpec(
                    (1, tokens, width),
                    lambda c, order: (lax.div(order[c], each), 0, lax.rem(order[c], each)),
                ),
                pl.BlockSpec((tokens, rank), lambda c, order: (0, 0)),
                pl.BlockSpec((width, rank), lambda c, order: (c, 0)),
            ],
            out_specs=pl.BlockSpec((tokens, width), lambda c, order: (0, c)),
        ),
        cost_estimate=pl.CostEstimate(
            flops=2 * tokens * columns * rank,
            bytes_accessed=4 * tokens * columns + 2 * columns * rank,
            transcendentals=0,
        ),
        name="finish",
    )(order, pieces, middle_gradient, down_maps)


def plane_scatter(value, bits):
    lo = lax.axis_index("lo")
    for bit in bits:
        mine = (lo // bit) % 2
        axis = 2 if bit == 1 and value.ndim == 5 else 1
        sent = pick(value, 1 - mine, axis).astype(jnp.bfloat16)
        value = pick(value, mine, axis) + swap_lo(sent, bit).astype(jnp.float32)
    return value


def dp_pieces(down_local, up_local):
    rows, rank = down_local.shape
    return jnp.concatenate(
        [
            down_local.reshape(16, rows // 16, rank),
            up_local.reshape(-1, 16, rank).transpose(1, 0, 2),
        ],
        axis=1,
    )


def dp_scatter(pieces):
    hi = lax.axis_index("hi")
    pieces = pieces.reshape(4, 2, 2, *pieces.shape[1:])
    column = jnp.concatenate(
        [plane_scatter(pieces[:2], (1, 2)), plane_scatter(pieces[2:], (2, 1))], axis=0
    )
    total = pick(column, hi, 0)
    for step in range(1, 4):
        sent = pick(column, (hi + step) % 4, 0).astype(jnp.bfloat16)
        total = total + turn_hi(sent, step).astype(jnp.float32)
    return total.astype(jnp.bfloat16)


def gather_hi(own):
    hi = lax.axis_index("hi")
    right, left = [own], [own]
    for step in range(1, 4):
        right.append(move_hi(right[-1], 1, step - 1, 2))
        left.append(move_hi(left[-1], -1, 1, 4 - step))
    slots = [
        own,
        jnp.where(hi == 3, right[1], left[1]),
        jnp.where(hi < 2, left[2], right[2]),
        jnp.where(hi == 0, left[3], jnp.where(hi == 3, right[3], right[1])),
    ]
    table = jnp.array([[0, 1, 2, 3], [3, 0, 1, 2], [2, 3, 0, 1], [3, 2, 1, 0]], jnp.int32)
    return slots, pick(table, hi, 0)


def fast_shards():
    def shards(
        normed,
        stored_queries,
        stored_keys,
        stored_values,
        head_output_grad,
        document_index,
        query_projection_weight,
        key_projection_weight,
        value_projection_weight,
        adapter_down_maps,
        query_up_map,
        key_value_up_maps,
    ):
        hi, lo, core = (lax.axis_index(name) for name in AXES)
        own_weights = jnp.concatenate(
            [query_projection_weight, key_projection_weight, value_projection_weight], axis=1
        )
        cut = own_weights.shape[0] // 2
        weights = []
        for part in range(2):
            rows = own_weights[part * cut : (part + 1) * cut]
            weights.append(lax.all_gather(rows, "lo", axis=0, tiled=True))

        query_gradient, key_gradient, value_gradient = attention_backward(
            stored_queries, stored_keys, stored_values, head_output_grad, document_index[0]
        )
        own = jnp.concatenate([query_gradient, key_gradient, value_gradient], axis=1)
        slots, slot_of = gather_hi(own)

        middle_local = jnp.concatenate(
            [
                jnp.dot(normed, adapter_down_maps, preferred_element_type=jnp.float32),
                adapter_scale * rows_product(query_gradient, query_up_map),
                adapter_scale * rows_product(key_gradient, key_value_up_maps[0]),
                adapter_scale * rows_product(value_gradient, key_value_up_maps[1]),
            ],
            axis=1,
        )
        middle = (middle_local + swap_core(middle_local)).astype(jnp.bfloat16)
        rank = adapter_down_maps.shape[1]
        adapter_middle, middle_gradient = middle[:, :rank], middle[:, rank:]
        down_local = lax.dot_general(
            normed, middle_gradient, (((0,), (0,)), ((), ())), preferred_element_type=jnp.float32
        )
        ups = up_gradients(adapter_middle, query_gradient, key_gradient, value_gradient)
        piece = dp_scatter(dp_pieces(down_local, jnp.concatenate(ups, axis=1)))
        piece = lax.optimization_barrier((piece, weights[1]))[0]
        every = lax.all_gather(piece, ("hi", "lo"), axis=0)
        down_rows = down_local.shape[0]
        down_total = every[:, : down_rows // 16].reshape(down_rows, rank).astype(jnp.float32)
        up_total = every[:, down_rows // 16 :].transpose(1, 0, 2).reshape(ADAPTER_RANK, -1)
        up_total = up_total.astype(jnp.float32)
        q_width = query_gradient.shape[1]
        k_width = key_gradient.shape[1]
        query_total = up_total[:, :q_width]
        key_value_total = jnp.stack(
            [up_total[:, q_width : q_width + k_width], up_total[:, q_width + k_width :]]
        )

        tokens = own.shape[0]
        source = (hi % 2) * 2 + core

        def owner(step):
            return lambda hi, lo, core: (((hi % 2) * 2 + core + step) % 4, lo, hi // 2)

        received = []
        for part in range(2):
            halves = term_halves(slots, weights[part], core)
            other = swap_core(halves[1])
            summed = halves[0].astype(jnp.float32) + other.astype(jnp.float32)
            summed = summed.astype(jnp.bfloat16).reshape(4, tokens, -1)
            for step in range(4):
                there = pick(slot_of, (source + step) % 4, 0)
                received.append(send(pick(summed, there, 0), owner(step)))
        pieces = jnp.stack(received)
        spot = jnp.arange(16, dtype=jnp.int32)
        from_hi, from_lo, part = spot // 8, spot // 2 % 4, spot % 2
        step = (hi - (from_hi * 2 + from_lo // 2)) % 4
        order = ((part * 4 + step) * 2 + from_lo % 2).astype(jnp.int32)
        normed_input_grad = finish(pieces, order, middle_gradient, adapter_down_maps, cut)
        return (normed_input_grad, down_total, query_total, key_value_total)

    return shards


def solution(mesh):
    ranks = mesh.shape["dp"]
    tensor = mesh.shape["tensor"]
    inner = math.gcd(ranks, 4)
    outer = ranks // inner
    split = Mesh(mesh.devices.reshape(outer, inner, tensor), AXES)
    rows = ("hi", "lo")
    in_specs = (
        P(rows, "tensor"),
        P(rows, "tensor"),
        P(rows, "tensor"),
        P(rows, "tensor"),
        P(rows, "tensor"),
        P(rows, None),
        P(rows, "tensor"),
        P(rows, "tensor"),
        P(rows, "tensor"),
        P("tensor", None),
        P(None, "tensor"),
        P(None, None, "tensor"),
    )
    out_specs = (P(rows, "tensor"), P("tensor", None), P(None, "tensor"), P(None, None, "tensor"))
    return jax.shard_map(
        fast_shards() if (outer, inner, tensor) == SIZES else general_shards(outer, inner, tensor),
        mesh=split,
        in_specs=in_specs,
        out_specs=out_specs,
        check_vma=False,
    )
```

```python
import math

import jax
import jax.numpy as jnp
from jax import lax
from jax.experimental import pallas as pl
from jax.experimental.pallas import tpu as pltpu
from jax.sharding import Mesh
from jax.sharding import PartitionSpec as P

QUERY_HEADS = 32
KEY_HEADS = 8
HEAD_SIZE = 128
ADAPTER_RANK = 64


adapter_scale = 0.5


def attention_backward(queries, keyrows, value_row_block, output_gradient, ids):
    token_count = queries.shape[0]
    key_value_heads = keyrows.shape[1] // HEAD_SIZE
    query_group = QUERY_HEADS // KEY_HEADS
    scale = 1.0 / math.sqrt(HEAD_SIZE)
    qmat = queries.reshape(token_count, key_value_heads, query_group, HEAD_SIZE)
    kmat = keyrows.reshape(token_count, key_value_heads, HEAD_SIZE)
    value_matrix = value_row_block.reshape(token_count, key_value_heads, HEAD_SIZE)
    output_matrix = output_gradient.reshape(token_count, key_value_heads, query_group, HEAD_SIZE)
    same = ids[:, None] == ids[None, :]
    scores = jnp.einsum("bmav,wmv->mabw", qmat, kmat, preferred_element_type=jnp.float32) * scale
    scores = jnp.where(same[None, None], scores, -1e30)
    probs = jax.nn.softmax(scores, axis=-1)
    probs_half = probs.astype(jnp.bfloat16)
    value_gradient = jnp.einsum(
        "kgtu,tkgd->ukd", probs_half, output_matrix, preferred_element_type=jnp.float32
    ).astype(jnp.bfloat16)
    probability_grad = jnp.einsum(
        "bmav,wmv->mabw", output_matrix, value_matrix, preferred_element_type=jnp.float32
    )
    row_dots = jnp.sum(probs * probability_grad, axis=-1, keepdims=True)
    score_grad = (probs * (probability_grad - row_dots) * scale).astype(jnp.bfloat16)
    query_gradient = jnp.einsum(
        "kgtu,ukd->tkgd", score_grad, kmat, preferred_element_type=jnp.float32
    ).astype(jnp.bfloat16)
    key_gradient = jnp.einsum(
        "kgtu,tkgd->ukd", score_grad, qmat, preferred_element_type=jnp.float32
    ).astype(jnp.bfloat16)
    return (
        query_gradient.reshape(token_count, -1),
        key_gradient.reshape(token_count, -1),
        value_gradient.reshape(token_count, -1),
    )


def rows_product(left, piece):
    return lax.dot_general(
        left, piece, (((1,), (1,)), ((), ())), preferred_element_type=jnp.float32
    )


def up_gradients(adapter_middle, query_gradient, key_gradient, value_gradient):
    rank = ADAPTER_RANK
    parts = []
    for place, gradient in enumerate((query_gradient, key_gradient, value_gradient)):
        parts.append(
            adapter_scale
            * lax.dot_general(
                adapter_middle[:, place * rank : (place + 1) * rank],
                gradient,
                (((0,), (0,)), ((), ())),
                preferred_element_type=jnp.float32,
            )
        )
    return parts


def general_shards(outer, inner, tensor):
    every = ("hi", "lo")

    def shards(
        normed,
        stored_queries,
        stored_keys,
        stored_values,
        head_output_grad,
        document_index,
        query_projection_weight,
        key_projection_weight,
        value_projection_weight,
        adapter_down_maps,
        query_up_map,
        key_value_up_maps,
    ):
        weights = lax.all_gather(
            jnp.concatenate(
                [query_projection_weight, key_projection_weight, value_projection_weight], axis=1
            ),
            "lo",
            axis=0,
            tiled=True,
        )
        query_gradient, key_gradient, value_gradient = attention_backward(
            stored_queries, stored_keys, stored_values, head_output_grad, document_index[0]
        )
        own = jnp.concatenate([query_gradient, key_gradient, value_gradient], axis=1)
        gathered = lax.all_gather(own, "hi", axis=0, tiled=True)
        local_middle = jnp.dot(normed, adapter_down_maps, preferred_element_type=jnp.float32)
        grad_local = jnp.concatenate(
            [
                adapter_scale * rows_product(query_gradient, query_up_map),
                adapter_scale * rows_product(key_gradient, key_value_up_maps[0]),
                adapter_scale * rows_product(value_gradient, key_value_up_maps[1]),
            ],
            axis=1,
        )
        middle_total, grad_sum = (
            lax.psum(local_middle.astype(jnp.bfloat16), "tensor").astype(jnp.float32),
            lax.psum(grad_local.astype(jnp.bfloat16), "tensor").astype(jnp.float32),
        )
        adapter_middle = middle_total.astype(jnp.bfloat16)
        middle_gradient = grad_sum.astype(jnp.bfloat16)

        down_local = lax.dot_general(
            normed, middle_gradient, (((0,), (0,)), ((), ())), preferred_element_type=jnp.float32
        )
        ups = up_gradients(adapter_middle, query_gradient, key_gradient, value_gradient)
        up_local = jnp.concatenate(ups, axis=1)
        down_piece = lax.psum_scatter(down_local, every, scatter_dimension=0, tiled=True)
        up_piece = lax.psum_scatter(up_local, every, scatter_dimension=1, tiled=True)
        down_total = lax.all_gather(down_piece, every, axis=0, tiled=True)
        up_total = lax.all_gather(up_piece, every, axis=1, tiled=True)
        q_width = query_gradient.shape[1]
        k_width = key_gradient.shape[1]
        query_total = up_total[:, :q_width]
        key_value_total = jnp.stack(
            [up_total[:, q_width : q_width + k_width], up_total[:, q_width + k_width :]]
        )

        term = rows_product(gathered, weights).astype(jnp.bfloat16)
        tokens = own.shape[0]
        block = weights.shape[0]
        summed = lax.psum_scatter(term, "tensor", scatter_dimension=1, tiled=True)
        piece = block // tensor
        moved = lax.all_to_all(
            summed.reshape(outer, tokens, piece), "hi", split_axis=0, concat_axis=0, tiled=True
        )
        moved = moved.reshape(tensor, outer // tensor, tokens, piece)
        moved = lax.all_to_all(moved, "tensor", split_axis=0, concat_axis=0, tiled=True)
        base = moved.transpose(2, 1, 0, 3).reshape(tokens, -1).astype(jnp.float32)
        normed_input_grad = (base + rows_product(middle_gradient, adapter_down_maps)).astype(
            jnp.bfloat16
        )
        return (normed_input_grad, down_total, query_total, key_value_total)

    return shards


SIZES = (4, 4, 2)
AXES = ("hi", "lo", "tensor")


def send(value, target):
    pairs = []
    for rank in range(32):
        hi, lo, core = rank // 8, rank // 2 % 4, rank % 2
        there = target(hi, lo, core)
        if there is not None:
            pairs.append((rank, there[0] * 8 + there[1] * 2 + there[2]))
    return lax.ppermute(value, AXES, pairs)


def after(value, first):
    return lax.optimization_barrier((value, first))[0]


def swap_lo(value, bit):
    return send(value, lambda hi, lo, core: (hi, lo ^ bit, core))


def swap_core(value):
    return send(value, lambda hi, lo, core: (hi, lo, 1 - core))


def turn_hi(value, step):
    return send(value, lambda hi, lo, core: ((hi + step) % 4, lo, core))


def move_hi(value, step, first, last):
    return send(
        value,
        lambda hi, lo, core: (hi + step, lo, core) if first <= hi <= last else None,
    )


def pick(value, index, axis):
    return lax.dynamic_index_in_dim(value, index, axis, keepdims=False)


def attention_kernel(
    query_ref, key_ref, value_ref, grad_ref, row_ids, column_ids, up_ref, key_up_ref, own_ref, middle_ref
):
    head = pl.program_id(0)
    group = query_ref.shape[1] // HEAD_SIZE
    scale = 1.0 / math.sqrt(HEAD_SIZE)
    tokens = query_ref.shape[0]

    def stacked(ref):
        return jnp.concatenate(
            [ref[:, j * HEAD_SIZE : (j + 1) * HEAD_SIZE] for j in range(group)], axis=0
        )

    def product(left, right, dims):
        return lax.dot_general(
            left, right, ((dims[:1], dims[1:]), ((), ())), preferred_element_type=jnp.float32
        )

    queries, gradients = stacked(query_ref), stacked(grad_ref)
    keys, values = key_ref[...], value_ref[...]
    same = jnp.concatenate([row_ids[...] == column_ids[...]] * group, axis=0)
    scores = jnp.where(same, product(queries, keys, (1, 1)) * scale, -1e30)
    raised = jnp.exp(scores - jnp.max(scores, axis=-1, keepdims=True))
    probs = raised / jnp.sum(raised, axis=-1, keepdims=True)
    value_gradient = product(probs.astype(jnp.bfloat16), gradients, (0, 0)).astype(jnp.bfloat16)
    prob_grad = product(gradients, values, (1, 1))
    dots = jnp.sum(probs * prob_grad, axis=-1, keepdims=True)
    score_grad = (probs * (prob_grad - dots) * scale).astype(jnp.bfloat16)
    stacked_gradient = product(score_grad, keys, (1, 0)).astype(jnp.bfloat16)
    key_gradient = product(score_grad, queries, (0, 0)).astype(jnp.bfloat16)
    query_gradient = jnp.concatenate(
        [stacked_gradient[j * tokens : (j + 1) * tokens] for j in range(group)], axis=1
    )

    count = own_ref.shape[1] // ((group + 2) * HEAD_SIZE)

    def columns(start, width):
        return pl.ds(pl.multiple_of(start, HEAD_SIZE), width)

    own_ref[:, columns(head * group * HEAD_SIZE, group * HEAD_SIZE)] = query_gradient
    own_ref[:, columns((count * group + head) * HEAD_SIZE, HEAD_SIZE)] = key_gradient
    own_ref[:, columns((count * (group + 1) + head) * HEAD_SIZE, HEAD_SIZE)] = value_gradient

    @pl.when(head == 0)
    def _():
        middle_ref[...] = jnp.zeros_like(middle_ref)

    middle_ref[...] += adapter_scale * jnp.concatenate(
        [
            product(query_gradient, up_ref[...], (1, 1)),
            product(key_gradient, key_up_ref[0], (1, 1)),
            product(value_gradient, key_up_ref[1], (1, 1)),
        ],
        axis=1,
    )


def attention(queries, keys, values, gradients, ids, query_up_map, key_value_up_maps):
    tokens, key_width = keys.shape
    heads = key_width // HEAD_SIZE
    wide = queries.shape[1] // heads
    rank = query_up_map.shape[0]
    return pl.pallas_call(
        attention_kernel,
        out_shape=(
            jax.ShapeDtypeStruct((tokens, queries.shape[1] + 2 * key_width), jnp.bfloat16),
            jax.ShapeDtypeStruct((tokens, 3 * rank), jnp.float32),
        ),
        grid=(heads,),
        in_specs=[
            pl.BlockSpec((tokens, wide), lambda h: (0, h)),
            pl.BlockSpec((tokens, HEAD_SIZE), lambda h: (0, h)),
            pl.BlockSpec((tokens, HEAD_SIZE), lambda h: (0, h)),
            pl.BlockSpec((tokens, wide), lambda h: (0, h)),
            pl.BlockSpec((tokens, 1), lambda h: (0, 0)),
            pl.BlockSpec((1, tokens), lambda h: (0, 0)),
            pl.BlockSpec((rank, wide), lambda h: (0, h)),
            pl.BlockSpec((2, rank, HEAD_SIZE), lambda h: (0, 0, h)),
        ],
        out_specs=(
            pl.BlockSpec((tokens, queries.shape[1] + 2 * key_width), lambda h: (0, 0)),
            pl.BlockSpec((tokens, 3 * rank), lambda h: (0, 0)),
        ),
        compiler_params=pltpu.CompilerParams(vmem_limit_bytes=32 << 20),
        cost_estimate=pl.CostEstimate(
            flops=10 * tokens * tokens * queries.shape[1],
            bytes_accessed=6 * tokens * queries.shape[1],
            transcendentals=tokens * tokens * queries.shape[1] // HEAD_SIZE,
        ),
        name="attention",
    )(
        queries,
        keys,
        values,
        gradients,
        ids.reshape(tokens, 1),
        ids.reshape(1, tokens),
        query_up_map,
        key_value_up_maps,
    )


def term_kernel(turn_ref, *refs):
    del turn_ref
    slots, rights, (out_ref, left, arrived) = refs[:4], refs[4:-3], refs[-3:]
    tokens = slots[0].shape[0]

    @pl.when(pl.program_id(0) == 0)
    def _():
        copies = [
            pltpu.make_async_copy(a, left.at[pl.ds(n * tokens, tokens), :], arrived.at[n])
            for n, a in enumerate(slots)
        ]
        for copy in copies:
            copy.start()
        for copy in copies:
            copy.wait()

    width = rights[0].shape[0]
    for n, right in enumerate(rights):
        out_ref[0, :, n * width : (n + 1) * width] = lax.dot_general(
            left[...],
            right[...],
            (((1,), (1,)), ((), ())),
            preferred_element_type=jnp.float32,
        ).astype(jnp.bfloat16)


def term_halves(slots, weights, core):
    tokens, depth = slots[0].shape
    rows = weights[0].shape[0] // 2
    count = len(weights)
    return pl.pallas_call(
        term_kernel,
        out_shape=jax.ShapeDtypeStruct((2, 4 * tokens, count * rows), jnp.bfloat16),
        grid_spec=pltpu.PrefetchScalarGridSpec(
            num_scalar_prefetch=1,
            grid=(2,),
            in_specs=[pl.BlockSpec(memory_space=pl.ANY)] * 4
            + [pl.BlockSpec((rows, depth), lambda i, turn: (lax.rem(turn[0] + 1 - i, 2), 0))]
            * count,
            out_specs=pl.BlockSpec((1, 4 * tokens, count * rows), lambda i, turn: (1 - i, 0, 0)),
            scratch_shapes=[
                pltpu.VMEM((4 * tokens, depth), jnp.bfloat16),
                pltpu.SemaphoreType.DMA((4,)),
            ],
        ),
        compiler_params=pltpu.CompilerParams(vmem_limit_bytes=40 << 20),
        cost_estimate=pl.CostEstimate(
            flops=16 * tokens * depth * rows * count,
            bytes_accessed=8 * tokens * depth + (4 * rows * depth + 16 * tokens * rows) * count,
            transcendentals=0,
        ),
        name="term",
    )(core[None], *slots, *weights)


def finish_kernel(spot_ref, added_ref, *refs):
    pieces, out_ref = refs[:-1], refs[-1]
    width = pieces[-1].shape[1]
    place = 0
    for piece in pieces:
        for start in range(0, piece.shape[1], width):
            there = pl.ds(pl.multiple_of(spot_ref[place] * width, width), width)
            out_ref[:, there] = (
                piece[:, start : start + width].astype(jnp.float32) + added_ref[:, there]
            ).astype(jnp.bfloat16)
            place += 1


def finish(pieces, spots, added):
    return pl.pallas_call(
        finish_kernel,
        out_shape=jax.ShapeDtypeStruct(added.shape, jnp.bfloat16),
        in_specs=[pl.BlockSpec(memory_space=pltpu.SMEM)]
        + [pl.BlockSpec(memory_space=pltpu.VMEM)] * (1 + len(pieces)),
        out_specs=pl.BlockSpec(memory_space=pltpu.VMEM),
        compiler_params=pltpu.CompilerParams(vmem_limit_bytes=24 << 20),
        cost_estimate=pl.CostEstimate(
            flops=added.size, bytes_accessed=8 * added.size, transcendentals=0
        ),
        name="finish",
    )(spots, added, *pieces)


def plane_scatter(value, bits):
    lo = lax.axis_index("lo")
    for bit in bits:
        mine = (lo // bit) % 2
        axis = 2 if bit == 1 and value.ndim == 5 else 1
        sent = pick(value, 1 - mine, axis).astype(jnp.bfloat16)
        value = pick(value, mine, axis) + swap_lo(sent, bit).astype(jnp.float32)
    return value


def dp_pieces(down_local, up_local):
    rows, rank = down_local.shape
    return jnp.concatenate(
        [
            down_local.reshape(16, rows // 16, rank),
            up_local.reshape(-1, 16, rank).transpose(1, 0, 2),
        ],
        axis=1,
    )


def dp_scatter(pieces):
    hi = lax.axis_index("hi")
    pieces = pieces.reshape(4, 2, 2, *pieces.shape[1:])
    column = jnp.concatenate(
        [plane_scatter(pieces[:2], (1, 2)), plane_scatter(pieces[2:], (2, 1))], axis=0
    )
    total = pick(column, hi, 0)
    for step in range(1, 4):
        sent = pick(column, (hi + step) % 4, 0).astype(jnp.bfloat16)
        total = total + turn_hi(sent, step).astype(jnp.float32)
    return total.astype(jnp.bfloat16)


def dp_gather(piece):
    hi, lo = lax.axis_index("hi"), lax.axis_index("lo")
    turned = jnp.stack([piece] + [turn_hi(piece, step) for step in range(1, 4)])
    column = jnp.stack([pick(turned, (hi - z) % 4, 0) for z in range(4)])
    planes = []
    for value, bits in ((column[:2], (1, 2)), (column[2:], (2, 1))):
        for bit in bits:
            other = swap_lo(value, bit)
            first = (lo // bit) % 2 == 0
            axis = 1 if bit == 2 or value.ndim == 3 else 2
            value = jnp.stack(
                [jnp.where(first, value, other), jnp.where(first, other, value)], axis=axis
            )
        planes.append(value)
    return jnp.concatenate(planes, axis=0).reshape(16, *piece.shape)


def gather_hi(own):
    hi = lax.axis_index("hi")
    right, left = [own], [own]
    for step in range(1, 4):
        right.append(move_hi(right[-1], 1, step - 1, 2))
        left.append(move_hi(left[-1], -1, 1, 4 - step))
    passed = (right[2], left[2])
    slots = [
        own,
        jnp.where(hi == 3, right[1], left[1]),
        jnp.where(hi < 2, left[2], right[2]),
        jnp.where(hi == 0, left[3], jnp.where(hi == 3, right[3], right[1])),
    ]
    table = jnp.array([[0, 1, 2, 3], [3, 0, 1, 2], [2, 3, 0, 1], [3, 2, 1, 0]], jnp.int32)
    return slots, pick(table, hi, 0), passed


def fast_shards():
    def shards(
        normed,
        stored_queries,
        stored_keys,
        stored_values,
        head_output_grad,
        document_index,
        query_projection_weight,
        key_projection_weight,
        value_projection_weight,
        adapter_down_maps,
        query_up_map,
        key_value_up_maps,
    ):
        hi, lo, core = (lax.axis_index(name) for name in AXES)
        own_weights = jnp.concatenate(
            [query_projection_weight, key_projection_weight, value_projection_weight], axis=1
        )
        cut = own_weights.shape[0] // 2
        by_x, by_y = swap_lo(own_weights, 1), swap_lo(own_weights, 2)
        stored_queries = after(stored_queries, own_weights)

        own, middle_part = attention(
            stored_queries,
            stored_keys,
            stored_values,
            head_output_grad,
            document_index[0],
            query_up_map,
            key_value_up_maps,
        )
        q_width = stored_queries.shape[1]
        k_width = stored_keys.shape[1]
        query_gradient = own[:, :q_width]
        key_gradient = own[:, q_width : q_width + k_width]
        value_gradient = own[:, q_width + k_width :]
        slots, slot_of, passed = gather_hi(own)

        by_x, by_y = after((by_x, by_y), passed)
        across = (swap_lo(by_x[:cut], 2), swap_lo(by_y[cut:], 1))

        middle_local = jnp.concatenate(
            [
                jnp.dot(normed, adapter_down_maps, preferred_element_type=jnp.float32),
                middle_part,
            ],
            axis=1,
        )
        middle = (middle_local + swap_core(middle_local)).astype(jnp.bfloat16)
        rank = adapter_down_maps.shape[1]
        adapter_middle, middle_gradient = middle[:, :rank], middle[:, rank:]
        adapter_middle, late_gradient = after((adapter_middle, middle_gradient), (by_x, by_y))
        down_local = lax.dot_general(
            normed, late_gradient, (((0,), (0,)), ((), ())), preferred_element_type=jnp.float32
        )
        ups = up_gradients(adapter_middle, query_gradient, key_gradient, value_gradient)
        piece = dp_scatter(dp_pieces(down_local, jnp.concatenate(ups, axis=1)))
        every = dp_gather(piece)
        down_rows = down_local.shape[0]
        down_total = every[:, : down_rows // 16].reshape(down_rows, rank).astype(jnp.float32)
        up_total = every[:, down_rows // 16 :].transpose(1, 0, 2).reshape(ADAPTER_RANK, -1)
        up_total = up_total.astype(jnp.float32)
        query_total = up_total[:, :q_width]
        key_value_total = jnp.stack(
            [up_total[:, q_width : q_width + k_width], up_total[:, q_width + k_width :]]
        )

        tokens = own.shape[0]
        source = (hi % 2) * 2 + core

        def owner(step):
            return lambda hi, lo, core: (((hi % 2) * 2 + core + step) % 4, lo, hi // 2)

        added = rows_product(middle_gradient, adapter_down_maps)
        received = []
        for part in range(2):
            if part:
                blocks = (jnp.concatenate(after(across, summed), axis=0),)
            else:
                blocks = (own_weights, by_x, by_y)
            halves = term_halves(slots, blocks, core)
            other = swap_core(halves[1])
            summed = halves[0].astype(jnp.float32) + other.astype(jnp.float32)
            summed = summed.astype(jnp.bfloat16).reshape(4, tokens, -1)
            for step in range(4):
                there = pick(slot_of, (source + step) % 4, 0)
                received.append(send(pick(summed, there, 0), owner(step)))
        spots = [
            (((hi - step) % 4) // 2) * 8 + (lo ^ block) * 2 + (hi - step) % 2
            for blocks in ((0, 1, 2), (3,))
            for step in range(4)
            for block in blocks
        ]
        normed_input_grad = finish(received, jnp.stack(spots).astype(jnp.int32), added)
        return (normed_input_grad, down_total, query_total, key_value_total)

    return shards


def solution(mesh):
    ranks = mesh.shape["dp"]
    tensor = mesh.shape["tensor"]
    inner = math.gcd(ranks, 4)
    outer = ranks // inner
    split = Mesh(mesh.devices.reshape(outer, inner, tensor), AXES)
    rows = ("hi", "lo")
    in_specs = (
        P(rows, "tensor"),
        P(rows, "tensor"),
        P(rows, "tensor"),
        P(rows, "tensor"),
        P(rows, "tensor"),
        P(rows, None),
        P(rows, "tensor"),
        P(rows, "tensor"),
        P(rows, "tensor"),
        P("tensor", None),
        P(None, "tensor"),
        P(None, None, "tensor"),
    )
    out_specs = (P(rows, "tensor"), P("tensor", None), P(None, "tensor"), P(None, None, "tensor"))
    return jax.shard_map(
        fast_shards() if (outer, inner, tensor) == SIZES else general_shards(outer, inner, tensor),
        mesh=split,
        in_specs=in_specs,
        out_specs=out_specs,
        check_vma=False,
    )
```

```python
import math

import jax
import jax.numpy as jnp
from jax import lax
from jax.experimental import pallas as pl
from jax.experimental.pallas import tpu as pltpu
from jax.sharding import Mesh
from jax.sharding import PartitionSpec as P

QUERY_HEADS = 32
KEY_HEADS = 8
HEAD_SIZE = 128
ADAPTER_RANK = 64


adapter_scale = 0.5


def attention_backward(queries, keyrows, value_row_block, output_gradient, ids):
    token_count = queries.shape[0]
    key_value_heads = keyrows.shape[1] // HEAD_SIZE
    query_group = QUERY_HEADS // KEY_HEADS
    scale = 1.0 / math.sqrt(HEAD_SIZE)
    qmat = queries.reshape(token_count, key_value_heads, query_group, HEAD_SIZE)
    kmat = keyrows.reshape(token_count, key_value_heads, HEAD_SIZE)
    value_matrix = value_row_block.reshape(token_count, key_value_heads, HEAD_SIZE)
    output_matrix = output_gradient.reshape(token_count, key_value_heads, query_group, HEAD_SIZE)
    same = ids[:, None] == ids[None, :]
    scores = jnp.einsum("bmav,wmv->mabw", qmat, kmat, preferred_element_type=jnp.float32) * scale
    scores = jnp.where(same[None, None], scores, -1e30)
    probs = jax.nn.softmax(scores, axis=-1)
    probs_half = probs.astype(jnp.bfloat16)
    value_gradient = jnp.einsum(
        "kgtu,tkgd->ukd", probs_half, output_matrix, preferred_element_type=jnp.float32
    ).astype(jnp.bfloat16)
    probability_grad = jnp.einsum(
        "bmav,wmv->mabw", output_matrix, value_matrix, preferred_element_type=jnp.float32
    )
    row_dots = jnp.sum(probs * probability_grad, axis=-1, keepdims=True)
    score_grad = (probs * (probability_grad - row_dots) * scale).astype(jnp.bfloat16)
    query_gradient = jnp.einsum(
        "kgtu,ukd->tkgd", score_grad, kmat, preferred_element_type=jnp.float32
    ).astype(jnp.bfloat16)
    key_gradient = jnp.einsum(
        "kgtu,tkgd->ukd", score_grad, qmat, preferred_element_type=jnp.float32
    ).astype(jnp.bfloat16)
    return (
        query_gradient.reshape(token_count, -1),
        key_gradient.reshape(token_count, -1),
        value_gradient.reshape(token_count, -1),
    )


def rows_product(left, piece):
    return lax.dot_general(
        left, piece, (((1,), (1,)), ((), ())), preferred_element_type=jnp.float32
    )


def up_gradients(adapter_middle, query_gradient, key_gradient, value_gradient):
    rank = ADAPTER_RANK
    parts = []
    for place, gradient in enumerate((query_gradient, key_gradient, value_gradient)):
        parts.append(
            adapter_scale
            * lax.dot_general(
                adapter_middle[:, place * rank : (place + 1) * rank],
                gradient,
                (((0,), (0,)), ((), ())),
                preferred_element_type=jnp.float32,
            )
        )
    return parts


def general_shards(outer, inner, tensor):
    every = ("hi", "lo")

    def shards(
        normed,
        stored_queries,
        stored_keys,
        stored_values,
        head_output_grad,
        document_index,
        query_projection_weight,
        key_projection_weight,
        value_projection_weight,
        adapter_down_maps,
        query_up_map,
        key_value_up_maps,
    ):
        weights = lax.all_gather(
            jnp.concatenate(
                [query_projection_weight, key_projection_weight, value_projection_weight], axis=1
            ),
            "lo",
            axis=0,
            tiled=True,
        )
        query_gradient, key_gradient, value_gradient = attention_backward(
            stored_queries, stored_keys, stored_values, head_output_grad, document_index[0]
        )
        own = jnp.concatenate([query_gradient, key_gradient, value_gradient], axis=1)
        gathered = lax.all_gather(own, "hi", axis=0, tiled=True)
        local_middle = jnp.dot(normed, adapter_down_maps, preferred_element_type=jnp.float32)
        grad_local = jnp.concatenate(
            [
                adapter_scale * rows_product(query_gradient, query_up_map),
                adapter_scale * rows_product(key_gradient, key_value_up_maps[0]),
                adapter_scale * rows_product(value_gradient, key_value_up_maps[1]),
            ],
            axis=1,
        )
        middle_total, grad_sum = (
            lax.psum(local_middle.astype(jnp.bfloat16), "tensor").astype(jnp.float32),
            lax.psum(grad_local.astype(jnp.bfloat16), "tensor").astype(jnp.float32),
        )
        adapter_middle = middle_total.astype(jnp.bfloat16)
        middle_gradient = grad_sum.astype(jnp.bfloat16)

        down_local = lax.dot_general(
            normed, middle_gradient, (((0,), (0,)), ((), ())), preferred_element_type=jnp.float32
        )
        ups = up_gradients(adapter_middle, query_gradient, key_gradient, value_gradient)
        up_local = jnp.concatenate(ups, axis=1)
        down_piece = lax.psum_scatter(down_local, every, scatter_dimension=0, tiled=True)
        up_piece = lax.psum_scatter(up_local, every, scatter_dimension=1, tiled=True)
        down_total = lax.all_gather(down_piece, every, axis=0, tiled=True)
        up_total = lax.all_gather(up_piece, every, axis=1, tiled=True)
        q_width = query_gradient.shape[1]
        k_width = key_gradient.shape[1]
        query_total = up_total[:, :q_width]
        key_value_total = jnp.stack(
            [up_total[:, q_width : q_width + k_width], up_total[:, q_width + k_width :]]
        )

        term = rows_product(gathered, weights).astype(jnp.bfloat16)
        tokens = own.shape[0]
        block = weights.shape[0]
        summed = lax.psum_scatter(term, "tensor", scatter_dimension=1, tiled=True)
        piece = block // tensor
        moved = lax.all_to_all(
            summed.reshape(outer, tokens, piece), "hi", split_axis=0, concat_axis=0, tiled=True
        )
        moved = moved.reshape(tensor, outer // tensor, tokens, piece)
        moved = lax.all_to_all(moved, "tensor", split_axis=0, concat_axis=0, tiled=True)
        base = moved.transpose(2, 1, 0, 3).reshape(tokens, -1).astype(jnp.float32)
        normed_input_grad = (base + rows_product(middle_gradient, adapter_down_maps)).astype(
            jnp.bfloat16
        )
        return (normed_input_grad, down_total, query_total, key_value_total)

    return shards


SIZES = (4, 4, 2)
AXES = ("hi", "lo", "tensor")


def send(value, target):
    pairs = []
    for rank in range(32):
        hi, lo, core = rank // 8, rank // 2 % 4, rank % 2
        there = target(hi, lo, core)
        if there is not None:
            pairs.append((rank, there[0] * 8 + there[1] * 2 + there[2]))
    return lax.ppermute(value, AXES, pairs)


def after(value, first):
    return lax.optimization_barrier((value, first))[0]


def swap_lo(value, bit):
    return send(value, lambda hi, lo, core: (hi, lo ^ bit, core))


def swap_core(value):
    return send(value, lambda hi, lo, core: (hi, lo, 1 - core))


def turn_hi(value, step):
    return send(value, lambda hi, lo, core: ((hi + step) % 4, lo, core))


def move_hi(value, step, first, last):
    return send(
        value,
        lambda hi, lo, core: (hi + step, lo, core) if first <= hi <= last else None,
    )


def pick(value, index, axis):
    return lax.dynamic_index_in_dim(value, index, axis, keepdims=False)


def attention_kernel(
    query_ref, key_ref, value_ref, grad_ref, row_ids, column_ids, up_ref, key_up_ref, own_ref, middle_ref
):
    head = pl.program_id(0)
    group = query_ref.shape[1] // HEAD_SIZE
    scale = 1.0 / math.sqrt(HEAD_SIZE)
    tokens = query_ref.shape[0]

    def stacked(ref):
        return jnp.concatenate(
            [ref[:, j * HEAD_SIZE : (j + 1) * HEAD_SIZE] for j in range(group)], axis=0
        )

    def product(left, right, dims):
        return lax.dot_general(
            left, right, ((dims[:1], dims[1:]), ((), ())), preferred_element_type=jnp.float32
        )

    queries, gradients = stacked(query_ref), stacked(grad_ref)
    keys, values = key_ref[...], value_ref[...]
    same = jnp.concatenate([row_ids[...] == column_ids[...]] * group, axis=0)
    scores = jnp.where(same, product(queries, keys, (1, 1)) * scale, -1e30)
    raised = jnp.exp(scores - jnp.max(scores, axis=-1, keepdims=True))
    probs = raised / jnp.sum(raised, axis=-1, keepdims=True)
    value_gradient = product(probs.astype(jnp.bfloat16), gradients, (0, 0)).astype(jnp.bfloat16)
    prob_grad = product(gradients, values, (1, 1))
    dots = jnp.sum(probs * prob_grad, axis=-1, keepdims=True)
    score_grad = (probs * (prob_grad - dots) * scale).astype(jnp.bfloat16)
    stacked_gradient = product(score_grad, keys, (1, 0)).astype(jnp.bfloat16)
    key_gradient = product(score_grad, queries, (0, 0)).astype(jnp.bfloat16)
    query_gradient = jnp.concatenate(
        [stacked_gradient[j * tokens : (j + 1) * tokens] for j in range(group)], axis=1
    )

    count = own_ref.shape[1] // ((group + 2) * HEAD_SIZE)

    def columns(start, width):
        return pl.ds(pl.multiple_of(start, HEAD_SIZE), width)

    own_ref[:, columns(head * group * HEAD_SIZE, group * HEAD_SIZE)] = query_gradient
    own_ref[:, columns((count * group + head) * HEAD_SIZE, HEAD_SIZE)] = key_gradient
    own_ref[:, columns((count * (group + 1) + head) * HEAD_SIZE, HEAD_SIZE)] = value_gradient

    @pl.when(head == 0)
    def _():
        middle_ref[...] = jnp.zeros_like(middle_ref)

    middle_ref[...] += adapter_scale * jnp.concatenate(
        [
            product(query_gradient, up_ref[...], (1, 1)),
            product(key_gradient, key_up_ref[0], (1, 1)),
            product(value_gradient, key_up_ref[1], (1, 1)),
        ],
        axis=1,
    )


def attention(queries, keys, values, gradients, ids, query_up_map, key_value_up_maps):
    tokens, key_width = keys.shape
    heads = key_width // HEAD_SIZE
    wide = queries.shape[1] // heads
    rank = query_up_map.shape[0]
    return pl.pallas_call(
        attention_kernel,
        out_shape=(
            jax.ShapeDtypeStruct((tokens, queries.shape[1] + 2 * key_width), jnp.bfloat16),
            jax.ShapeDtypeStruct((tokens, 3 * rank), jnp.float32),
        ),
        grid=(heads,),
        in_specs=[
            pl.BlockSpec((tokens, wide), lambda h: (0, h)),
            pl.BlockSpec((tokens, HEAD_SIZE), lambda h: (0, h)),
            pl.BlockSpec((tokens, HEAD_SIZE), lambda h: (0, h)),
            pl.BlockSpec((tokens, wide), lambda h: (0, h)),
            pl.BlockSpec((tokens, 1), lambda h: (0, 0)),
            pl.BlockSpec((1, tokens), lambda h: (0, 0)),
            pl.BlockSpec((rank, wide), lambda h: (0, h)),
            pl.BlockSpec((2, rank, HEAD_SIZE), lambda h: (0, 0, h)),
        ],
        out_specs=(
            pl.BlockSpec((tokens, queries.shape[1] + 2 * key_width), lambda h: (0, 0)),
            pl.BlockSpec((tokens, 3 * rank), lambda h: (0, 0)),
        ),
        compiler_params=pltpu.CompilerParams(vmem_limit_bytes=32 << 20),
        cost_estimate=pl.CostEstimate(
            flops=10 * tokens * tokens * queries.shape[1],
            bytes_accessed=6 * tokens * queries.shape[1],
            transcendentals=tokens * tokens * queries.shape[1] // HEAD_SIZE,
        ),
        name="attention",
    )(
        queries,
        keys,
        values,
        gradients,
        ids.reshape(tokens, 1),
        ids.reshape(1, tokens),
        query_up_map,
        key_value_up_maps,
    )


def term_kernel(place_ref, *refs):
    blocks, weights = refs[:7], refs[7:-6]
    kept_ref, sent_ref, left, right, arrived, landed = refs[-6:]
    tokens = blocks[0].shape[0]
    core, hi = place_ref[0], place_ref[1]
    count = len(weights) // 2
    width = weights[0].shape[0]

    for n in range(4):
        there = left.at[pl.ds(n * tokens, tokens), :]
        for step, block in zip((0, 1, 2, 3, -1, -2, -3), blocks):

            @pl.when(hi == n + step)
            def _(block=block, there=there, n=n):
                pltpu.make_async_copy(block, there, arrived.at[n]).start()

    for turn in range(2):
        for n in range(count):
            slot = turn * count + n
            for half in range(2):

                @pl.when(core == (half + 1 - turn) % 2)
                def _(n=n, half=half, slot=slot):
                    pltpu.make_async_copy(
                        weights[2 * n + half], right.at[slot], landed.at[slot]
                    ).start()

    for n in range(4):
        there = left.at[pl.ds(n * tokens, tokens), :]
        pltpu.make_async_copy(blocks[0], there, arrived.at[n]).wait()
    for turn, out_ref in enumerate((sent_ref, kept_ref)):
        for n in range(count):
            slot = turn * count + n
            pltpu.make_async_copy(weights[2 * n], right.at[slot], landed.at[slot]).wait()
            out_ref[:, n * width : (n + 1) * width] = lax.dot_general(
                left[...],
                right[slot],
                (((1,), (1,)), ((), ())),
                preferred_element_type=jnp.float32,
            ).astype(jnp.bfloat16)


def term_halves(blocks, weights, core, hi):
    tokens, depth = blocks[0].shape
    rows = weights[0][0].shape[0]
    count = len(weights)
    flat = [w for pair in weights for w in pair]
    out = jax.ShapeDtypeStruct((4 * tokens, count * rows), jnp.bfloat16)
    return pl.pallas_call(
        term_kernel,
        out_shape=(out, out),
        in_specs=[pl.BlockSpec(memory_space=pltpu.SMEM)]
        + [pl.BlockSpec(memory_space=pl.ANY)] * (7 + len(flat)),
        out_specs=(pl.BlockSpec(memory_space=pltpu.VMEM),) * 2,
        scratch_shapes=[
            pltpu.VMEM((4 * tokens, depth), jnp.bfloat16),
            pltpu.VMEM((2 * count, rows, depth), jnp.bfloat16),
            pltpu.SemaphoreType.DMA((4,)),
            pltpu.SemaphoreType.DMA((2 * count,)),
        ],
        compiler_params=pltpu.CompilerParams(vmem_limit_bytes=40 << 20),
        cost_estimate=pl.CostEstimate(
            flops=16 * tokens * depth * rows * count,
            bytes_accessed=8 * tokens * depth + (4 * rows * depth + 16 * tokens * rows) * count,
            transcendentals=0,
        ),
        name="term",
    )(jnp.stack([core, hi]), *blocks, *flat)


def finish_kernel(spot_ref, added_ref, *refs):
    pieces, out_ref = refs[:-1], refs[-1]
    width = pieces[-1].shape[1]
    place = 0
    for piece in pieces:
        for start in range(0, piece.shape[1], width):
            there = pl.ds(pl.multiple_of(spot_ref[place] * width, width), width)
            out_ref[:, there] = (
                piece[:, start : start + width].astype(jnp.float32) + added_ref[:, there]
            ).astype(jnp.bfloat16)
            place += 1


def finish(pieces, spots, added):
    return pl.pallas_call(
        finish_kernel,
        out_shape=jax.ShapeDtypeStruct(added.shape, jnp.bfloat16),
        in_specs=[pl.BlockSpec(memory_space=pltpu.SMEM)]
        + [pl.BlockSpec(memory_space=pltpu.VMEM)] * (1 + len(pieces)),
        out_specs=pl.BlockSpec(memory_space=pltpu.VMEM),
        compiler_params=pltpu.CompilerParams(vmem_limit_bytes=24 << 20),
        cost_estimate=pl.CostEstimate(
            flops=added.size, bytes_accessed=8 * added.size, transcendentals=0
        ),
        name="finish",
    )(spots, added, *pieces)


def dp_pieces(down_turned, up_local):
    rank, rows = down_turned.shape
    width = rows // 16
    return jnp.concatenate(
        [
            down_turned.reshape(rank, 4, 4, width).transpose(2, 1, 0, 3),
            up_local.reshape(4, 16, -1, width).transpose(2, 0, 1, 3).reshape(4, 4, -1, width),
        ],
        axis=2,
    ).astype(jnp.bfloat16)


def dp_results(every, rank, up_shape):
    rows, width = every.shape[2:]
    down = every[:, :, :rank].transpose(1, 0, 3, 2).reshape(16 * width, rank)
    up = every[:, :, rank:].reshape(-1, 4, 16, width).transpose(1, 2, 0, 3).reshape(up_shape)
    return down.astype(jnp.float32), up.astype(jnp.float32)


def scatter_sum(value, axis):
    return jnp.sum(
        lax.all_to_all(value, axis, 0, 0), axis=0, dtype=jnp.float32
    ).astype(jnp.bfloat16)


def gather_line(piece):
    hi = lax.axis_index("hi")
    turned = jnp.stack([piece] + [turn_hi(piece, step) for step in range(1, 4)])
    return jnp.stack([pick(turned, (hi - z) % 4, 0) for z in range(4)])


def gather(value, axis):
    return lax.all_to_all(jnp.broadcast_to(value[None], (4, *value.shape)), axis, 0, 0)


def chain_hi(own, first):
    right, left = [own], [own]
    for step in range(1, 4):
        right.append(move_hi(right[-1], 1, step - 1, 2))
        left.append(move_hi(left[-1], -1, 1, 4 - step))
        if step < 3:
            right[step], left[step] = after((right[step], left[step]), first[step - 1])
    return right[1:], left[1:]


def fast_shards():
    def shards(
        normed,
        stored_queries,
        stored_keys,
        stored_values,
        head_output_grad,
        document_index,
        query_projection_weight,
        key_projection_weight,
        value_projection_weight,
        adapter_down_maps,
        query_up_map,
        key_value_up_maps,
    ):
        hi, lo, core = (lax.axis_index(name) for name in AXES)
        parts = (query_projection_weight, key_projection_weight, value_projection_weight)
        cut = query_projection_weight.shape[0] // 2
        own_a = jnp.concatenate([w[:cut] for w in parts], axis=1)
        own_b = jnp.concatenate([w[cut:] for w in parts], axis=1)
        x_a, y_a = swap_lo(own_a, 1), swap_lo(own_a, 2)
        next_b = after(own_b, (x_a, y_a))
        x_b, y_b = swap_lo(next_b, 1), swap_lo(next_b, 2)
        stored_queries = after(stored_queries, own_a)

        own, middle_part = attention(
            stored_queries,
            stored_keys,
            stored_values,
            head_output_grad,
            document_index[0],
            query_up_map,
            key_value_up_maps,
        )
        q_width = stored_queries.shape[1]
        k_width = stored_keys.shape[1]
        query_gradient = own[:, :q_width]
        key_gradient = own[:, q_width : q_width + k_width]
        value_gradient = own[:, q_width + k_width :]
        right, left = chain_hi(own, ((x_a, y_a), (x_b, y_b)))
        blocks = (own, *right, *left)
        across_a, across_b = after((x_a, y_b), (right[1], left[1]))
        quarter = cut // 2
        across = [(swap_lo(across_a[:quarter], 2), swap_lo(across_b[:quarter], 1))]
        rest_a, rest_b = after((across_a[quarter:], across_b[quarter:]), across[0])
        across.append((swap_lo(rest_a, 2), swap_lo(rest_b, 1)))

        middle_local = jnp.concatenate(
            [
                jnp.dot(normed, adapter_down_maps, preferred_element_type=jnp.float32),
                middle_part,
            ],
            axis=1,
        )
        middle = (middle_local + swap_core(middle_local)).astype(jnp.bfloat16)
        rank = adapter_down_maps.shape[1]
        adapter_middle, middle_gradient = middle[:, :rank], middle[:, rank:]
        down_turned = lax.dot_general(
            middle_gradient, normed, (((0,), (0,)), ((), ())), preferred_element_type=jnp.float32
        )
        ups = up_gradients(adapter_middle, query_gradient, key_gradient, value_gradient)
        up_local = jnp.concatenate(ups, axis=1)
        column = scatter_sum(dp_pieces(down_turned, up_local), "lo")
        piece = scatter_sum(column, "hi")
        tokens = own.shape[0]
        source = (hi % 2) * 2 + core

        def owner(step):
            return lambda hi, lo, core: (((hi % 2) * 2 + core + step) % 4, lo, hi // 2)

        added = rows_product(middle_gradient, adapter_down_maps)
        received = []
        for part in range(2):
            if part:
                weights = after(across, summed)
            else:
                weights = ((own_a, own_b), (x_a, x_b), (y_a, y_b))
            kept, sent = term_halves(after(blocks, (piece, across[0])), weights, core, hi)
            summed = kept.astype(jnp.float32) + swap_core(sent).astype(jnp.float32)
            summed = summed.astype(jnp.bfloat16).reshape(4, tokens, -1)
            if not part:
                first_line = after(piece, summed)
            for step in range(4):
                received.append(send(pick(summed, (source + step) % 4, 0), owner(step)))
        every = gather(gather_line(first_line), "lo")
        down_total, up_total = dp_results(every, rank, up_local.shape)
        query_total = up_total[:, :q_width]
        key_value_total = jnp.stack(
            [up_total[:, q_width : q_width + k_width], up_total[:, q_width + k_width :]]
        )

        spots = [
            (((hi - step) % 4) // 2) * 8 + (lo ^ block) * 2 + (hi - step) % 2
            for blocks in ((0, 1, 2), (3,))
            for step in range(4)
            for block in blocks
        ]
        normed_input_grad = finish(received, jnp.stack(spots).astype(jnp.int32), added)
        return (normed_input_grad, down_total, query_total, key_value_total)

    return shards


def solution(mesh):
    ranks = mesh.shape["dp"]
    tensor = mesh.shape["tensor"]
    inner = math.gcd(ranks, 4)
    outer = ranks // inner
    split = Mesh(mesh.devices.reshape(outer, inner, tensor), AXES)
    rows = ("hi", "lo")
    in_specs = (
        P(rows, "tensor"),
        P(rows, "tensor"),
        P(rows, "tensor"),
        P(rows, "tensor"),
        P(rows, "tensor"),
        P(rows, None),
        P(rows, "tensor"),
        P(rows, "tensor"),
        P(rows, "tensor"),
        P("tensor", None),
        P(None, "tensor"),
        P(None, None, "tensor"),
    )
    out_specs = (P(rows, "tensor"), P("tensor", None), P(None, "tensor"), P(None, None, "tensor"))
    return jax.shard_map(
        fast_shards() if (outer, inner, tensor) == SIZES else general_shards(outer, inner, tensor),
        mesh=split,
        in_specs=in_specs,
        out_specs=out_specs,
        check_vma=False,
    )
```

```python
import math

import jax
import jax.numpy as jnp
from jax import lax
from jax.experimental import pallas as pl
from jax.experimental.pallas import tpu as pltpu
from jax.sharding import Mesh
from jax.sharding import PartitionSpec as P

QUERY_HEADS = 32
KEY_HEADS = 8
HEAD_SIZE = 128
ADAPTER_RANK = 64


adapter_scale = 0.5


def attention_backward(queries, keyrows, value_row_block, output_gradient, ids):
    token_count = queries.shape[0]
    key_value_heads = keyrows.shape[1] // HEAD_SIZE
    query_group = QUERY_HEADS // KEY_HEADS
    scale = 1.0 / math.sqrt(HEAD_SIZE)
    qmat = queries.reshape(token_count, key_value_heads, query_group, HEAD_SIZE)
    kmat = keyrows.reshape(token_count, key_value_heads, HEAD_SIZE)
    value_matrix = value_row_block.reshape(token_count, key_value_heads, HEAD_SIZE)
    output_matrix = output_gradient.reshape(token_count, key_value_heads, query_group, HEAD_SIZE)
    same = ids[:, None] == ids[None, :]
    scores = jnp.einsum("bmav,wmv->mabw", qmat, kmat, preferred_element_type=jnp.float32) * scale
    scores = jnp.where(same[None, None], scores, -1e30)
    probs = jax.nn.softmax(scores, axis=-1)
    probs_half = probs.astype(jnp.bfloat16)
    value_gradient = jnp.einsum(
        "kgtu,tkgd->ukd", probs_half, output_matrix, preferred_element_type=jnp.float32
    ).astype(jnp.bfloat16)
    probability_grad = jnp.einsum(
        "bmav,wmv->mabw", output_matrix, value_matrix, preferred_element_type=jnp.float32
    )
    row_dots = jnp.sum(probs * probability_grad, axis=-1, keepdims=True)
    score_grad = (probs * (probability_grad - row_dots) * scale).astype(jnp.bfloat16)
    query_gradient = jnp.einsum(
        "kgtu,ukd->tkgd", score_grad, kmat, preferred_element_type=jnp.float32
    ).astype(jnp.bfloat16)
    key_gradient = jnp.einsum(
        "kgtu,tkgd->ukd", score_grad, qmat, preferred_element_type=jnp.float32
    ).astype(jnp.bfloat16)
    return (
        query_gradient.reshape(token_count, -1),
        key_gradient.reshape(token_count, -1),
        value_gradient.reshape(token_count, -1),
    )


def rows_product(left, piece):
    return lax.dot_general(
        left, piece, (((1,), (1,)), ((), ())), preferred_element_type=jnp.float32
    )


def up_gradients(adapter_middle, query_gradient, key_gradient, value_gradient):
    rank = ADAPTER_RANK
    parts = []
    for place, gradient in enumerate((query_gradient, key_gradient, value_gradient)):
        parts.append(
            adapter_scale
            * lax.dot_general(
                adapter_middle[:, place * rank : (place + 1) * rank],
                gradient,
                (((0,), (0,)), ((), ())),
                preferred_element_type=jnp.float32,
            )
        )
    return parts


def general_shards(outer, inner, tensor):
    every = ("hi", "lo")

    def shards(
        normed,
        stored_queries,
        stored_keys,
        stored_values,
        head_output_grad,
        document_index,
        query_projection_weight,
        key_projection_weight,
        value_projection_weight,
        adapter_down_maps,
        query_up_map,
        key_value_up_maps,
    ):
        weights = lax.all_gather(
            jnp.concatenate(
                [query_projection_weight, key_projection_weight, value_projection_weight], axis=1
            ),
            "lo",
            axis=0,
            tiled=True,
        )
        query_gradient, key_gradient, value_gradient = attention_backward(
            stored_queries, stored_keys, stored_values, head_output_grad, document_index[0]
        )
        own = jnp.concatenate([query_gradient, key_gradient, value_gradient], axis=1)
        gathered = lax.all_gather(own, "hi", axis=0, tiled=True)
        local_middle = jnp.dot(normed, adapter_down_maps, preferred_element_type=jnp.float32)
        grad_local = jnp.concatenate(
            [
                adapter_scale * rows_product(query_gradient, query_up_map),
                adapter_scale * rows_product(key_gradient, key_value_up_maps[0]),
                adapter_scale * rows_product(value_gradient, key_value_up_maps[1]),
            ],
            axis=1,
        )
        middle_total, grad_sum = (
            lax.psum(local_middle.astype(jnp.bfloat16), "tensor").astype(jnp.float32),
            lax.psum(grad_local.astype(jnp.bfloat16), "tensor").astype(jnp.float32),
        )
        adapter_middle = middle_total.astype(jnp.bfloat16)
        middle_gradient = grad_sum.astype(jnp.bfloat16)

        down_local = lax.dot_general(
            normed, middle_gradient, (((0,), (0,)), ((), ())), preferred_element_type=jnp.float32
        )
        ups = up_gradients(adapter_middle, query_gradient, key_gradient, value_gradient)
        up_local = jnp.concatenate(ups, axis=1)
        down_piece = lax.psum_scatter(down_local, every, scatter_dimension=0, tiled=True)
        up_piece = lax.psum_scatter(up_local, every, scatter_dimension=1, tiled=True)
        down_total = lax.all_gather(down_piece, every, axis=0, tiled=True)
        up_total = lax.all_gather(up_piece, every, axis=1, tiled=True)
        q_width = query_gradient.shape[1]
        k_width = key_gradient.shape[1]
        query_total = up_total[:, :q_width]
        key_value_total = jnp.stack(
            [up_total[:, q_width : q_width + k_width], up_total[:, q_width + k_width :]]
        )

        term = rows_product(gathered, weights).astype(jnp.bfloat16)
        tokens = own.shape[0]
        block = weights.shape[0]
        summed = lax.psum_scatter(term, "tensor", scatter_dimension=1, tiled=True)
        piece = block // tensor
        moved = lax.all_to_all(
            summed.reshape(outer, tokens, piece), "hi", split_axis=0, concat_axis=0, tiled=True
        )
        moved = moved.reshape(tensor, outer // tensor, tokens, piece)
        moved = lax.all_to_all(moved, "tensor", split_axis=0, concat_axis=0, tiled=True)
        base = moved.transpose(2, 1, 0, 3).reshape(tokens, -1).astype(jnp.float32)
        normed_input_grad = (base + rows_product(middle_gradient, adapter_down_maps)).astype(
            jnp.bfloat16
        )
        return (normed_input_grad, down_total, query_total, key_value_total)

    return shards


SIZES = (4, 4, 2)
AXES = ("hi", "lo", "tensor")


def send(value, target):
    pairs = []
    for rank in range(32):
        hi, lo, core = rank // 8, rank // 2 % 4, rank % 2
        there = target(hi, lo, core)
        if there is not None:
            pairs.append((rank, there[0] * 8 + there[1] * 2 + there[2]))
    return lax.ppermute(value, AXES, pairs)


def after(value, first):
    return lax.optimization_barrier((value, first))[0]


def swap_lo(value, bit):
    return send(value, lambda hi, lo, core: (hi, lo ^ bit, core))


def swap_core(value):
    return send(value, lambda hi, lo, core: (hi, lo, 1 - core))


def move_hi(value, step, first, last):
    return send(
        value,
        lambda hi, lo, core: (hi + step, lo, core) if first <= hi <= last else None,
    )


def pick(value, index, axis):
    return lax.dynamic_index_in_dim(value, index, axis, keepdims=False)


def attention_kernel(
    query_ref, key_ref, value_ref, grad_ref, row_ids, column_ids, up_ref, key_up_ref, own_ref, middle_ref
):
    head = pl.program_id(0)
    group = query_ref.shape[1] // HEAD_SIZE
    scale = 1.0 / math.sqrt(HEAD_SIZE)
    tokens = query_ref.shape[0]

    def stacked(ref):
        return jnp.concatenate(
            [ref[:, j * HEAD_SIZE : (j + 1) * HEAD_SIZE] for j in range(group)], axis=0
        )

    def product(left, right, dims):
        return lax.dot_general(
            left, right, ((dims[:1], dims[1:]), ((), ())), preferred_element_type=jnp.float32
        )

    queries, gradients = stacked(query_ref), stacked(grad_ref)
    keys, values = key_ref[...], value_ref[...]
    same = jnp.concatenate([row_ids[...] == column_ids[...]] * group, axis=0)
    scores = jnp.where(same, product(queries, keys, (1, 1)) * scale, -1e30)
    raised = jnp.exp(scores - jnp.max(scores, axis=-1, keepdims=True))
    probs = raised / jnp.sum(raised, axis=-1, keepdims=True)
    value_gradient = product(probs.astype(jnp.bfloat16), gradients, (0, 0)).astype(jnp.bfloat16)
    prob_grad = product(gradients, values, (1, 1))
    dots = jnp.sum(probs * prob_grad, axis=-1, keepdims=True)
    score_grad = (probs * (prob_grad - dots) * scale).astype(jnp.bfloat16)
    stacked_gradient = product(score_grad, keys, (1, 0)).astype(jnp.bfloat16)
    key_gradient = product(score_grad, queries, (0, 0)).astype(jnp.bfloat16)
    query_gradient = jnp.concatenate(
        [stacked_gradient[j * tokens : (j + 1) * tokens] for j in range(group)], axis=1
    )

    count = own_ref.shape[1] // ((group + 2) * HEAD_SIZE)

    def columns(start, width):
        return pl.ds(pl.multiple_of(start, HEAD_SIZE), width)

    own_ref[:, columns(head * group * HEAD_SIZE, group * HEAD_SIZE)] = query_gradient
    own_ref[:, columns((count * group + head) * HEAD_SIZE, HEAD_SIZE)] = key_gradient
    own_ref[:, columns((count * (group + 1) + head) * HEAD_SIZE, HEAD_SIZE)] = value_gradient

    @pl.when(head == 0)
    def _():
        middle_ref[...] = jnp.zeros_like(middle_ref)

    middle_ref[...] += adapter_scale * jnp.concatenate(
        [
            product(query_gradient, up_ref[...], (1, 1)),
            product(key_gradient, key_up_ref[0], (1, 1)),
            product(value_gradient, key_up_ref[1], (1, 1)),
        ],
        axis=1,
    )


def attention(queries, keys, values, gradients, ids, query_up_map, key_value_up_maps):
    tokens, key_width = keys.shape
    heads = key_width // HEAD_SIZE
    wide = queries.shape[1] // heads
    rank = query_up_map.shape[0]
    return pl.pallas_call(
        attention_kernel,
        out_shape=(
            jax.ShapeDtypeStruct((tokens, queries.shape[1] + 2 * key_width), jnp.bfloat16),
            jax.ShapeDtypeStruct((tokens, 3 * rank), jnp.float32),
        ),
        grid=(heads,),
        in_specs=[
            pl.BlockSpec((tokens, wide), lambda h: (0, h)),
            pl.BlockSpec((tokens, HEAD_SIZE), lambda h: (0, h)),
            pl.BlockSpec((tokens, HEAD_SIZE), lambda h: (0, h)),
            pl.BlockSpec((tokens, wide), lambda h: (0, h)),
            pl.BlockSpec((tokens, 1), lambda h: (0, 0)),
            pl.BlockSpec((1, tokens), lambda h: (0, 0)),
            pl.BlockSpec((rank, wide), lambda h: (0, h)),
            pl.BlockSpec((2, rank, HEAD_SIZE), lambda h: (0, 0, h)),
        ],
        out_specs=(
            pl.BlockSpec((tokens, queries.shape[1] + 2 * key_width), lambda h: (0, 0)),
            pl.BlockSpec((tokens, 3 * rank), lambda h: (0, 0)),
        ),
        compiler_params=pltpu.CompilerParams(vmem_limit_bytes=32 << 20),
        cost_estimate=pl.CostEstimate(
            flops=10 * tokens * tokens * queries.shape[1],
            bytes_accessed=6 * tokens * queries.shape[1],
            transcendentals=tokens * tokens * queries.shape[1] // HEAD_SIZE,
        ),
        name="attention",
    )(
        queries,
        keys,
        values,
        gradients,
        ids.reshape(tokens, 1),
        ids.reshape(1, tokens),
        query_up_map,
        key_value_up_maps,
    )


def term_kernel(place_ref, *refs):
    blocks, weights, (sent_ref, kept_ref, left, arrived) = refs[:7], refs[7:-4], refs[-4:]
    tokens = blocks[0].shape[0]
    hi = place_ref[1]

    @pl.when(pl.program_id(0) == 0)
    def _():
        for n in range(4):
            there = left.at[pl.ds(n * tokens, tokens), :]
            for step, block in zip((0, 1, 2, 3, -1, -2, -3), blocks):

                @pl.when(hi == n + step)
                def _(block=block, there=there, n=n):
                    pltpu.make_async_copy(block, there, arrived.at[n]).start()

        for n in range(4):
            there = left.at[pl.ds(n * tokens, tokens), :]
            pltpu.make_async_copy(blocks[0], there, arrived.at[n]).wait()

    for turn, out_ref in enumerate((sent_ref, kept_ref)):

        @pl.when(pl.program_id(0) == turn)
        def _(out_ref=out_ref):
            width = 2 * weights[0].shape[0]
            for n in range(len(weights) // 2):
                right = jnp.concatenate([weights[2 * n][...], weights[2 * n + 1][...]], axis=0)
                out_ref[:, n * width : (n + 1) * width] = lax.dot_general(
                    left[...], right, (((1,), (1,)), ((), ())), preferred_element_type=jnp.float32
                ).astype(jnp.bfloat16)


def term_halves(blocks, weights, core, hi):
    tokens, depth = blocks[0].shape
    rows = weights[0].shape[0] // 2
    count = len(weights)
    out = jax.ShapeDtypeStruct((4 * tokens, count * rows), jnp.bfloat16)
    return pl.pallas_call(
        term_kernel,
        out_shape=(out, out),
        grid_spec=pltpu.PrefetchScalarGridSpec(
            num_scalar_prefetch=1,
            grid=(2,),
            in_specs=[pl.BlockSpec(memory_space=pl.ANY)] * 7
            + [pl.BlockSpec((rows, depth), lambda i, place: (lax.rem(place[0] + 1 - i, 2), 0))]
            * count,
            out_specs=(pl.BlockSpec(out.shape, lambda i, place: (0, 0)),) * 2,
            scratch_shapes=[
                pltpu.VMEM((4 * tokens, depth), jnp.bfloat16),
                pltpu.SemaphoreType.DMA((4,)),
            ],
        ),
        compiler_params=pltpu.CompilerParams(vmem_limit_bytes=40 << 20),
        cost_estimate=pl.CostEstimate(
            flops=16 * tokens * depth * rows * count,
            bytes_accessed=8 * tokens * depth + (4 * rows * depth + 16 * tokens * rows) * count,
            transcendentals=0,
        ),
        name="term",
    )(jnp.stack([core, hi]), *blocks, *weights)


def finish_kernel(spot_ref, added_ref, *refs):
    pieces, out_ref = refs[:-1], refs[-1]
    width = sum(piece.shape[1] for piece in pieces) // spot_ref.shape[0]
    place = 0
    for piece in pieces:
        for start in range(0, piece.shape[1], width):
            there = pl.ds(pl.multiple_of(spot_ref[place] * width, width), width)
            out_ref[:, there] = (
                piece[:, start : start + width].astype(jnp.float32) + added_ref[:, there]
            ).astype(jnp.bfloat16)
            place += 1


def finish(pieces, spots, added):
    return pl.pallas_call(
        finish_kernel,
        out_shape=jax.ShapeDtypeStruct(added.shape, jnp.bfloat16),
        in_specs=[pl.BlockSpec(memory_space=pltpu.SMEM)]
        + [pl.BlockSpec(memory_space=pltpu.VMEM)] * (1 + len(pieces)),
        out_specs=pl.BlockSpec(memory_space=pltpu.VMEM),
        compiler_params=pltpu.CompilerParams(vmem_limit_bytes=24 << 20),
        cost_estimate=pl.CostEstimate(
            flops=added.size, bytes_accessed=8 * added.size, transcendentals=0
        ),
        name="finish",
    )(spots, added, *pieces)


def dp_pieces(down_turned, up_local):
    rank, rows = down_turned.shape
    width = rows // 16
    return jnp.concatenate(
        [
            down_turned.reshape(rank, 4, 4, width).transpose(2, 1, 0, 3),
            up_local.reshape(4, 16, -1, width).transpose(2, 0, 1, 3).reshape(4, 4, -1, width),
        ],
        axis=2,
    ).astype(jnp.bfloat16)


def dp_results(every, rank, up_shape):
    rows, width = every.shape[2:]
    down = every[:, :, :rank].transpose(1, 0, 3, 2).reshape(16 * width, rank)
    up = every[:, :, rank:].reshape(-1, 4, 16, width).transpose(1, 2, 0, 3).reshape(up_shape)
    return down.astype(jnp.float32), up.astype(jnp.float32)


def scatter_sum(value, axis):
    return jnp.sum(
        lax.all_to_all(value, axis, 0, 0), axis=0, dtype=jnp.float32
    ).astype(jnp.bfloat16)


def gather(value, axis):
    return lax.all_to_all(jnp.broadcast_to(value[None], (4, *value.shape)), axis, 0, 0)


def chain_hi(own, first):
    right, left = [own], [own]
    for step in range(1, 4):
        right.append(move_hi(right[-1], 1, step - 1, 2))
        left.append(move_hi(left[-1], -1, 1, 4 - step))
        if step == 1:
            right[1], left[1] = after((right[1], left[1]), first)
    return right[1:], left[1:]


def fast_shards():
    def shards(
        normed,
        stored_queries,
        stored_keys,
        stored_values,
        head_output_grad,
        document_index,
        query_projection_weight,
        key_projection_weight,
        value_projection_weight,
        adapter_down_maps,
        query_up_map,
        key_value_up_maps,
    ):
        hi, lo, core = (lax.axis_index(name) for name in AXES)
        parts = (query_projection_weight, key_projection_weight, value_projection_weight)
        cut = query_projection_weight.shape[0] // 2
        own_a = jnp.concatenate([w[:cut] for w in parts], axis=1)
        own_b = jnp.concatenate([w[cut:] for w in parts], axis=1)
        x_a, y_a = swap_lo(own_a, 1), swap_lo(own_a, 2)
        next_b = after(own_b, (x_a, y_a))
        x_b, y_b = swap_lo(next_b, 1), swap_lo(next_b, 2)
        stored_queries = after(stored_queries, own_a)

        own, middle_part = attention(
            stored_queries,
            stored_keys,
            stored_values,
            head_output_grad,
            document_index[0],
            query_up_map,
            key_value_up_maps,
        )
        q_width = stored_queries.shape[1]
        k_width = stored_keys.shape[1]
        query_gradient = own[:, :q_width]
        key_gradient = own[:, q_width : q_width + k_width]
        value_gradient = own[:, q_width + k_width :]
        right, left = chain_hi(own, (x_a, y_a))
        blocks = (own, *right, *left)
        from_a, from_b = after((x_a, y_b), (x_b, right[1], left[1]))
        weights = (own_a, own_b, x_a, x_b, y_a, y_b, swap_lo(from_a, 2), swap_lo(from_b, 1))

        middle_local = jnp.concatenate(
            [
                jnp.dot(normed, adapter_down_maps, preferred_element_type=jnp.float32),
                middle_part,
            ],
            axis=1,
        )
        middle = (middle_local + swap_core(middle_local)).astype(jnp.bfloat16)
        middle = after(middle, (x_a, y_a))
        rank = adapter_down_maps.shape[1]
        adapter_middle, middle_gradient = middle[:, :rank], middle[:, rank:]
        down_turned = lax.dot_general(
            middle_gradient, normed, (((0,), (0,)), ((), ())), preferred_element_type=jnp.float32
        )
        ups = up_gradients(adapter_middle, query_gradient, key_gradient, value_gradient)
        up_local = jnp.concatenate(ups, axis=1)
        column = scatter_sum(dp_pieces(down_turned, up_local), "lo")
        piece = scatter_sum(after(column, (right[1], left[1])), "hi")
        tokens = own.shape[0]
        source = (hi % 2) * 2 + core

        def owner(step):
            return lambda hi, lo, core: (((hi % 2) * 2 + core + step) % 4, lo, hi // 2)

        added = rows_product(middle_gradient, adapter_down_maps)
        sent, kept = term_halves(blocks, weights, core, hi)
        line = after(gather(after(piece, (right[2], left[2])), "hi"), weights[-2:])
        summed = kept.astype(jnp.float32) + swap_core(sent).astype(jnp.float32)
        summed = summed.astype(jnp.bfloat16).reshape(4, tokens, -1)
        received = [
            send(pick(summed, (source + step) % 4, 0), owner(step)) for step in range(4)
        ]
        every = after(gather(line, "lo"), received[0])
        down_total, up_total = dp_results(every, rank, up_local.shape)
        query_total = up_total[:, :q_width]
        key_value_total = jnp.stack(
            [up_total[:, q_width : q_width + k_width], up_total[:, q_width + k_width :]]
        )

        spots = [
            (((hi - step) % 4) // 2) * 16 + (lo ^ block) * 4 + part * 2 + (hi - step) % 2
            for step in range(4)
            for block in range(4)
            for part in range(2)
        ]
        normed_input_grad = finish(received, jnp.stack(spots).astype(jnp.int32), added)
        return (normed_input_grad, down_total, query_total, key_value_total)

    return shards


def solution(mesh):
    ranks = mesh.shape["dp"]
    tensor = mesh.shape["tensor"]
    inner = math.gcd(ranks, 4)
    outer = ranks // inner
    split = Mesh(mesh.devices.reshape(outer, inner, tensor), AXES)
    rows = ("hi", "lo")
    in_specs = (
        P(rows, "tensor"),
        P(rows, "tensor"),
        P(rows, "tensor"),
        P(rows, "tensor"),
        P(rows, "tensor"),
        P(rows, None),
        P(rows, "tensor"),
        P(rows, "tensor"),
        P(rows, "tensor"),
        P("tensor", None),
        P(None, "tensor"),
        P(None, None, "tensor"),
    )
    out_specs = (P(rows, "tensor"), P("tensor", None), P(None, "tensor"), P(None, None, "tensor"))
    return jax.shard_map(
        fast_shards() if (outer, inner, tensor) == SIZES else general_shards(outer, inner, tensor),
        mesh=split,
        in_specs=in_specs,
        out_specs=out_specs,
        check_vma=False,
    )
```

```python
import functools
import math

import jax
import jax.numpy as jnp
from jax import lax
from jax.experimental import pallas as pl
from jax.experimental.pallas import tpu as pltpu
from jax.sharding import Mesh
from jax.sharding import PartitionSpec as P

QUERY_HEADS = 32
KEY_HEADS = 8
HEAD_SIZE = 128
ADAPTER_RANK = 64


adapter_scale = 0.5


def attention_backward(queries, keyrows, value_row_block, output_gradient, ids):
    token_count = queries.shape[0]
    key_value_heads = keyrows.shape[1] // HEAD_SIZE
    query_group = QUERY_HEADS // KEY_HEADS
    scale = 1.0 / math.sqrt(HEAD_SIZE)
    qmat = queries.reshape(token_count, key_value_heads, query_group, HEAD_SIZE)
    kmat = keyrows.reshape(token_count, key_value_heads, HEAD_SIZE)
    value_matrix = value_row_block.reshape(token_count, key_value_heads, HEAD_SIZE)
    output_matrix = output_gradient.reshape(token_count, key_value_heads, query_group, HEAD_SIZE)
    same = ids[:, None] == ids[None, :]
    scores = jnp.einsum("bmav,wmv->mabw", qmat, kmat, preferred_element_type=jnp.float32) * scale
    scores = jnp.where(same[None, None], scores, -1e30)
    probs = jax.nn.softmax(scores, axis=-1)
    probs_half = probs.astype(jnp.bfloat16)
    value_gradient = jnp.einsum(
        "kgtu,tkgd->ukd", probs_half, output_matrix, preferred_element_type=jnp.float32
    ).astype(jnp.bfloat16)
    probability_grad = jnp.einsum(
        "bmav,wmv->mabw", output_matrix, value_matrix, preferred_element_type=jnp.float32
    )
    row_dots = jnp.sum(probs * probability_grad, axis=-1, keepdims=True)
    score_grad = (probs * (probability_grad - row_dots) * scale).astype(jnp.bfloat16)
    query_gradient = jnp.einsum(
        "kgtu,ukd->tkgd", score_grad, kmat, preferred_element_type=jnp.float32
    ).astype(jnp.bfloat16)
    key_gradient = jnp.einsum(
        "kgtu,tkgd->ukd", score_grad, qmat, preferred_element_type=jnp.float32
    ).astype(jnp.bfloat16)
    return (
        query_gradient.reshape(token_count, -1),
        key_gradient.reshape(token_count, -1),
        value_gradient.reshape(token_count, -1),
    )


def rows_product(left, piece):
    return lax.dot_general(
        left, piece, (((1,), (1,)), ((), ())), preferred_element_type=jnp.float32
    )


def up_gradients(adapter_middle, query_gradient, key_gradient, value_gradient):
    rank = ADAPTER_RANK
    parts = []
    for place, gradient in enumerate((query_gradient, key_gradient, value_gradient)):
        parts.append(
            adapter_scale
            * lax.dot_general(
                adapter_middle[:, place * rank : (place + 1) * rank],
                gradient,
                (((0,), (0,)), ((), ())),
                preferred_element_type=jnp.float32,
            )
        )
    return parts


def general_shards(outer, inner, tensor):
    every = ("hi", "lo")

    def shards(
        normed,
        stored_queries,
        stored_keys,
        stored_values,
        head_output_grad,
        document_index,
        query_projection_weight,
        key_projection_weight,
        value_projection_weight,
        adapter_down_maps,
        query_up_map,
        key_value_up_maps,
    ):
        weights = lax.all_gather(
            jnp.concatenate(
                [query_projection_weight, key_projection_weight, value_projection_weight], axis=1
            ),
            "lo",
            axis=0,
            tiled=True,
        )
        query_gradient, key_gradient, value_gradient = attention_backward(
            stored_queries, stored_keys, stored_values, head_output_grad, document_index[0]
        )
        own = jnp.concatenate([query_gradient, key_gradient, value_gradient], axis=1)
        gathered = lax.all_gather(own, "hi", axis=0, tiled=True)
        local_middle = jnp.dot(normed, adapter_down_maps, preferred_element_type=jnp.float32)
        grad_local = jnp.concatenate(
            [
                adapter_scale * rows_product(query_gradient, query_up_map),
                adapter_scale * rows_product(key_gradient, key_value_up_maps[0]),
                adapter_scale * rows_product(value_gradient, key_value_up_maps[1]),
            ],
            axis=1,
        )
        middle_total, grad_sum = (
            lax.psum(local_middle.astype(jnp.bfloat16), "tensor").astype(jnp.float32),
            lax.psum(grad_local.astype(jnp.bfloat16), "tensor").astype(jnp.float32),
        )
        adapter_middle = middle_total.astype(jnp.bfloat16)
        middle_gradient = grad_sum.astype(jnp.bfloat16)

        down_local = lax.dot_general(
            normed, middle_gradient, (((0,), (0,)), ((), ())), preferred_element_type=jnp.float32
        )
        ups = up_gradients(adapter_middle, query_gradient, key_gradient, value_gradient)
        up_local = jnp.concatenate(ups, axis=1)
        down_piece = lax.psum_scatter(down_local, every, scatter_dimension=0, tiled=True)
        up_piece = lax.psum_scatter(up_local, every, scatter_dimension=1, tiled=True)
        down_total = lax.all_gather(down_piece, every, axis=0, tiled=True)
        up_total = lax.all_gather(up_piece, every, axis=1, tiled=True)
        q_width = query_gradient.shape[1]
        k_width = key_gradient.shape[1]
        query_total = up_total[:, :q_width]
        key_value_total = jnp.stack(
            [up_total[:, q_width : q_width + k_width], up_total[:, q_width + k_width :]]
        )

        term = rows_product(gathered, weights).astype(jnp.bfloat16)
        tokens = own.shape[0]
        block = weights.shape[0]
        summed = lax.psum_scatter(term, "tensor", scatter_dimension=1, tiled=True)
        piece = block // tensor
        moved = lax.all_to_all(
            summed.reshape(outer, tokens, piece), "hi", split_axis=0, concat_axis=0, tiled=True
        )
        moved = moved.reshape(tensor, outer // tensor, tokens, piece)
        moved = lax.all_to_all(moved, "tensor", split_axis=0, concat_axis=0, tiled=True)
        base = moved.transpose(2, 1, 0, 3).reshape(tokens, -1).astype(jnp.float32)
        normed_input_grad = (base + rows_product(middle_gradient, adapter_down_maps)).astype(
            jnp.bfloat16
        )
        return (normed_input_grad, down_total, query_total, key_value_total)

    return shards


SIZES = (4, 4, 2)
AXES = ("hi", "lo", "tensor")


def send(value, target):
    pairs = []
    for rank in range(32):
        hi, lo, core = rank // 8, rank // 2 % 4, rank % 2
        there = target(hi, lo, core)
        if there is not None:
            pairs.append((rank, there[0] * 8 + there[1] * 2 + there[2]))
    return lax.ppermute(value, AXES, pairs)


def after(value, first):
    return lax.optimization_barrier((value, first))[0]


def swap_lo(value, bit):
    return send(value, lambda hi, lo, core: (hi, lo ^ bit, core))


def swap_core(value):
    return send(value, lambda hi, lo, core: (hi, lo, 1 - core))


def move_hi(value, step, first, last):
    return send(
        value,
        lambda hi, lo, core: (hi + step, lo, core) if first <= hi <= last else None,
    )


def pick(value, index, axis):
    return lax.dynamic_index_in_dim(value, index, axis, keepdims=False)


def attention_kernel(
    query_ref, key_ref, value_ref, grad_ref, row_ids, column_ids, up_ref, key_up_ref, own_ref, middle_ref
):
    head = pl.program_id(0)
    group = query_ref.shape[1] // HEAD_SIZE
    scale = 1.0 / math.sqrt(HEAD_SIZE)
    tokens = query_ref.shape[0]

    def stacked(ref):
        return jnp.concatenate(
            [ref[:, j * HEAD_SIZE : (j + 1) * HEAD_SIZE] for j in range(group)], axis=0
        )

    def product(left, right, dims):
        return lax.dot_general(
            left, right, ((dims[:1], dims[1:]), ((), ())), preferred_element_type=jnp.float32
        )

    queries, gradients = stacked(query_ref), stacked(grad_ref)
    keys, values = key_ref[...], value_ref[...]
    same = jnp.concatenate([row_ids[...] == column_ids[...]] * group, axis=0)
    scores = jnp.where(same, product(queries, keys, (1, 1)) * scale, -1e30)
    raised = jnp.exp(scores - jnp.max(scores, axis=-1, keepdims=True))
    probs = raised / jnp.sum(raised, axis=-1, keepdims=True)
    value_gradient = product(probs.astype(jnp.bfloat16), gradients, (0, 0)).astype(jnp.bfloat16)
    prob_grad = product(gradients, values, (1, 1))
    dots = jnp.sum(probs * prob_grad, axis=-1, keepdims=True)
    score_grad = (probs * (prob_grad - dots) * scale).astype(jnp.bfloat16)
    stacked_gradient = product(score_grad, keys, (1, 0)).astype(jnp.bfloat16)
    key_gradient = product(score_grad, queries, (0, 0)).astype(jnp.bfloat16)
    query_gradient = jnp.concatenate(
        [stacked_gradient[j * tokens : (j + 1) * tokens] for j in range(group)], axis=1
    )

    count = own_ref.shape[1] // ((group + 2) * HEAD_SIZE)

    def columns(start, width):
        return pl.ds(pl.multiple_of(start, HEAD_SIZE), width)

    own_ref[:, columns(head * group * HEAD_SIZE, group * HEAD_SIZE)] = query_gradient
    own_ref[:, columns((count * group + head) * HEAD_SIZE, HEAD_SIZE)] = key_gradient
    own_ref[:, columns((count * (group + 1) + head) * HEAD_SIZE, HEAD_SIZE)] = value_gradient

    @pl.when(head == 0)
    def _():
        middle_ref[...] = jnp.zeros_like(middle_ref)

    middle_ref[...] += adapter_scale * jnp.concatenate(
        [
            product(query_gradient, up_ref[...], (1, 1)),
            product(key_gradient, key_up_ref[0], (1, 1)),
            product(value_gradient, key_up_ref[1], (1, 1)),
        ],
        axis=1,
    )


def attention(queries, keys, values, gradients, ids, query_up_map, key_value_up_maps):
    tokens, key_width = keys.shape
    heads = key_width // HEAD_SIZE
    wide = queries.shape[1] // heads
    rank = query_up_map.shape[0]
    return pl.pallas_call(
        attention_kernel,
        out_shape=(
            jax.ShapeDtypeStruct((tokens, queries.shape[1] + 2 * key_width), jnp.bfloat16),
            jax.ShapeDtypeStruct((tokens, 3 * rank), jnp.float32),
        ),
        grid=(heads,),
        in_specs=[
            pl.BlockSpec((tokens, wide), lambda h: (0, h)),
            pl.BlockSpec((tokens, HEAD_SIZE), lambda h: (0, h)),
            pl.BlockSpec((tokens, HEAD_SIZE), lambda h: (0, h)),
            pl.BlockSpec((tokens, wide), lambda h: (0, h)),
            pl.BlockSpec((tokens, 1), lambda h: (0, 0)),
            pl.BlockSpec((1, tokens), lambda h: (0, 0)),
            pl.BlockSpec((rank, wide), lambda h: (0, h)),
            pl.BlockSpec((2, rank, HEAD_SIZE), lambda h: (0, 0, h)),
        ],
        out_specs=(
            pl.BlockSpec((tokens, queries.shape[1] + 2 * key_width), lambda h: (0, 0)),
            pl.BlockSpec((tokens, 3 * rank), lambda h: (0, 0)),
        ),
        compiler_params=pltpu.CompilerParams(vmem_limit_bytes=32 << 20),
        cost_estimate=pl.CostEstimate(
            flops=10 * tokens * tokens * queries.shape[1],
            bytes_accessed=6 * tokens * queries.shape[1],
            transcendentals=tokens * tokens * queries.shape[1] // HEAD_SIZE,
        ),
        name="attention",
    )(
        queries,
        keys,
        values,
        gradients,
        ids.reshape(tokens, 1),
        ids.reshape(1, tokens),
        query_up_map,
        key_value_up_maps,
    )


def term_kernel(cuts, place_ref, *refs):
    blocks, weights, (sent_ref, kept_ref, left, arrived) = refs[:7], refs[7:-4], refs[-4:]
    tokens = blocks[0].shape[0]
    hi = place_ref[1]

    @pl.when(pl.program_id(0) == 0)
    def _():
        for n in range(4):
            there = left.at[pl.ds(n * tokens, tokens), :]
            for step, block in zip((0, 1, 2, 3, -1, -2, -3), blocks):

                @pl.when(hi == n + step)
                def _(block=block, there=there, n=n):
                    pltpu.make_async_copy(block, there, arrived.at[n]).start()

        for n in range(4):
            there = left.at[pl.ds(n * tokens, tokens), :]
            pltpu.make_async_copy(blocks[0], there, arrived.at[n]).wait()

    pairs = len(weights) // (2 * len(cuts))
    for turn, out_ref in enumerate((sent_ref, kept_ref)):

        @pl.when(pl.program_id(0) == turn)
        def _(out_ref=out_ref):
            width = 2 * weights[0].shape[0]
            for n in range(pairs):
                total = None
                for m, (start, stop) in enumerate(cuts):
                    part = 2 * (n * len(cuts) + m)
                    right = jnp.concatenate([weights[part][...], weights[part + 1][...]], axis=0)
                    product = lax.dot_general(
                        left[:, start:stop],
                        right,
                        (((1,), (1,)), ((), ())),
                        preferred_element_type=jnp.float32,
                    )
                    total = product if total is None else total + product
                out_ref[:, n * width : (n + 1) * width] = total.astype(jnp.bfloat16)


def term_halves(blocks, weights, core, hi):
    tokens, depth = blocks[0].shape
    rows = weights[0][0].shape[0] // 2
    count = len(weights[0])
    cuts, start = [], 0
    for piece in weights:
        cuts.append((start, start + piece[0].shape[1]))
        start += piece[0].shape[1]
    flat = [w for n in range(0, count, 2) for piece in weights for w in piece[n : n + 2]]
    out = jax.ShapeDtypeStruct((4 * tokens, count * rows), jnp.bfloat16)
    return pl.pallas_call(
        functools.partial(term_kernel, tuple(cuts)),
        out_shape=(out, out),
        grid_spec=pltpu.PrefetchScalarGridSpec(
            num_scalar_prefetch=1,
            grid=(2,),
            in_specs=[pl.BlockSpec(memory_space=pl.ANY)] * 7
            + [
                pl.BlockSpec(
                    (rows, w.shape[1]), lambda i, place: (lax.rem(place[0] + 1 - i, 2), 0)
                )
                for w in flat
            ],
            out_specs=(pl.BlockSpec(out.shape, lambda i, place: (0, 0)),) * 2,
            scratch_shapes=[
                pltpu.VMEM((4 * tokens, depth), jnp.bfloat16),
                pltpu.SemaphoreType.DMA((4,)),
            ],
        ),
        compiler_params=pltpu.CompilerParams(vmem_limit_bytes=40 << 20),
        cost_estimate=pl.CostEstimate(
            flops=16 * tokens * depth * rows * count,
            bytes_accessed=8 * tokens * depth + (4 * rows * depth + 16 * tokens * rows) * count,
            transcendentals=0,
        ),
        name="term",
    )(jnp.stack([core, hi]), *blocks, *flat)


def finish_kernel(spot_ref, added_ref, *refs):
    pieces, out_ref = refs[:-1], refs[-1]
    width = 128
    place = 0
    for piece in pieces:
        for h in range(piece.shape[0]):
            for start in range(0, piece.shape[2], width):
                there = pl.ds(pl.multiple_of(spot_ref[place] * width, width), width)
                out_ref[:, there] = (
                    piece[h, :, start : start + width].astype(jnp.float32) + added_ref[:, there]
                ).astype(jnp.bfloat16)
                place += 1


def finish(pieces, spots, added):
    return pl.pallas_call(
        finish_kernel,
        out_shape=jax.ShapeDtypeStruct(added.shape, jnp.bfloat16),
        in_specs=[pl.BlockSpec(memory_space=pltpu.SMEM)]
        + [pl.BlockSpec(memory_space=pltpu.VMEM)] * (1 + len(pieces)),
        out_specs=pl.BlockSpec(memory_space=pltpu.VMEM),
        compiler_params=pltpu.CompilerParams(vmem_limit_bytes=24 << 20),
        cost_estimate=pl.CostEstimate(
            flops=added.size, bytes_accessed=8 * added.size, transcendentals=0
        ),
        name="finish",
    )(spots, added, *pieces)


def dp_pieces(down_turned, up_local):
    rank, rows = down_turned.shape
    width = rows // 16
    return jnp.concatenate(
        [
            down_turned.reshape(rank, 4, 4, width).transpose(2, 1, 0, 3),
            up_local.reshape(4, 16, -1, width).transpose(2, 0, 1, 3).reshape(4, 4, -1, width),
        ],
        axis=2,
    ).astype(jnp.bfloat16)


def dp_results(every, rank, up_shape):
    rows, width = every.shape[2:]
    down = every[:, :, :rank].transpose(1, 0, 3, 2).reshape(16 * width, rank)
    up = every[:, :, rank:].reshape(-1, 4, 16, width).transpose(1, 2, 0, 3).reshape(up_shape)
    return down.astype(jnp.float32), up.astype(jnp.float32)


def scatter_sum(value, axis):
    return jnp.sum(
        lax.all_to_all(value, axis, 0, 0), axis=0, dtype=jnp.float32
    ).astype(jnp.bfloat16)


def gather(value, axis):
    return lax.all_to_all(jnp.broadcast_to(value[None], (4, *value.shape)), axis, 0, 0)


def gather_plane(value):
    lo = lax.axis_index("lo")
    others = jnp.stack([value] + [swap_lo(value, bit) for bit in range(1, 4)])
    return jnp.stack([pick(others, lo ^ place, 0) for place in range(4)])


def chain_hi(own, first):
    right, left = [own], [own]
    for step in range(1, 4):
        right.append(move_hi(right[-1], 1, step - 1, 2))
        left.append(move_hi(left[-1], -1, 1, 4 - step))
        if step == 1:
            right[1], left[1] = after((right[1], left[1]), first)
    return right[1:], left[1:]


def fast_shards():
    def shards(
        normed,
        stored_queries,
        stored_keys,
        stored_values,
        head_output_grad,
        document_index,
        query_projection_weight,
        key_projection_weight,
        value_projection_weight,
        adapter_down_maps,
        query_up_map,
        key_value_up_maps,
    ):
        hi, lo, core = (lax.axis_index(name) for name in AXES)
        parts = (query_projection_weight, key_projection_weight, value_projection_weight)
        cut = query_projection_weight.shape[0] // 2
        own_a = jnp.concatenate([w[:cut] for w in parts], axis=1)
        own_b = jnp.concatenate([w[cut:] for w in parts], axis=1)
        x_a, y_a = swap_lo(own_a, 1), swap_lo(own_a, 2)
        next_b = after(own_b, (x_a, y_a))
        x_b, y_b = swap_lo(next_b, 1), swap_lo(next_b, 2)
        stored_queries = after(stored_queries, own_a)

        own, middle_part = attention(
            stored_queries,
            stored_keys,
            stored_values,
            head_output_grad,
            document_index[0],
            query_up_map,
            key_value_up_maps,
        )
        q_width = stored_queries.shape[1]
        k_width = stored_keys.shape[1]
        query_gradient = own[:, :q_width]
        key_gradient = own[:, q_width : q_width + k_width]
        value_gradient = own[:, q_width + k_width :]
        right, left = chain_hi(own, (x_a, y_a))
        blocks = (own, *right, *left)
        from_a, from_b = after((x_a, y_b), (x_b, right[1], left[1]))
        q_width = stored_queries.shape[1]
        first = (swap_lo(from_a[:, :q_width], 2), swap_lo(from_b[:, :q_width], 1))
        from_a, from_b = after((from_a, from_b), first)
        second = (swap_lo(from_a[:, q_width:], 2), swap_lo(from_b[:, q_width:], 1))

        middle_local = jnp.concatenate(
            [
                jnp.dot(normed, adapter_down_maps, preferred_element_type=jnp.float32),
                middle_part,
            ],
            axis=1,
        )
        middle = (middle_local + swap_core(middle_local)).astype(jnp.bfloat16)
        middle = after(middle, (x_a, y_a))
        rank = adapter_down_maps.shape[1]
        adapter_middle, middle_gradient = middle[:, :rank], middle[:, rank:]
        down_turned = lax.dot_general(
            middle_gradient, normed, (((0,), (0,)), ((), ())), preferred_element_type=jnp.float32
        )
        ups = up_gradients(adapter_middle, query_gradient, key_gradient, value_gradient)
        up_local = jnp.concatenate(ups, axis=1)
        column = scatter_sum(dp_pieces(down_turned, up_local), "lo")
        piece = scatter_sum(after(column, (right[1], left[1])), "hi")
        tokens = own.shape[0]
        added = rows_product(middle_gradient, adapter_down_maps)
        pieces = []
        for part in range(2):
            if part:
                weights = after((first, second), summed)
            else:
                weights = ((own_a, own_b, x_a, x_b, y_a, y_b),)
            sent, kept = term_halves(after(blocks, (first, piece)), weights, core, hi)
            summed = kept.astype(jnp.float32) + swap_core(sent).astype(jnp.float32)
            summed = summed.astype(jnp.bfloat16).reshape(4, tokens, -1)
            moved = lax.all_to_all(summed, "hi", 0, 0)
            pieces.append(lax.dynamic_slice_in_dim(moved, 2 * core, 2, 0))
            pieces.append(swap_core(lax.dynamic_slice_in_dim(moved, 2 - 2 * core, 2, 0)))
        every = gather_plane(gather(piece, "hi"))
        down_total, up_total = dp_results(every, rank, up_local.shape)
        query_total = up_total[:, :q_width]
        key_value_total = jnp.stack(
            [up_total[:, q_width : q_width + k_width], up_total[:, q_width + k_width :]]
        )

        spots = [
            h * 16 + (lo ^ block) * 4 + part * 2 + other
            for blocks in ((0, 1, 2), (3,))
            for other in (core, 1 - core)
            for h in range(2)
            for block in blocks
            for part in range(2)
        ]
        normed_input_grad = finish(pieces, jnp.stack(spots).astype(jnp.int32), added)
        return (normed_input_grad, down_total, query_total, key_value_total)

    return shards


def solution(mesh):
    ranks = mesh.shape["dp"]
    tensor = mesh.shape["tensor"]
    inner = math.gcd(ranks, 4)
    outer = ranks // inner
    split = Mesh(mesh.devices.reshape(outer, inner, tensor), AXES)
    rows = ("hi", "lo")
    in_specs = (
        P(rows, "tensor"),
        P(rows, "tensor"),
        P(rows, "tensor"),
        P(rows, "tensor"),
        P(rows, "tensor"),
        P(rows, None),
        P(rows, "tensor"),
        P(rows, "tensor"),
        P(rows, "tensor"),
        P("tensor", None),
        P(None, "tensor"),
        P(None, None, "tensor"),
    )
    out_specs = (P(rows, "tensor"), P("tensor", None), P(None, "tensor"), P(None, None, "tensor"))
    return jax.shard_map(
        fast_shards() if (outer, inner, tensor) == SIZES else general_shards(outer, inner, tensor),
        mesh=split,
        in_specs=in_specs,
        out_specs=out_specs,
        check_vma=False,
    )
```

```python
import math

import jax
import jax.numpy as jnp
from jax import lax
from jax.experimental import pallas as pl
from jax.experimental.pallas import tpu as pltpu
from jax.sharding import Mesh
from jax.sharding import PartitionSpec as P

QUERY_HEADS = 32
KEY_HEADS = 8
HEAD_SIZE = 128
ADAPTER_RANK = 64


adapter_scale = 0.5


def attention_backward(queries, keyrows, value_row_block, output_gradient, ids):
    token_count = queries.shape[0]
    key_value_heads = keyrows.shape[1] // HEAD_SIZE
    query_group = QUERY_HEADS // KEY_HEADS
    scale = 1.0 / math.sqrt(HEAD_SIZE)
    qmat = queries.reshape(token_count, key_value_heads, query_group, HEAD_SIZE)
    kmat = keyrows.reshape(token_count, key_value_heads, HEAD_SIZE)
    value_matrix = value_row_block.reshape(token_count, key_value_heads, HEAD_SIZE)
    output_matrix = output_gradient.reshape(token_count, key_value_heads, query_group, HEAD_SIZE)
    same = ids[:, None] == ids[None, :]
    scores = jnp.einsum("bmav,wmv->mabw", qmat, kmat, preferred_element_type=jnp.float32) * scale
    scores = jnp.where(same[None, None], scores, -1e30)
    probs = jax.nn.softmax(scores, axis=-1)
    probs_half = probs.astype(jnp.bfloat16)
    value_gradient = jnp.einsum(
        "kgtu,tkgd->ukd", probs_half, output_matrix, preferred_element_type=jnp.float32
    ).astype(jnp.bfloat16)
    probability_grad = jnp.einsum(
        "bmav,wmv->mabw", output_matrix, value_matrix, preferred_element_type=jnp.float32
    )
    row_dots = jnp.sum(probs * probability_grad, axis=-1, keepdims=True)
    score_grad = (probs * (probability_grad - row_dots) * scale).astype(jnp.bfloat16)
    query_gradient = jnp.einsum(
        "kgtu,ukd->tkgd", score_grad, kmat, preferred_element_type=jnp.float32
    ).astype(jnp.bfloat16)
    key_gradient = jnp.einsum(
        "kgtu,tkgd->ukd", score_grad, qmat, preferred_element_type=jnp.float32
    ).astype(jnp.bfloat16)
    return (
        query_gradient.reshape(token_count, -1),
        key_gradient.reshape(token_count, -1),
        value_gradient.reshape(token_count, -1),
    )


def rows_product(left, piece):
    return lax.dot_general(
        left, piece, (((1,), (1,)), ((), ())), preferred_element_type=jnp.float32
    )


def up_gradients(adapter_middle, query_gradient, key_gradient, value_gradient):
    rank = ADAPTER_RANK
    parts = []
    for place, gradient in enumerate((query_gradient, key_gradient, value_gradient)):
        parts.append(
            adapter_scale
            * lax.dot_general(
                adapter_middle[:, place * rank : (place + 1) * rank],
                gradient,
                (((0,), (0,)), ((), ())),
                preferred_element_type=jnp.float32,
            )
        )
    return parts


def general_shards(outer, inner, tensor):
    every = ("hi", "lo")

    def shards(
        normed,
        stored_queries,
        stored_keys,
        stored_values,
        head_output_grad,
        document_index,
        query_projection_weight,
        key_projection_weight,
        value_projection_weight,
        adapter_down_maps,
        query_up_map,
        key_value_up_maps,
    ):
        weights = lax.all_gather(
            jnp.concatenate(
                [query_projection_weight, key_projection_weight, value_projection_weight], axis=1
            ),
            "lo",
            axis=0,
            tiled=True,
        )
        query_gradient, key_gradient, value_gradient = attention_backward(
            stored_queries, stored_keys, stored_values, head_output_grad, document_index[0]
        )
        own = jnp.concatenate([query_gradient, key_gradient, value_gradient], axis=1)
        gathered = lax.all_gather(own, "hi", axis=0, tiled=True)
        local_middle = jnp.dot(normed, adapter_down_maps, preferred_element_type=jnp.float32)
        grad_local = jnp.concatenate(
            [
                adapter_scale * rows_product(query_gradient, query_up_map),
                adapter_scale * rows_product(key_gradient, key_value_up_maps[0]),
                adapter_scale * rows_product(value_gradient, key_value_up_maps[1]),
            ],
            axis=1,
        )
        middle_total, grad_sum = (
            lax.psum(local_middle.astype(jnp.bfloat16), "tensor").astype(jnp.float32),
            lax.psum(grad_local.astype(jnp.bfloat16), "tensor").astype(jnp.float32),
        )
        adapter_middle = middle_total.astype(jnp.bfloat16)
        middle_gradient = grad_sum.astype(jnp.bfloat16)

        down_local = lax.dot_general(
            normed, middle_gradient, (((0,), (0,)), ((), ())), preferred_element_type=jnp.float32
        )
        ups = up_gradients(adapter_middle, query_gradient, key_gradient, value_gradient)
        up_local = jnp.concatenate(ups, axis=1)
        down_piece = lax.psum_scatter(down_local, every, scatter_dimension=0, tiled=True)
        up_piece = lax.psum_scatter(up_local, every, scatter_dimension=1, tiled=True)
        down_total = lax.all_gather(down_piece, every, axis=0, tiled=True)
        up_total = lax.all_gather(up_piece, every, axis=1, tiled=True)
        q_width = query_gradient.shape[1]
        k_width = key_gradient.shape[1]
        query_total = up_total[:, :q_width]
        key_value_total = jnp.stack(
            [up_total[:, q_width : q_width + k_width], up_total[:, q_width + k_width :]]
        )

        term = rows_product(gathered, weights).astype(jnp.bfloat16)
        tokens = own.shape[0]
        block = weights.shape[0]
        summed = lax.psum_scatter(term, "tensor", scatter_dimension=1, tiled=True)
        piece = block // tensor
        moved = lax.all_to_all(
            summed.reshape(outer, tokens, piece), "hi", split_axis=0, concat_axis=0, tiled=True
        )
        moved = moved.reshape(tensor, outer // tensor, tokens, piece)
        moved = lax.all_to_all(moved, "tensor", split_axis=0, concat_axis=0, tiled=True)
        base = moved.transpose(2, 1, 0, 3).reshape(tokens, -1).astype(jnp.float32)
        normed_input_grad = (base + rows_product(middle_gradient, adapter_down_maps)).astype(
            jnp.bfloat16
        )
        return (normed_input_grad, down_total, query_total, key_value_total)

    return shards


SIZES = (4, 4, 2)
AXES = ("hi", "lo", "tensor")


def send(value, target):
    pairs = []
    for rank in range(32):
        hi, lo, core = rank // 8, rank // 2 % 4, rank % 2
        there = target(hi, lo, core)
        if there is not None:
            pairs.append((rank, there[0] * 8 + there[1] * 2 + there[2]))
    return lax.ppermute(value, AXES, pairs)


def after(value, first):
    return lax.optimization_barrier((value, first))[0]


def swap_lo(value, bit):
    return send(value, lambda hi, lo, core: (hi, lo ^ bit, core))


def swap_core(value):
    return send(value, lambda hi, lo, core: (hi, lo, 1 - core))


def move_hi(value, step, first, last):
    return send(
        value,
        lambda hi, lo, core: (hi + step, lo, core) if first <= hi <= last else None,
    )


def pick(value, index, axis):
    return lax.dynamic_index_in_dim(value, index, axis, keepdims=False)


def attention_kernel(
    query_ref, key_ref, value_ref, grad_ref, row_ids, column_ids, up_ref, key_up_ref, own_ref, middle_ref
):
    head = pl.program_id(0)
    group = query_ref.shape[1] // HEAD_SIZE
    scale = 1.0 / math.sqrt(HEAD_SIZE)
    tokens = query_ref.shape[0]

    def stacked(ref):
        return jnp.concatenate(
            [ref[:, j * HEAD_SIZE : (j + 1) * HEAD_SIZE] for j in range(group)], axis=0
        )

    def product(left, right, dims):
        return lax.dot_general(
            left, right, ((dims[:1], dims[1:]), ((), ())), preferred_element_type=jnp.float32
        )

    queries, gradients = stacked(query_ref), stacked(grad_ref)
    keys, values = key_ref[...], value_ref[...]
    same = jnp.concatenate([row_ids[...] == column_ids[...]] * group, axis=0)
    scores = jnp.where(same, product(queries, keys, (1, 1)) * scale, -1e30)
    raised = jnp.exp(scores - jnp.max(scores, axis=-1, keepdims=True))
    probs = raised / jnp.sum(raised, axis=-1, keepdims=True)
    value_gradient = product(probs.astype(jnp.bfloat16), gradients, (0, 0)).astype(jnp.bfloat16)
    prob_grad = product(gradients, values, (1, 1))
    dots = jnp.sum(probs * prob_grad, axis=-1, keepdims=True)
    score_grad = (probs * (prob_grad - dots) * scale).astype(jnp.bfloat16)
    stacked_gradient = product(score_grad, keys, (1, 0)).astype(jnp.bfloat16)
    key_gradient = product(score_grad, queries, (0, 0)).astype(jnp.bfloat16)
    query_gradient = jnp.concatenate(
        [stacked_gradient[j * tokens : (j + 1) * tokens] for j in range(group)], axis=1
    )

    count = own_ref.shape[1] // ((group + 2) * HEAD_SIZE)

    def columns(start, width):
        return pl.ds(pl.multiple_of(start, HEAD_SIZE), width)

    own_ref[:, columns(head * group * HEAD_SIZE, group * HEAD_SIZE)] = query_gradient
    own_ref[:, columns((count * group + head) * HEAD_SIZE, HEAD_SIZE)] = key_gradient
    own_ref[:, columns((count * (group + 1) + head) * HEAD_SIZE, HEAD_SIZE)] = value_gradient

    @pl.when(head == 0)
    def _():
        middle_ref[...] = jnp.zeros_like(middle_ref)

    middle_ref[...] += adapter_scale * jnp.concatenate(
        [
            product(query_gradient, up_ref[...], (1, 1)),
            product(key_gradient, key_up_ref[0], (1, 1)),
            product(value_gradient, key_up_ref[1], (1, 1)),
        ],
        axis=1,
    )


def attention(queries, keys, values, gradients, ids, query_up_map, key_value_up_maps):
    tokens, key_width = keys.shape
    heads = key_width // HEAD_SIZE
    wide = queries.shape[1] // heads
    rank = query_up_map.shape[0]
    return pl.pallas_call(
        attention_kernel,
        out_shape=(
            jax.ShapeDtypeStruct((tokens, queries.shape[1] + 2 * key_width), jnp.bfloat16),
            jax.ShapeDtypeStruct((tokens, 3 * rank), jnp.float32),
        ),
        grid=(heads,),
        in_specs=[
            pl.BlockSpec((tokens, wide), lambda h: (0, h)),
            pl.BlockSpec((tokens, HEAD_SIZE), lambda h: (0, h)),
            pl.BlockSpec((tokens, HEAD_SIZE), lambda h: (0, h)),
            pl.BlockSpec((tokens, wide), lambda h: (0, h)),
            pl.BlockSpec((tokens, 1), lambda h: (0, 0)),
            pl.BlockSpec((1, tokens), lambda h: (0, 0)),
            pl.BlockSpec((rank, wide), lambda h: (0, h)),
            pl.BlockSpec((2, rank, HEAD_SIZE), lambda h: (0, 0, h)),
        ],
        out_specs=(
            pl.BlockSpec((tokens, queries.shape[1] + 2 * key_width), lambda h: (0, 0)),
            pl.BlockSpec((tokens, 3 * rank), lambda h: (0, 0)),
        ),
        compiler_params=pltpu.CompilerParams(vmem_limit_bytes=32 << 20),
        cost_estimate=pl.CostEstimate(
            flops=10 * tokens * tokens * queries.shape[1],
            bytes_accessed=6 * tokens * queries.shape[1],
            transcendentals=tokens * tokens * queries.shape[1] // HEAD_SIZE,
        ),
        name="attention",
    )(
        queries,
        keys,
        values,
        gradients,
        ids.reshape(tokens, 1),
        ids.reshape(1, tokens),
        query_up_map,
        key_value_up_maps,
    )


def term_kernel(place_ref, *refs):
    blocks, weights, (sent_ref, kept_ref, left, arrived) = refs[:7], refs[7:-4], refs[-4:]
    tokens = blocks[0].shape[0]
    hi = place_ref[1]

    @pl.when(pl.program_id(0) == 0)
    def _():
        for n in range(4):
            there = left.at[pl.ds(n * tokens, tokens), :]
            for step, block in zip((0, 1, 2, 3, -1, -2, -3), blocks):

                @pl.when(hi == n + step)
                def _(block=block, there=there, n=n):
                    pltpu.make_async_copy(block, there, arrived.at[n]).start()

        for n in range(4):
            there = left.at[pl.ds(n * tokens, tokens), :]
            pltpu.make_async_copy(blocks[0], there, arrived.at[n]).wait()

    for turn, out_ref in enumerate((sent_ref, kept_ref)):

        @pl.when(pl.program_id(0) == turn)
        def _(out_ref=out_ref):
            width = 2 * weights[0].shape[0]
            for n in range(len(weights) // 2):
                right = jnp.concatenate([weights[2 * n][...], weights[2 * n + 1][...]], axis=0)
                out_ref[:, n * width : (n + 1) * width] = lax.dot_general(
                    left[...], right, (((1,), (1,)), ((), ())), preferred_element_type=jnp.float32
                ).astype(jnp.bfloat16)


def term_halves(blocks, weights, core, hi):
    tokens, depth = blocks[0].shape
    rows = weights[0].shape[0] // 2
    count = len(weights)
    out = jax.ShapeDtypeStruct((4 * tokens, count * rows), jnp.bfloat16)
    return pl.pallas_call(
        term_kernel,
        out_shape=(out, out),
        grid_spec=pltpu.PrefetchScalarGridSpec(
            num_scalar_prefetch=1,
            grid=(2,),
            in_specs=[pl.BlockSpec(memory_space=pl.ANY)] * 7
            + [pl.BlockSpec((rows, depth), lambda i, place: (lax.rem(place[0] + 1 - i, 2), 0))]
            * count,
            out_specs=(pl.BlockSpec(out.shape, lambda i, place: (0, 0)),) * 2,
            scratch_shapes=[
                pltpu.VMEM((4 * tokens, depth), jnp.bfloat16),
                pltpu.SemaphoreType.DMA((4,)),
            ],
        ),
        compiler_params=pltpu.CompilerParams(vmem_limit_bytes=40 << 20),
        cost_estimate=pl.CostEstimate(
            flops=16 * tokens * depth * rows * count,
            bytes_accessed=8 * tokens * depth + (4 * rows * depth + 16 * tokens * rows) * count,
            transcendentals=0,
        ),
        name="term",
    )(jnp.stack([core, hi]), *blocks, *weights)


def finish_kernel(spot_ref, added_ref, *refs):
    pieces, out_ref = refs[:-1], refs[-1]
    width = sum(piece.shape[1] for piece in pieces) // spot_ref.shape[0]
    place = 0
    for piece in pieces:
        for start in range(0, piece.shape[1], width):
            there = pl.ds(pl.multiple_of(spot_ref[place] * width, width), width)
            out_ref[:, there] = (
                piece[:, start : start + width].astype(jnp.float32) + added_ref[:, there]
            ).astype(jnp.bfloat16)
            place += 1


def finish(pieces, spots, added):
    return pl.pallas_call(
        finish_kernel,
        out_shape=jax.ShapeDtypeStruct(added.shape, jnp.bfloat16),
        in_specs=[pl.BlockSpec(memory_space=pltpu.SMEM)]
        + [pl.BlockSpec(memory_space=pltpu.VMEM)] * (1 + len(pieces)),
        out_specs=pl.BlockSpec(memory_space=pltpu.VMEM),
        compiler_params=pltpu.CompilerParams(vmem_limit_bytes=24 << 20),
        cost_estimate=pl.CostEstimate(
            flops=added.size, bytes_accessed=8 * added.size, transcendentals=0
        ),
        name="finish",
    )(spots, added, *pieces)


def dp_pieces(down_turned, up_local):
    rank, rows = down_turned.shape
    width = rows // 16
    return jnp.concatenate(
        [
            down_turned.reshape(rank, 4, 4, width).transpose(2, 1, 0, 3),
            up_local.reshape(4, 16, -1, width).transpose(2, 0, 1, 3).reshape(4, 4, -1, width),
        ],
        axis=2,
    ).astype(jnp.bfloat16)


def dp_results(every, rank, up_shape):
    rows, width = every.shape[2:]
    down = every[:, :, :rank].transpose(1, 0, 3, 2).reshape(16 * width, rank)
    up = every[:, :, rank:].reshape(-1, 4, 16, width).transpose(1, 2, 0, 3).reshape(up_shape)
    return down.astype(jnp.float32), up.astype(jnp.float32)


def scatter_sum(value, axis):
    return jnp.sum(
        lax.all_to_all(value, axis, 0, 0), axis=0, dtype=jnp.float32
    ).astype(jnp.bfloat16)


def gather(value, axis):
    return lax.all_to_all(jnp.broadcast_to(value[None], (4, *value.shape)), axis, 0, 0)


def chain_hi(own, first):
    right, left = [own], [own]
    for step in range(1, 4):
        right.append(move_hi(right[-1], 1, step - 1, 2))
        left.append(move_hi(left[-1], -1, 1, 4 - step))
        if step == 1:
            right[1], left[1] = after((right[1], left[1]), first)
    return right[1:], left[1:]


def fast_shards():
    def shards(
        normed,
        stored_queries,
        stored_keys,
        stored_values,
        head_output_grad,
        document_index,
        query_projection_weight,
        key_projection_weight,
        value_projection_weight,
        adapter_down_maps,
        query_up_map,
        key_value_up_maps,
    ):
        hi, lo, core = (lax.axis_index(name) for name in AXES)
        parts = (query_projection_weight, key_projection_weight, value_projection_weight)
        cut = query_projection_weight.shape[0] // 2
        own_a = jnp.concatenate([w[:cut] for w in parts], axis=1)
        own_b = jnp.concatenate([w[cut:] for w in parts], axis=1)
        x_a, y_a = swap_lo(own_a, 1), swap_lo(own_a, 2)
        next_b = after(own_b, (x_a, y_a))
        x_b, y_b = swap_lo(next_b, 1), swap_lo(next_b, 2)
        stored_queries = after(stored_queries, own_a)

        own, middle_part = attention(
            stored_queries,
            stored_keys,
            stored_values,
            head_output_grad,
            document_index[0],
            query_up_map,
            key_value_up_maps,
        )
        q_width = stored_queries.shape[1]
        k_width = stored_keys.shape[1]
        query_gradient = own[:, :q_width]
        key_gradient = own[:, q_width : q_width + k_width]
        value_gradient = own[:, q_width + k_width :]
        right, left = chain_hi(own, (x_a, y_a))
        blocks = (own, *right, *left)
        from_a, from_b = after((x_a, y_b), (x_b, right[1], left[1]))
        weights = (own_a, own_b, x_a, x_b, y_a, y_b, swap_lo(from_a, 2), swap_lo(from_b, 1))

        middle_local = jnp.concatenate(
            [
                jnp.dot(normed, adapter_down_maps, preferred_element_type=jnp.float32),
                middle_part,
            ],
            axis=1,
        )
        middle = (middle_local + swap_core(middle_local)).astype(jnp.bfloat16)
        middle = after(middle, (x_a, y_a))
        rank = adapter_down_maps.shape[1]
        adapter_middle, middle_gradient = middle[:, :rank], middle[:, rank:]
        down_turned = lax.dot_general(
            middle_gradient, normed, (((0,), (0,)), ((), ())), preferred_element_type=jnp.float32
        )
        ups = up_gradients(adapter_middle, query_gradient, key_gradient, value_gradient)
        up_local = jnp.concatenate(ups, axis=1)
        column = scatter_sum(dp_pieces(down_turned, up_local), "lo")
        piece = scatter_sum(after(column, (right[1], left[1])), "hi")
        tokens = own.shape[0]
        source = (hi % 2) * 2 + core

        def owner(step):
            return lambda hi, lo, core: (((hi % 2) * 2 + core + step) % 4, lo, hi // 2)

        added = rows_product(middle_gradient, adapter_down_maps)
        line = after(gather(after(piece, (right[2], left[2])), "hi"), weights[-2:])
        sent, kept = term_halves(after(blocks, line), weights, core, hi)
        summed = kept.astype(jnp.float32) + swap_core(sent).astype(jnp.float32)
        summed = summed.astype(jnp.bfloat16).reshape(4, tokens, -1)
        received = [
            send(pick(summed, (source + step) % 4, 0), owner(step)) for step in range(4)
        ]
        every = after(gather(line, "lo"), received[0])
        down_total, up_total = dp_results(every, rank, up_local.shape)
        query_total = up_total[:, :q_width]
        key_value_total = jnp.stack(
            [up_total[:, q_width : q_width + k_width], up_total[:, q_width + k_width :]]
        )

        spots = [
            (((hi - step) % 4) // 2) * 16 + (lo ^ block) * 4 + part * 2 + (hi - step) % 2
            for step in range(4)
            for block in range(4)
            for part in range(2)
        ]
        normed_input_grad = finish(received, jnp.stack(spots).astype(jnp.int32), added)
        return (normed_input_grad, down_total, query_total, key_value_total)

    return shards


def solution(mesh):
    ranks = mesh.shape["dp"]
    tensor = mesh.shape["tensor"]
    inner = math.gcd(ranks, 4)
    outer = ranks // inner
    split = Mesh(mesh.devices.reshape(outer, inner, tensor), AXES)
    rows = ("hi", "lo")
    in_specs = (
        P(rows, "tensor"),
        P(rows, "tensor"),
        P(rows, "tensor"),
        P(rows, "tensor"),
        P(rows, "tensor"),
        P(rows, None),
        P(rows, "tensor"),
        P(rows, "tensor"),
        P(rows, "tensor"),
        P("tensor", None),
        P(None, "tensor"),
        P(None, None, "tensor"),
    )
    out_specs = (P(rows, "tensor"), P("tensor", None), P(None, "tensor"), P(None, None, "tensor"))
    return jax.shard_map(
        fast_shards() if (outer, inner, tensor) == SIZES else general_shards(outer, inner, tensor),
        mesh=split,
        in_specs=in_specs,
        out_specs=out_specs,
        check_vma=False,
    )
```

```python
import math

import jax
import jax.numpy as jnp
from jax import lax
from jax.experimental import pallas as pl
from jax.experimental.pallas import tpu as pltpu
from jax.sharding import Mesh
from jax.sharding import PartitionSpec as P

QUERY_HEADS = 32
KEY_HEADS = 8
HEAD_SIZE = 128
ADAPTER_RANK = 64


adapter_scale = 0.5


def attention_backward(queries, keyrows, value_row_block, output_gradient, ids):
    token_count = queries.shape[0]
    key_value_heads = keyrows.shape[1] // HEAD_SIZE
    query_group = QUERY_HEADS // KEY_HEADS
    scale = 1.0 / math.sqrt(HEAD_SIZE)
    qmat = queries.reshape(token_count, key_value_heads, query_group, HEAD_SIZE)
    kmat = keyrows.reshape(token_count, key_value_heads, HEAD_SIZE)
    value_matrix = value_row_block.reshape(token_count, key_value_heads, HEAD_SIZE)
    output_matrix = output_gradient.reshape(token_count, key_value_heads, query_group, HEAD_SIZE)
    same = ids[:, None] == ids[None, :]
    scores = jnp.einsum("bmav,wmv->mabw", qmat, kmat, preferred_element_type=jnp.float32) * scale
    scores = jnp.where(same[None, None], scores, -1e30)
    probs = jax.nn.softmax(scores, axis=-1)
    probs_half = probs.astype(jnp.bfloat16)
    value_gradient = jnp.einsum(
        "kgtu,tkgd->ukd", probs_half, output_matrix, preferred_element_type=jnp.float32
    ).astype(jnp.bfloat16)
    probability_grad = jnp.einsum(
        "bmav,wmv->mabw", output_matrix, value_matrix, preferred_element_type=jnp.float32
    )
    row_dots = jnp.sum(probs * probability_grad, axis=-1, keepdims=True)
    score_grad = (probs * (probability_grad - row_dots) * scale).astype(jnp.bfloat16)
    query_gradient = jnp.einsum(
        "kgtu,ukd->tkgd", score_grad, kmat, preferred_element_type=jnp.float32
    ).astype(jnp.bfloat16)
    key_gradient = jnp.einsum(
        "kgtu,tkgd->ukd", score_grad, qmat, preferred_element_type=jnp.float32
    ).astype(jnp.bfloat16)
    return (
        query_gradient.reshape(token_count, -1),
        key_gradient.reshape(token_count, -1),
        value_gradient.reshape(token_count, -1),
    )


def rows_product(left, piece):
    return lax.dot_general(
        left, piece, (((1,), (1,)), ((), ())), preferred_element_type=jnp.float32
    )


def up_gradients(adapter_middle, query_gradient, key_gradient, value_gradient):
    rank = ADAPTER_RANK
    parts = []
    for place, gradient in enumerate((query_gradient, key_gradient, value_gradient)):
        parts.append(
            adapter_scale
            * lax.dot_general(
                adapter_middle[:, place * rank : (place + 1) * rank],
                gradient,
                (((0,), (0,)), ((), ())),
                preferred_element_type=jnp.float32,
            )
        )
    return parts


def general_shards(outer, inner, tensor):
    every = ("hi", "lo")

    def shards(
        normed,
        stored_queries,
        stored_keys,
        stored_values,
        head_output_grad,
        document_index,
        query_projection_weight,
        key_projection_weight,
        value_projection_weight,
        adapter_down_maps,
        query_up_map,
        key_value_up_maps,
    ):
        weights = lax.all_gather(
            jnp.concatenate(
                [query_projection_weight, key_projection_weight, value_projection_weight], axis=1
            ),
            "lo",
            axis=0,
            tiled=True,
        )
        query_gradient, key_gradient, value_gradient = attention_backward(
            stored_queries, stored_keys, stored_values, head_output_grad, document_index[0]
        )
        own = jnp.concatenate([query_gradient, key_gradient, value_gradient], axis=1)
        gathered = lax.all_gather(own, "hi", axis=0, tiled=True)
        local_middle = jnp.dot(normed, adapter_down_maps, preferred_element_type=jnp.float32)
        grad_local = jnp.concatenate(
            [
                adapter_scale * rows_product(query_gradient, query_up_map),
                adapter_scale * rows_product(key_gradient, key_value_up_maps[0]),
                adapter_scale * rows_product(value_gradient, key_value_up_maps[1]),
            ],
            axis=1,
        )
        middle_total, grad_sum = (
            lax.psum(local_middle.astype(jnp.bfloat16), "tensor").astype(jnp.float32),
            lax.psum(grad_local.astype(jnp.bfloat16), "tensor").astype(jnp.float32),
        )
        adapter_middle = middle_total.astype(jnp.bfloat16)
        middle_gradient = grad_sum.astype(jnp.bfloat16)

        down_local = lax.dot_general(
            normed, middle_gradient, (((0,), (0,)), ((), ())), preferred_element_type=jnp.float32
        )
        ups = up_gradients(adapter_middle, query_gradient, key_gradient, value_gradient)
        up_local = jnp.concatenate(ups, axis=1)
        down_piece = lax.psum_scatter(down_local, every, scatter_dimension=0, tiled=True)
        up_piece = lax.psum_scatter(up_local, every, scatter_dimension=1, tiled=True)
        down_total = lax.all_gather(down_piece, every, axis=0, tiled=True)
        up_total = lax.all_gather(up_piece, every, axis=1, tiled=True)
        q_width = query_gradient.shape[1]
        k_width = key_gradient.shape[1]
        query_total = up_total[:, :q_width]
        key_value_total = jnp.stack(
            [up_total[:, q_width : q_width + k_width], up_total[:, q_width + k_width :]]
        )

        term = rows_product(gathered, weights).astype(jnp.bfloat16)
        tokens = own.shape[0]
        block = weights.shape[0]
        summed = lax.psum_scatter(term, "tensor", scatter_dimension=1, tiled=True)
        piece = block // tensor
        moved = lax.all_to_all(
            summed.reshape(outer, tokens, piece), "hi", split_axis=0, concat_axis=0, tiled=True
        )
        moved = moved.reshape(tensor, outer // tensor, tokens, piece)
        moved = lax.all_to_all(moved, "tensor", split_axis=0, concat_axis=0, tiled=True)
        base = moved.transpose(2, 1, 0, 3).reshape(tokens, -1).astype(jnp.float32)
        normed_input_grad = (base + rows_product(middle_gradient, adapter_down_maps)).astype(
            jnp.bfloat16
        )
        return (normed_input_grad, down_total, query_total, key_value_total)

    return shards


SIZES = (4, 4, 2)
AXES = ("hi", "lo", "tensor")


def send(value, target):
    pairs = []
    for rank in range(32):
        hi, lo, core = rank // 8, rank // 2 % 4, rank % 2
        there = target(hi, lo, core)
        if there is not None:
            pairs.append((rank, there[0] * 8 + there[1] * 2 + there[2]))
    return lax.ppermute(value, AXES, pairs)


def after(value, first):
    return lax.optimization_barrier((value, first))[0]


def swap_lo(value, bit):
    return send(value, lambda hi, lo, core: (hi, lo ^ bit, core))


def swap_core(value):
    return send(value, lambda hi, lo, core: (hi, lo, 1 - core))


def move_hi(value, step, first, last):
    return send(
        value,
        lambda hi, lo, core: (hi + step, lo, core) if first <= hi <= last else None,
    )


def pick(value, index, axis):
    return lax.dynamic_index_in_dim(value, index, axis, keepdims=False)


def attention_kernel(
    query_ref, key_ref, value_ref, grad_ref, row_ids, column_ids, up_ref, key_up_ref, own_ref, middle_ref
):
    head = pl.program_id(0)
    group = query_ref.shape[1] // HEAD_SIZE
    scale = 1.0 / math.sqrt(HEAD_SIZE)
    tokens = query_ref.shape[0]

    def stacked(ref):
        return jnp.concatenate(
            [ref[:, j * HEAD_SIZE : (j + 1) * HEAD_SIZE] for j in range(group)], axis=0
        )

    def product(left, right, dims):
        return lax.dot_general(
            left, right, ((dims[:1], dims[1:]), ((), ())), preferred_element_type=jnp.float32
        )

    queries, gradients = stacked(query_ref), stacked(grad_ref)
    keys, values = key_ref[...], value_ref[...]
    same = jnp.concatenate([row_ids[...] == column_ids[...]] * group, axis=0)
    scores = jnp.where(same, product(queries, keys, (1, 1)) * scale, -1e30)
    raised = jnp.exp(scores - jnp.max(scores, axis=-1, keepdims=True))
    probs = raised / jnp.sum(raised, axis=-1, keepdims=True)
    value_gradient = product(probs.astype(jnp.bfloat16), gradients, (0, 0)).astype(jnp.bfloat16)
    prob_grad = product(gradients, values, (1, 1))
    dots = jnp.sum(probs * prob_grad, axis=-1, keepdims=True)
    score_grad = (probs * (prob_grad - dots) * scale).astype(jnp.bfloat16)
    stacked_gradient = product(score_grad, keys, (1, 0)).astype(jnp.bfloat16)
    key_gradient = product(score_grad, queries, (0, 0)).astype(jnp.bfloat16)
    query_gradient = jnp.concatenate(
        [stacked_gradient[j * tokens : (j + 1) * tokens] for j in range(group)], axis=1
    )

    count = own_ref.shape[1] // ((group + 2) * HEAD_SIZE)

    def columns(start, width):
        return pl.ds(pl.multiple_of(start, HEAD_SIZE), width)

    own_ref[:, columns(head * group * HEAD_SIZE, group * HEAD_SIZE)] = query_gradient
    own_ref[:, columns((count * group + head) * HEAD_SIZE, HEAD_SIZE)] = key_gradient
    own_ref[:, columns((count * (group + 1) + head) * HEAD_SIZE, HEAD_SIZE)] = value_gradient

    @pl.when(head == 0)
    def _():
        middle_ref[...] = jnp.zeros_like(middle_ref)

    middle_ref[...] += adapter_scale * jnp.concatenate(
        [
            product(query_gradient, up_ref[...], (1, 1)),
            product(key_gradient, key_up_ref[0], (1, 1)),
            product(value_gradient, key_up_ref[1], (1, 1)),
        ],
        axis=1,
    )


def attention(queries, keys, values, gradients, ids, query_up_map, key_value_up_maps):
    tokens, key_width = keys.shape
    heads = key_width // HEAD_SIZE
    wide = queries.shape[1] // heads
    rank = query_up_map.shape[0]
    return pl.pallas_call(
        attention_kernel,
        out_shape=(
            jax.ShapeDtypeStruct((tokens, queries.shape[1] + 2 * key_width), jnp.bfloat16),
            jax.ShapeDtypeStruct((tokens, 3 * rank), jnp.float32),
        ),
        grid=(heads,),
        in_specs=[
            pl.BlockSpec((tokens, wide), lambda h: (0, h)),
            pl.BlockSpec((tokens, HEAD_SIZE), lambda h: (0, h)),
            pl.BlockSpec((tokens, HEAD_SIZE), lambda h: (0, h)),
            pl.BlockSpec((tokens, wide), lambda h: (0, h)),
            pl.BlockSpec((tokens, 1), lambda h: (0, 0)),
            pl.BlockSpec((1, tokens), lambda h: (0, 0)),
            pl.BlockSpec((rank, wide), lambda h: (0, h)),
            pl.BlockSpec((2, rank, HEAD_SIZE), lambda h: (0, 0, h)),
        ],
        out_specs=(
            pl.BlockSpec((tokens, queries.shape[1] + 2 * key_width), lambda h: (0, 0)),
            pl.BlockSpec((tokens, 3 * rank), lambda h: (0, 0)),
        ),
        compiler_params=pltpu.CompilerParams(vmem_limit_bytes=32 << 20),
        cost_estimate=pl.CostEstimate(
            flops=10 * tokens * tokens * queries.shape[1],
            bytes_accessed=6 * tokens * queries.shape[1],
            transcendentals=tokens * tokens * queries.shape[1] // HEAD_SIZE,
        ),
        name="attention",
    )(
        queries,
        keys,
        values,
        gradients,
        ids.reshape(tokens, 1),
        ids.reshape(1, tokens),
        query_up_map,
        key_value_up_maps,
    )


def term_kernel(place_ref, *refs):
    blocks, weights, (sent_ref, kept_ref, left, arrived) = refs[:7], refs[7:-4], refs[-4:]
    tokens = blocks[0].shape[0]
    hi = place_ref[1]

    @pl.when(pl.program_id(0) == 0)
    def _():
        for n in range(4):
            there = left.at[pl.ds(n * tokens, tokens), :]
            for step, block in zip((0, 1, 2, 3, -1, -2, -3), blocks):

                @pl.when(hi == n + step)
                def _(block=block, there=there, n=n):
                    pltpu.make_async_copy(block, there, arrived.at[n]).start()

        for n in range(4):
            there = left.at[pl.ds(n * tokens, tokens), :]
            pltpu.make_async_copy(blocks[0], there, arrived.at[n]).wait()

    for turn, out_ref in enumerate((sent_ref, kept_ref)):

        @pl.when(pl.program_id(0) == turn)
        def _(out_ref=out_ref):
            width = 2 * weights[0].shape[0]
            for n in range(len(weights) // 2):
                right = jnp.concatenate([weights[2 * n][...], weights[2 * n + 1][...]], axis=0)
                out_ref[:, n * width : (n + 1) * width] = lax.dot_general(
                    left[...], right, (((1,), (1,)), ((), ())), preferred_element_type=jnp.float32
                ).astype(jnp.bfloat16)


def term_halves(blocks, weights, core, hi):
    tokens, depth = blocks[0].shape
    rows = weights[0].shape[0] // 2
    count = len(weights)
    out = jax.ShapeDtypeStruct((4 * tokens, count * rows), jnp.bfloat16)
    return pl.pallas_call(
        term_kernel,
        out_shape=(out, out),
        grid_spec=pltpu.PrefetchScalarGridSpec(
            num_scalar_prefetch=1,
            grid=(2,),
            in_specs=[pl.BlockSpec(memory_space=pl.ANY)] * 7
            + [pl.BlockSpec((rows, depth), lambda i, place: (lax.rem(place[0] + 1 - i, 2), 0))]
            * count,
            out_specs=(pl.BlockSpec(out.shape, lambda i, place: (0, 0)),) * 2,
            scratch_shapes=[
                pltpu.VMEM((4 * tokens, depth), jnp.bfloat16),
                pltpu.SemaphoreType.DMA((4,)),
            ],
        ),
        compiler_params=pltpu.CompilerParams(vmem_limit_bytes=40 << 20),
        cost_estimate=pl.CostEstimate(
            flops=16 * tokens * depth * rows * count,
            bytes_accessed=8 * tokens * depth + (4 * rows * depth + 16 * tokens * rows) * count,
            transcendentals=0,
        ),
        name="term",
    )(jnp.stack([core, hi]), *blocks, *weights)


def finish_kernel(spot_ref, added_ref, *refs):
    pieces, out_ref = refs[:-1], refs[-1]
    width = sum(piece.shape[1] for piece in pieces) // spot_ref.shape[0]
    place = 0
    for piece in pieces:
        for start in range(0, piece.shape[1], width):
            there = pl.ds(pl.multiple_of(spot_ref[place] * width, width), width)
            out_ref[:, there] = (
                piece[:, start : start + width].astype(jnp.float32) + added_ref[:, there]
            ).astype(jnp.bfloat16)
            place += 1


def finish(pieces, spots, added):
    return pl.pallas_call(
        finish_kernel,
        out_shape=jax.ShapeDtypeStruct(added.shape, jnp.bfloat16),
        in_specs=[pl.BlockSpec(memory_space=pltpu.SMEM)]
        + [pl.BlockSpec(memory_space=pltpu.VMEM)] * (1 + len(pieces)),
        out_specs=pl.BlockSpec(memory_space=pltpu.VMEM),
        compiler_params=pltpu.CompilerParams(vmem_limit_bytes=24 << 20),
        cost_estimate=pl.CostEstimate(
            flops=added.size, bytes_accessed=8 * added.size, transcendentals=0
        ),
        name="finish",
    )(spots, added, *pieces)


def dp_pieces(down_turned, up_local):
    rank, rows = down_turned.shape
    width = rows // 16
    return jnp.concatenate(
        [
            down_turned.reshape(rank, 4, 4, width).transpose(2, 1, 0, 3),
            up_local.reshape(4, 16, -1, width).transpose(2, 0, 1, 3).reshape(4, 4, -1, width),
        ],
        axis=2,
    ).astype(jnp.bfloat16)


def results_kernel(every_ref, down_ref, query_ref, key_value_ref):
    rank = down_ref.shape[0]
    width = every_ref.shape[3]
    each = (every_ref.shape[2] - rank) // 16
    for hi in range(4):
        for lo in range(4):
            piece = every_ref[lo, hi].astype(jnp.float32)
            start = (hi * 4 + lo) * width
            down_ref[:, start : start + width] = piece[:rank]
            for n in range(each):
                part = piece[rank + n * 16 : rank + (n + 1) * 16]
                column, row = divmod((lo * 4 + hi) * each + n, 4)
                rows = slice(row * 16, (row + 1) * 16)
                column = column * width
                if column < query_ref.shape[1]:
                    query_ref[rows, column : column + width] = part
                else:
                    which, column = divmod(column - query_ref.shape[1], key_value_ref.shape[2])
                    key_value_ref[which, rows, column : column + width] = part


def dp_results(every, rank, q_width, k_width):
    width = every.shape[3]
    down_turned, query, key_value = pl.pallas_call(
        results_kernel,
        out_shape=(
            jax.ShapeDtypeStruct((rank, 16 * width), jnp.float32),
            jax.ShapeDtypeStruct((ADAPTER_RANK, q_width), jnp.float32),
            jax.ShapeDtypeStruct((2, ADAPTER_RANK, k_width), jnp.float32),
        ),
        in_specs=[pl.BlockSpec(memory_space=pltpu.VMEM)],
        out_specs=(pl.BlockSpec(memory_space=pltpu.VMEM),) * 3,
        compiler_params=pltpu.CompilerParams(vmem_limit_bytes=24 << 20),
        cost_estimate=pl.CostEstimate(
            flops=every.size, bytes_accessed=6 * every.size, transcendentals=0
        ),
        name="results",
    )(every)
    return down_turned.T, query, key_value


def scatter_sum(value, axis):
    return jnp.sum(
        lax.all_to_all(value, axis, 0, 0), axis=0, dtype=jnp.float32
    ).astype(jnp.bfloat16)


def gather(value, axis):
    return lax.all_to_all(jnp.broadcast_to(value[None], (4, *value.shape)), axis, 0, 0)


def chain_hi(own, first):
    right, left = [own], [own]
    for step in range(1, 4):
        right.append(move_hi(right[-1], 1, step - 1, 2))
        left.append(move_hi(left[-1], -1, 1, 4 - step))
        if step == 1:
            right[1], left[1] = after((right[1], left[1]), first)
    return right[1:], left[1:]


def fast_shards():
    def shards(
        normed,
        stored_queries,
        stored_keys,
        stored_values,
        head_output_grad,
        document_index,
        query_projection_weight,
        key_projection_weight,
        value_projection_weight,
        adapter_down_maps,
        query_up_map,
        key_value_up_maps,
    ):
        hi, lo, core = (lax.axis_index(name) for name in AXES)
        parts = (query_projection_weight, key_projection_weight, value_projection_weight)
        cut = query_projection_weight.shape[0] // 2
        own_a = jnp.concatenate([w[:cut] for w in parts], axis=1)
        own_b = jnp.concatenate([w[cut:] for w in parts], axis=1)
        x_a, y_a = swap_lo(own_a, 1), swap_lo(own_a, 2)
        next_b = after(own_b, (x_a, y_a))
        x_b, y_b = swap_lo(next_b, 1), swap_lo(next_b, 2)
        document_index = after(document_index, own_a)

        own, middle_part = attention(
            stored_queries,
            stored_keys,
            stored_values,
            head_output_grad,
            document_index[0],
            query_up_map,
            key_value_up_maps,
        )
        q_width = stored_queries.shape[1]
        k_width = stored_keys.shape[1]
        query_gradient = own[:, :q_width]
        key_gradient = own[:, q_width : q_width + k_width]
        value_gradient = own[:, q_width + k_width :]
        right, left = chain_hi(own, (x_a, y_a))
        blocks = (own, *right, *left)
        from_a, from_b = after((x_a, y_b), (x_b, right[1], left[1]))
        weights = (own_a, own_b, x_a, x_b, y_a, y_b, swap_lo(from_a, 2), swap_lo(from_b, 1))

        middle_local = jnp.concatenate(
            [
                jnp.dot(normed, adapter_down_maps, preferred_element_type=jnp.float32),
                middle_part,
            ],
            axis=1,
        )
        middle = (middle_local + swap_core(middle_local)).astype(jnp.bfloat16)
        middle = after(middle, (x_a, y_a))
        rank = adapter_down_maps.shape[1]
        adapter_middle, middle_gradient = middle[:, :rank], middle[:, rank:]
        down_turned = lax.dot_general(
            middle_gradient, normed, (((0,), (0,)), ((), ())), preferred_element_type=jnp.float32
        )
        ups = up_gradients(adapter_middle, query_gradient, key_gradient, value_gradient)
        down_turned, ups = after((down_turned, ups), (right[0], left[0]))
        up_local = jnp.concatenate(ups, axis=1)
        column = scatter_sum(dp_pieces(down_turned, up_local), "lo")
        piece = scatter_sum(after(column, (right[1], left[1])), "hi")
        tokens = own.shape[0]
        source = (hi % 2) * 2 + core

        def owner(step):
            return lambda hi, lo, core: (((hi % 2) * 2 + core + step) % 4, lo, hi // 2)

        added = rows_product(middle_gradient, adapter_down_maps)
        line = after(gather(after(piece, (right[2], left[2])), "hi"), weights[-2:])
        sent, kept = term_halves(after(blocks, line), weights, core, hi)
        summed = kept.astype(jnp.float32) + swap_core(sent).astype(jnp.float32)
        summed = summed.astype(jnp.bfloat16).reshape(4, tokens, -1)
        received = [
            send(pick(summed, (source + step) % 4, 0), owner(step)) for step in range(4)
        ]
        every = after(gather(line, "lo"), received[0])
        down_total, query_total, key_value_total = dp_results(every, rank, q_width, k_width)

        spots = [
            (((hi - step) % 4) // 2) * 16 + (lo ^ block) * 4 + part * 2 + (hi - step) % 2
            for step in range(4)
            for block in range(4)
            for part in range(2)
        ]
        normed_input_grad = finish(received, jnp.stack(spots).astype(jnp.int32), added)
        return (normed_input_grad, down_total, query_total, key_value_total)

    return shards


def solution(mesh):
    ranks = mesh.shape["dp"]
    tensor = mesh.shape["tensor"]
    inner = math.gcd(ranks, 4)
    outer = ranks // inner
    split = Mesh(mesh.devices.reshape(outer, inner, tensor), AXES)
    rows = ("hi", "lo")
    in_specs = (
        P(rows, "tensor"),
        P(rows, "tensor"),
        P(rows, "tensor"),
        P(rows, "tensor"),
        P(rows, "tensor"),
        P(rows, None),
        P(rows, "tensor"),
        P(rows, "tensor"),
        P(rows, "tensor"),
        P("tensor", None),
        P(None, "tensor"),
        P(None, None, "tensor"),
    )
    out_specs = (P(rows, "tensor"), P("tensor", None), P(None, "tensor"), P(None, None, "tensor"))
    return jax.shard_map(
        fast_shards() if (outer, inner, tensor) == SIZES else general_shards(outer, inner, tensor),
        mesh=split,
        in_specs=in_specs,
        out_specs=out_specs,
        check_vma=False,
    )
```

```python
import math

import jax
import jax.numpy as jnp
from jax import lax
from jax.experimental import pallas as pl
from jax.experimental.pallas import tpu as pltpu
from jax.sharding import Mesh
from jax.sharding import PartitionSpec as P

QUERY_HEADS = 32
KEY_HEADS = 8
HEAD_SIZE = 128
ADAPTER_RANK = 64


adapter_scale = 0.5


def attention_backward(queries, keyrows, value_row_block, output_gradient, ids):
    token_count = queries.shape[0]
    key_value_heads = keyrows.shape[1] // HEAD_SIZE
    query_group = QUERY_HEADS // KEY_HEADS
    scale = 1.0 / math.sqrt(HEAD_SIZE)
    qmat = queries.reshape(token_count, key_value_heads, query_group, HEAD_SIZE)
    kmat = keyrows.reshape(token_count, key_value_heads, HEAD_SIZE)
    value_matrix = value_row_block.reshape(token_count, key_value_heads, HEAD_SIZE)
    output_matrix = output_gradient.reshape(token_count, key_value_heads, query_group, HEAD_SIZE)
    same = ids[:, None] == ids[None, :]
    scores = jnp.einsum("bmav,wmv->mabw", qmat, kmat, preferred_element_type=jnp.float32) * scale
    scores = jnp.where(same[None, None], scores, -1e30)
    probs = jax.nn.softmax(scores, axis=-1)
    probs_half = probs.astype(jnp.bfloat16)
    value_gradient = jnp.einsum(
        "kgtu,tkgd->ukd", probs_half, output_matrix, preferred_element_type=jnp.float32
    ).astype(jnp.bfloat16)
    probability_grad = jnp.einsum(
        "bmav,wmv->mabw", output_matrix, value_matrix, preferred_element_type=jnp.float32
    )
    row_dots = jnp.sum(probs * probability_grad, axis=-1, keepdims=True)
    score_grad = (probs * (probability_grad - row_dots) * scale).astype(jnp.bfloat16)
    query_gradient = jnp.einsum(
        "kgtu,ukd->tkgd", score_grad, kmat, preferred_element_type=jnp.float32
    ).astype(jnp.bfloat16)
    key_gradient = jnp.einsum(
        "kgtu,tkgd->ukd", score_grad, qmat, preferred_element_type=jnp.float32
    ).astype(jnp.bfloat16)
    return (
        query_gradient.reshape(token_count, -1),
        key_gradient.reshape(token_count, -1),
        value_gradient.reshape(token_count, -1),
    )


def rows_product(left, piece):
    return lax.dot_general(
        left, piece, (((1,), (1,)), ((), ())), preferred_element_type=jnp.float32
    )


def up_gradients(adapter_middle, query_gradient, key_gradient, value_gradient):
    rank = ADAPTER_RANK
    parts = []
    for place, gradient in enumerate((query_gradient, key_gradient, value_gradient)):
        parts.append(
            adapter_scale
            * lax.dot_general(
                adapter_middle[:, place * rank : (place + 1) * rank],
                gradient,
                (((0,), (0,)), ((), ())),
                preferred_element_type=jnp.float32,
            )
        )
    return parts


def general_shards(outer, inner, tensor):
    every = ("hi", "lo")

    def shards(
        normed,
        stored_queries,
        stored_keys,
        stored_values,
        head_output_grad,
        document_index,
        query_projection_weight,
        key_projection_weight,
        value_projection_weight,
        adapter_down_maps,
        query_up_map,
        key_value_up_maps,
    ):
        weights = lax.all_gather(
            jnp.concatenate(
                [query_projection_weight, key_projection_weight, value_projection_weight], axis=1
            ),
            "lo",
            axis=0,
            tiled=True,
        )
        query_gradient, key_gradient, value_gradient = attention_backward(
            stored_queries, stored_keys, stored_values, head_output_grad, document_index[0]
        )
        own = jnp.concatenate([query_gradient, key_gradient, value_gradient], axis=1)
        gathered = lax.all_gather(own, "hi", axis=0, tiled=True)
        local_middle = jnp.dot(normed, adapter_down_maps, preferred_element_type=jnp.float32)
        grad_local = jnp.concatenate(
            [
                adapter_scale * rows_product(query_gradient, query_up_map),
                adapter_scale * rows_product(key_gradient, key_value_up_maps[0]),
                adapter_scale * rows_product(value_gradient, key_value_up_maps[1]),
            ],
            axis=1,
        )
        middle_total, grad_sum = (
            lax.psum(local_middle.astype(jnp.bfloat16), "tensor").astype(jnp.float32),
            lax.psum(grad_local.astype(jnp.bfloat16), "tensor").astype(jnp.float32),
        )
        adapter_middle = middle_total.astype(jnp.bfloat16)
        middle_gradient = grad_sum.astype(jnp.bfloat16)

        down_local = lax.dot_general(
            normed, middle_gradient, (((0,), (0,)), ((), ())), preferred_element_type=jnp.float32
        )
        ups = up_gradients(adapter_middle, query_gradient, key_gradient, value_gradient)
        up_local = jnp.concatenate(ups, axis=1)
        down_piece = lax.psum_scatter(down_local, every, scatter_dimension=0, tiled=True)
        up_piece = lax.psum_scatter(up_local, every, scatter_dimension=1, tiled=True)
        down_total = lax.all_gather(down_piece, every, axis=0, tiled=True)
        up_total = lax.all_gather(up_piece, every, axis=1, tiled=True)
        q_width = query_gradient.shape[1]
        k_width = key_gradient.shape[1]
        query_total = up_total[:, :q_width]
        key_value_total = jnp.stack(
            [up_total[:, q_width : q_width + k_width], up_total[:, q_width + k_width :]]
        )

        term = rows_product(gathered, weights).astype(jnp.bfloat16)
        tokens = own.shape[0]
        block = weights.shape[0]
        summed = lax.psum_scatter(term, "tensor", scatter_dimension=1, tiled=True)
        piece = block // tensor
        moved = lax.all_to_all(
            summed.reshape(outer, tokens, piece), "hi", split_axis=0, concat_axis=0, tiled=True
        )
        moved = moved.reshape(tensor, outer // tensor, tokens, piece)
        moved = lax.all_to_all(moved, "tensor", split_axis=0, concat_axis=0, tiled=True)
        base = moved.transpose(2, 1, 0, 3).reshape(tokens, -1).astype(jnp.float32)
        normed_input_grad = (base + rows_product(middle_gradient, adapter_down_maps)).astype(
            jnp.bfloat16
        )
        return (normed_input_grad, down_total, query_total, key_value_total)

    return shards


SIZES = (4, 4, 2)
AXES = ("hi", "lo", "tensor")


def send(value, target):
    pairs = []
    for rank in range(32):
        hi, lo, core = rank // 8, rank // 2 % 4, rank % 2
        there = target(hi, lo, core)
        if there is not None:
            pairs.append((rank, there[0] * 8 + there[1] * 2 + there[2]))
    return lax.ppermute(value, AXES, pairs)


def after(value, first):
    return lax.optimization_barrier((value, first))[0]


def swap_lo(value, bit):
    return send(value, lambda hi, lo, core: (hi, lo ^ bit, core))


def swap_core(value):
    return send(value, lambda hi, lo, core: (hi, lo, 1 - core))


def move_hi(value, step, first, last):
    return send(
        value,
        lambda hi, lo, core: (hi + step, lo, core) if first <= hi <= last else None,
    )


def pick(value, index, axis):
    return lax.dynamic_index_in_dim(value, index, axis, keepdims=False)


def attention_kernel(
    query_ref, key_ref, value_ref, grad_ref, row_ids, column_ids, up_ref, key_up_ref, own_ref, middle_ref
):
    head = pl.program_id(0)
    group = query_ref.shape[1] // HEAD_SIZE
    scale = 1.0 / math.sqrt(HEAD_SIZE)
    tokens = query_ref.shape[0]

    def stacked(ref):
        return jnp.concatenate(
            [ref[:, j * HEAD_SIZE : (j + 1) * HEAD_SIZE] for j in range(group)], axis=0
        )

    def product(left, right, dims):
        return lax.dot_general(
            left, right, ((dims[:1], dims[1:]), ((), ())), preferred_element_type=jnp.float32
        )

    queries, gradients = stacked(query_ref), stacked(grad_ref)
    keys, values = key_ref[...], value_ref[...]
    same = jnp.concatenate([row_ids[...] == column_ids[...]] * group, axis=0)
    scores = jnp.where(same, product(queries, keys, (1, 1)) * scale, -1e30)
    raised = jnp.exp(scores - jnp.max(scores, axis=-1, keepdims=True))
    probs = raised / jnp.sum(raised, axis=-1, keepdims=True)
    value_gradient = product(probs.astype(jnp.bfloat16), gradients, (0, 0)).astype(jnp.bfloat16)
    prob_grad = product(gradients, values, (1, 1))
    dots = jnp.sum(probs * prob_grad, axis=-1, keepdims=True)
    score_grad = (probs * (prob_grad - dots) * scale).astype(jnp.bfloat16)
    stacked_gradient = product(score_grad, keys, (1, 0)).astype(jnp.bfloat16)
    key_gradient = product(score_grad, queries, (0, 0)).astype(jnp.bfloat16)
    query_gradient = jnp.concatenate(
        [stacked_gradient[j * tokens : (j + 1) * tokens] for j in range(group)], axis=1
    )

    count = own_ref.shape[1] // ((group + 2) * HEAD_SIZE)

    def columns(start, width):
        return pl.ds(pl.multiple_of(start, HEAD_SIZE), width)

    own_ref[:, columns(head * group * HEAD_SIZE, group * HEAD_SIZE)] = query_gradient
    own_ref[:, columns((count * group + head) * HEAD_SIZE, HEAD_SIZE)] = key_gradient
    own_ref[:, columns((count * (group + 1) + head) * HEAD_SIZE, HEAD_SIZE)] = value_gradient

    @pl.when(head == 0)
    def _():
        middle_ref[...] = jnp.zeros_like(middle_ref)

    middle_ref[...] += adapter_scale * jnp.concatenate(
        [
            product(query_gradient, up_ref[...], (1, 1)),
            product(key_gradient, key_up_ref[0], (1, 1)),
            product(value_gradient, key_up_ref[1], (1, 1)),
        ],
        axis=1,
    )


def attention(queries, keys, values, gradients, ids, query_up_map, key_value_up_maps):
    tokens, key_width = keys.shape
    heads = key_width // HEAD_SIZE
    wide = queries.shape[1] // heads
    rank = query_up_map.shape[0]
    return pl.pallas_call(
        attention_kernel,
        out_shape=(
            jax.ShapeDtypeStruct((tokens, queries.shape[1] + 2 * key_width), jnp.bfloat16),
            jax.ShapeDtypeStruct((tokens, 3 * rank), jnp.float32),
        ),
        grid=(heads,),
        in_specs=[
            pl.BlockSpec((tokens, wide), lambda h: (0, h)),
            pl.BlockSpec((tokens, HEAD_SIZE), lambda h: (0, h)),
            pl.BlockSpec((tokens, HEAD_SIZE), lambda h: (0, h)),
            pl.BlockSpec((tokens, wide), lambda h: (0, h)),
            pl.BlockSpec((tokens, 1), lambda h: (0, 0)),
            pl.BlockSpec((1, tokens), lambda h: (0, 0)),
            pl.BlockSpec((rank, wide), lambda h: (0, h)),
            pl.BlockSpec((2, rank, HEAD_SIZE), lambda h: (0, 0, h)),
        ],
        out_specs=(
            pl.BlockSpec((tokens, queries.shape[1] + 2 * key_width), lambda h: (0, 0)),
            pl.BlockSpec((tokens, 3 * rank), lambda h: (0, 0)),
        ),
        compiler_params=pltpu.CompilerParams(vmem_limit_bytes=56 << 20),
        cost_estimate=pl.CostEstimate(
            flops=10 * tokens * tokens * queries.shape[1],
            bytes_accessed=6 * tokens * queries.shape[1],
            transcendentals=tokens * tokens * queries.shape[1] // HEAD_SIZE,
        ),
        name="attention",
    )(
        queries,
        keys,
        values,
        gradients,
        ids.reshape(tokens, 1),
        ids.reshape(1, tokens),
        query_up_map,
        key_value_up_maps,
    )


def term_kernel(place_ref, *refs):
    blocks, weights = refs[:7], refs[7:-6]
    sent_ref, kept_ref, left, right, arrived, landed = refs[-6:]
    tokens = blocks[0].shape[0]
    core, hi = place_ref[0], place_ref[1]
    rows = weights[0].shape[0] // 2
    pairs = len(weights) // 2
    steps = [(turn, n) for turn in range(2) for n in range(pairs)]

    def fetch(step):
        turn, n = steps[step]
        start = pl.multiple_of(lax.rem(core + 1 - turn, 2) * rows, rows)
        return [
            pltpu.make_async_copy(
                weights[2 * n + part].at[pl.ds(start, rows), :],
                right.at[step, pl.ds(part * rows, rows), :],
                landed.at[step, part],
            )
            for part in range(2)
        ]

    for n in range(4):
        there = left.at[pl.ds(n * tokens, tokens), :]
        for step, block in zip((0, 1, 2, 3, -1, -2, -3), blocks):

            @pl.when(hi == n + step)
            def _(block=block, there=there, n=n):
                pltpu.make_async_copy(block, there, arrived.at[n]).start()

    for copy in fetch(0):
        copy.start()
    for n in range(4):
        there = left.at[pl.ds(n * tokens, tokens), :]
        pltpu.make_async_copy(blocks[0], there, arrived.at[n]).wait()
    for step in range(1, len(steps)):
        for copy in fetch(step):
            copy.start()
    for step, (turn, n) in enumerate(steps):
        for copy in fetch(step):
            copy.wait()
        out_ref = (sent_ref, kept_ref)[turn]
        out_ref[:, n * 2 * rows : (n + 1) * 2 * rows] = lax.dot_general(
            left[...], right[step], (((1,), (1,)), ((), ())), preferred_element_type=jnp.float32
        ).astype(jnp.bfloat16)


def term_halves(blocks, weights, core, hi):
    tokens, depth = blocks[0].shape
    rows = weights[0].shape[0] // 2
    count = len(weights)
    out = jax.ShapeDtypeStruct((4 * tokens, count * rows), jnp.bfloat16)
    return pl.pallas_call(
        term_kernel,
        out_shape=(out, out),
        in_specs=[pl.BlockSpec(memory_space=pltpu.SMEM)]
        + [pl.BlockSpec(memory_space=pl.ANY)] * (7 + count),
        out_specs=(pl.BlockSpec(memory_space=pltpu.VMEM),) * 2,
        scratch_shapes=[
            pltpu.VMEM((4 * tokens, depth), jnp.bfloat16),
            pltpu.VMEM((count, 2 * rows, depth), jnp.bfloat16),
            pltpu.SemaphoreType.DMA((4,)),
            pltpu.SemaphoreType.DMA((count, 2)),
        ],
        compiler_params=pltpu.CompilerParams(vmem_limit_bytes=40 << 20),
        cost_estimate=pl.CostEstimate(
            flops=16 * tokens * depth * rows * count,
            bytes_accessed=8 * tokens * depth + (4 * rows * depth + 16 * tokens * rows) * count,
            transcendentals=0,
        ),
        name="term",
    )(jnp.stack([core, hi]), *blocks, *weights)


def finish_kernel(spot_ref, added_ref, *refs):
    pieces, out_ref = refs[:-1], refs[-1]
    width = sum(piece.shape[1] for piece in pieces) // spot_ref.shape[0]
    place = 0
    for piece in pieces:
        for start in range(0, piece.shape[1], width):
            there = pl.ds(pl.multiple_of(spot_ref[place] * width, width), width)
            out_ref[:, there] = (
                piece[:, start : start + width].astype(jnp.float32) + added_ref[:, there]
            ).astype(jnp.bfloat16)
            place += 1


def finish(pieces, spots, added):
    return pl.pallas_call(
        finish_kernel,
        out_shape=jax.ShapeDtypeStruct(added.shape, jnp.bfloat16),
        in_specs=[pl.BlockSpec(memory_space=pltpu.SMEM)]
        + [pl.BlockSpec(memory_space=pltpu.VMEM)] * (1 + len(pieces)),
        out_specs=pl.BlockSpec(memory_space=pltpu.VMEM),
        compiler_params=pltpu.CompilerParams(vmem_limit_bytes=24 << 20),
        cost_estimate=pl.CostEstimate(
            flops=added.size, bytes_accessed=8 * added.size, transcendentals=0
        ),
        name="finish",
    )(spots, added, *pieces)


def pieces_kernel(middle_ref, normed_ref, own_ref, out_ref):
    rank = middle_ref.shape[1] // 2
    width = out_ref.shape[3]
    each = (out_ref.shape[2] - rank) // 16
    heads = own_ref.shape[1] // 6

    def product(left, right):
        return lax.dot_general(
            left, right, (((0,), (0,)), ((), ())), preferred_element_type=jnp.float32
        )

    turned = middle_ref[:, rank:]
    for hi in range(4):
        for lo in range(4):
            start = (hi * 4 + lo) * width
            down = product(turned, normed_ref[:, start : start + width])
            out_ref[lo, hi, :rank, :] = down.astype(jnp.bfloat16)
    for column in range(own_ref.shape[1] // width):
        which = max(column * width // heads - 3, 0)
        part = middle_ref[:, which * ADAPTER_RANK : (which + 1) * ADAPTER_RANK]
        up = adapter_scale * product(part, own_ref[:, column * width : (column + 1) * width])
        for row in range(4):
            owner, n = divmod(column * 4 + row, each)
            lo, hi = divmod(owner, 4)
            out_ref[lo, hi, rank + n * 16 : rank + (n + 1) * 16, :] = up[
                row * 16 : (row + 1) * 16
            ].astype(jnp.bfloat16)


def dp_pieces(middle, normed, own):
    rank = middle.shape[1] // 2
    width = normed.shape[1] // 16
    rows = rank + ADAPTER_RANK * own.shape[1] // (16 * width)
    return pl.pallas_call(
        pieces_kernel,
        out_shape=jax.ShapeDtypeStruct((4, 4, rows, width), jnp.bfloat16),
        in_specs=[pl.BlockSpec(memory_space=pltpu.VMEM)] * 3,
        out_specs=pl.BlockSpec(memory_space=pltpu.VMEM),
        compiler_params=pltpu.CompilerParams(vmem_limit_bytes=24 << 20),
        cost_estimate=pl.CostEstimate(
            flops=2 * normed.size * rank + 2 * own.size * ADAPTER_RANK,
            bytes_accessed=2 * (normed.size + own.size) + 32 * rows * width,
            transcendentals=0,
        ),
        name="pieces",
    )(middle, normed, own)


def results_kernel(every_ref, down_ref, query_ref, key_value_ref):
    rank = down_ref.shape[0]
    width = every_ref.shape[3]
    each = (every_ref.shape[2] - rank) // 16
    for hi in range(4):
        for lo in range(4):
            piece = every_ref[lo, hi].astype(jnp.float32)
            start = (hi * 4 + lo) * width
            down_ref[:, start : start + width] = piece[:rank]
            for n in range(each):
                part = piece[rank + n * 16 : rank + (n + 1) * 16]
                column, row = divmod((lo * 4 + hi) * each + n, 4)
                rows = slice(row * 16, (row + 1) * 16)
                column = column * width
                if column < query_ref.shape[1]:
                    query_ref[rows, column : column + width] = part
                else:
                    which, column = divmod(column - query_ref.shape[1], key_value_ref.shape[2])
                    key_value_ref[which, rows, column : column + width] = part


def dp_results(every, rank, q_width, k_width):
    width = every.shape[3]
    down_turned, query, key_value = pl.pallas_call(
        results_kernel,
        out_shape=(
            jax.ShapeDtypeStruct((rank, 16 * width), jnp.float32),
            jax.ShapeDtypeStruct((ADAPTER_RANK, q_width), jnp.float32),
            jax.ShapeDtypeStruct((2, ADAPTER_RANK, k_width), jnp.float32),
        ),
        in_specs=[pl.BlockSpec(memory_space=pltpu.VMEM)],
        out_specs=(pl.BlockSpec(memory_space=pltpu.VMEM),) * 3,
        compiler_params=pltpu.CompilerParams(vmem_limit_bytes=24 << 20),
        cost_estimate=pl.CostEstimate(
            flops=every.size, bytes_accessed=6 * every.size, transcendentals=0
        ),
        name="results",
    )(every)
    return down_turned.T, query, key_value


def scatter_sum(value, axis):
    return jnp.sum(
        lax.all_to_all(value, axis, 0, 0), axis=0, dtype=jnp.float32
    ).astype(jnp.bfloat16)


def gather(value, axis):
    return lax.all_to_all(jnp.broadcast_to(value[None], (4, *value.shape)), axis, 0, 0)


def chain_hi(own, first):
    right, left = [own], [own]
    for step in range(1, 4):
        right.append(move_hi(right[-1], 1, step - 1, 2))
        left.append(move_hi(left[-1], -1, 1, 4 - step))
        if step == 1:
            right[1], left[1] = after((right[1], left[1]), first)
    return right[1:], left[1:]


def fast_shards():
    def shards(
        normed,
        stored_queries,
        stored_keys,
        stored_values,
        head_output_grad,
        document_index,
        query_projection_weight,
        key_projection_weight,
        value_projection_weight,
        adapter_down_maps,
        query_up_map,
        key_value_up_maps,
    ):
        hi, lo, core = (lax.axis_index(name) for name in AXES)
        parts = (query_projection_weight, key_projection_weight, value_projection_weight)
        cut = query_projection_weight.shape[0] // 2
        own_a = jnp.concatenate([w[:cut] for w in parts], axis=1)
        own_b = jnp.concatenate([w[cut:] for w in parts], axis=1)
        x_a, y_a = swap_lo(own_a, 1), swap_lo(own_a, 2)
        next_b = after(own_b, (x_a, y_a))
        x_b, y_b = swap_lo(next_b, 1), swap_lo(next_b, 2)
        document_index = after(document_index, own_a)

        own, middle_part = attention(
            stored_queries,
            stored_keys,
            stored_values,
            head_output_grad,
            document_index[0],
            query_up_map,
            key_value_up_maps,
        )
        q_width = stored_queries.shape[1]
        k_width = stored_keys.shape[1]
        query_gradient = own[:, :q_width]
        key_gradient = own[:, q_width : q_width + k_width]
        value_gradient = own[:, q_width + k_width :]
        right, left = chain_hi(own, (x_a, y_a))
        blocks = (own, *right, *left)
        from_a, from_b = after((x_a, y_b), (x_b, right[1], left[1]))
        weights = (own_a, own_b, x_a, x_b, y_a, y_b, swap_lo(from_a, 2), swap_lo(from_b, 1))

        middle_local = jnp.concatenate(
            [
                jnp.dot(normed, adapter_down_maps, preferred_element_type=jnp.float32),
                middle_part,
            ],
            axis=1,
        )
        middle = (middle_local + swap_core(middle_local)).astype(jnp.bfloat16)
        middle = after(middle, (x_a, y_a))
        rank = adapter_down_maps.shape[1]
        adapter_middle, middle_gradient = middle[:, :rank], middle[:, rank:]
        column = scatter_sum(dp_pieces(middle, normed, own), "lo")
        piece = scatter_sum(after(column, (right[1], left[1])), "hi")
        tokens = own.shape[0]
        source = (hi % 2) * 2 + core

        def owner(step):
            return lambda hi, lo, core: (((hi % 2) * 2 + core + step) % 4, lo, hi // 2)

        added = rows_product(middle_gradient, adapter_down_maps)
        line = after(gather(after(piece, (right[2], left[2])), "hi"), weights[-2:])
        sent, kept = term_halves(after(blocks, line), weights, core, hi)
        summed = kept.astype(jnp.float32) + swap_core(sent).astype(jnp.float32)
        summed = summed.astype(jnp.bfloat16).reshape(4, tokens, -1)
        received = [
            send(pick(summed, (source + step) % 4, 0), owner(step)) for step in range(4)
        ]
        every = after(gather(line, "lo"), received[0])
        down_total, query_total, key_value_total = dp_results(every, rank, q_width, k_width)

        spots = [
            (((hi - step) % 4) // 2) * 16 + (lo ^ block) * 4 + part * 2 + (hi - step) % 2
            for step in range(4)
            for block in range(4)
            for part in range(2)
        ]
        normed_input_grad = finish(received, jnp.stack(spots).astype(jnp.int32), added)
        return (normed_input_grad, down_total, query_total, key_value_total)

    return shards


def solution(mesh):
    ranks = mesh.shape["dp"]
    tensor = mesh.shape["tensor"]
    inner = math.gcd(ranks, 4)
    outer = ranks // inner
    split = Mesh(mesh.devices.reshape(outer, inner, tensor), AXES)
    rows = ("hi", "lo")
    in_specs = (
        P(rows, "tensor"),
        P(rows, "tensor"),
        P(rows, "tensor"),
        P(rows, "tensor"),
        P(rows, "tensor"),
        P(rows, None),
        P(rows, "tensor"),
        P(rows, "tensor"),
        P(rows, "tensor"),
        P("tensor", None),
        P(None, "tensor"),
        P(None, None, "tensor"),
    )
    out_specs = (P(rows, "tensor"), P("tensor", None), P(None, "tensor"), P(None, None, "tensor"))
    return jax.shard_map(
        fast_shards() if (outer, inner, tensor) == SIZES else general_shards(outer, inner, tensor),
        mesh=split,
        in_specs=in_specs,
        out_specs=out_specs,
        check_vma=False,
    )
```

```python
import math

import jax
import jax.numpy as jnp
from jax import lax
from jax.experimental import pallas as pl
from jax.experimental.pallas import tpu as pltpu
from jax.sharding import Mesh
from jax.sharding import PartitionSpec as P

QUERY_HEADS = 32
KEY_HEADS = 8
HEAD_SIZE = 128
ADAPTER_RANK = 64


adapter_scale = 0.5


def attention_backward(queries, keyrows, value_row_block, output_gradient, ids):
    token_count = queries.shape[0]
    key_value_heads = keyrows.shape[1] // HEAD_SIZE
    query_group = QUERY_HEADS // KEY_HEADS
    scale = 1.0 / math.sqrt(HEAD_SIZE)
    qmat = queries.reshape(token_count, key_value_heads, query_group, HEAD_SIZE)
    kmat = keyrows.reshape(token_count, key_value_heads, HEAD_SIZE)
    value_matrix = value_row_block.reshape(token_count, key_value_heads, HEAD_SIZE)
    output_matrix = output_gradient.reshape(token_count, key_value_heads, query_group, HEAD_SIZE)
    same = ids[:, None] == ids[None, :]
    scores = jnp.einsum("bmav,wmv->mabw", qmat, kmat, preferred_element_type=jnp.float32) * scale
    scores = jnp.where(same[None, None], scores, -1e30)
    probs = jax.nn.softmax(scores, axis=-1)
    probs_half = probs.astype(jnp.bfloat16)
    value_gradient = jnp.einsum(
        "kgtu,tkgd->ukd", probs_half, output_matrix, preferred_element_type=jnp.float32
    ).astype(jnp.bfloat16)
    probability_grad = jnp.einsum(
        "bmav,wmv->mabw", output_matrix, value_matrix, preferred_element_type=jnp.float32
    )
    row_dots = jnp.sum(probs * probability_grad, axis=-1, keepdims=True)
    score_grad = (probs * (probability_grad - row_dots) * scale).astype(jnp.bfloat16)
    query_gradient = jnp.einsum(
        "kgtu,ukd->tkgd", score_grad, kmat, preferred_element_type=jnp.float32
    ).astype(jnp.bfloat16)
    key_gradient = jnp.einsum(
        "kgtu,tkgd->ukd", score_grad, qmat, preferred_element_type=jnp.float32
    ).astype(jnp.bfloat16)
    return (
        query_gradient.reshape(token_count, -1),
        key_gradient.reshape(token_count, -1),
        value_gradient.reshape(token_count, -1),
    )


def rows_product(left, piece):
    return lax.dot_general(
        left, piece, (((1,), (1,)), ((), ())), preferred_element_type=jnp.float32
    )


def up_gradients(adapter_middle, query_gradient, key_gradient, value_gradient):
    rank = ADAPTER_RANK
    parts = []
    for place, gradient in enumerate((query_gradient, key_gradient, value_gradient)):
        parts.append(
            adapter_scale
            * lax.dot_general(
                adapter_middle[:, place * rank : (place + 1) * rank],
                gradient,
                (((0,), (0,)), ((), ())),
                preferred_element_type=jnp.float32,
            )
        )
    return parts


def general_shards(outer, inner, tensor):
    every = ("hi", "lo")

    def shards(
        normed,
        stored_queries,
        stored_keys,
        stored_values,
        head_output_grad,
        document_index,
        query_projection_weight,
        key_projection_weight,
        value_projection_weight,
        adapter_down_maps,
        query_up_map,
        key_value_up_maps,
    ):
        weights = lax.all_gather(
            jnp.concatenate(
                [query_projection_weight, key_projection_weight, value_projection_weight], axis=1
            ),
            "lo",
            axis=0,
            tiled=True,
        )
        query_gradient, key_gradient, value_gradient = attention_backward(
            stored_queries, stored_keys, stored_values, head_output_grad, document_index[0]
        )
        own = jnp.concatenate([query_gradient, key_gradient, value_gradient], axis=1)
        gathered = lax.all_gather(own, "hi", axis=0, tiled=True)
        local_middle = jnp.dot(normed, adapter_down_maps, preferred_element_type=jnp.float32)
        grad_local = jnp.concatenate(
            [
                adapter_scale * rows_product(query_gradient, query_up_map),
                adapter_scale * rows_product(key_gradient, key_value_up_maps[0]),
                adapter_scale * rows_product(value_gradient, key_value_up_maps[1]),
            ],
            axis=1,
        )
        middle_total, grad_sum = (
            lax.psum(local_middle.astype(jnp.bfloat16), "tensor").astype(jnp.float32),
            lax.psum(grad_local.astype(jnp.bfloat16), "tensor").astype(jnp.float32),
        )
        adapter_middle = middle_total.astype(jnp.bfloat16)
        middle_gradient = grad_sum.astype(jnp.bfloat16)

        down_local = lax.dot_general(
            normed, middle_gradient, (((0,), (0,)), ((), ())), preferred_element_type=jnp.float32
        )
        ups = up_gradients(adapter_middle, query_gradient, key_gradient, value_gradient)
        up_local = jnp.concatenate(ups, axis=1)
        down_piece = lax.psum_scatter(down_local, every, scatter_dimension=0, tiled=True)
        up_piece = lax.psum_scatter(up_local, every, scatter_dimension=1, tiled=True)
        down_total = lax.all_gather(down_piece, every, axis=0, tiled=True)
        up_total = lax.all_gather(up_piece, every, axis=1, tiled=True)
        q_width = query_gradient.shape[1]
        k_width = key_gradient.shape[1]
        query_total = up_total[:, :q_width]
        key_value_total = jnp.stack(
            [up_total[:, q_width : q_width + k_width], up_total[:, q_width + k_width :]]
        )

        term = rows_product(gathered, weights).astype(jnp.bfloat16)
        tokens = own.shape[0]
        block = weights.shape[0]
        summed = lax.psum_scatter(term, "tensor", scatter_dimension=1, tiled=True)
        piece = block // tensor
        moved = lax.all_to_all(
            summed.reshape(outer, tokens, piece), "hi", split_axis=0, concat_axis=0, tiled=True
        )
        moved = moved.reshape(tensor, outer // tensor, tokens, piece)
        moved = lax.all_to_all(moved, "tensor", split_axis=0, concat_axis=0, tiled=True)
        base = moved.transpose(2, 1, 0, 3).reshape(tokens, -1).astype(jnp.float32)
        normed_input_grad = (base + rows_product(middle_gradient, adapter_down_maps)).astype(
            jnp.bfloat16
        )
        return (normed_input_grad, down_total, query_total, key_value_total)

    return shards


SIZES = (4, 4, 2)
AXES = ("hi", "lo", "tensor")


def send(value, target):
    pairs = []
    for rank in range(32):
        hi, lo, core = rank // 8, rank // 2 % 4, rank % 2
        there = target(hi, lo, core)
        if there is not None:
            pairs.append((rank, there[0] * 8 + there[1] * 2 + there[2]))
    return lax.ppermute(value, AXES, pairs)


def after(value, first):
    return lax.optimization_barrier((value, first))[0]


def swap_lo(value, bit):
    return send(value, lambda hi, lo, core: (hi, lo ^ bit, core))


def swap_core(value):
    return send(value, lambda hi, lo, core: (hi, lo, 1 - core))


def move_hi(value, step, first, last):
    return send(
        value,
        lambda hi, lo, core: (hi + step, lo, core) if first <= hi <= last else None,
    )


def pick(value, index, axis):
    return lax.dynamic_index_in_dim(value, index, axis, keepdims=False)


def attention_kernel(
    query_ref, key_ref, value_ref, grad_ref, row_ids, column_ids, up_ref, key_up_ref, own_ref, middle_ref
):
    head = pl.program_id(0)
    group = query_ref.shape[1] // HEAD_SIZE
    scale = 1.0 / math.sqrt(HEAD_SIZE)
    tokens = query_ref.shape[0]

    def stacked(ref):
        return jnp.concatenate(
            [ref[:, j * HEAD_SIZE : (j + 1) * HEAD_SIZE] for j in range(group)], axis=0
        )

    def product(left, right, dims):
        return lax.dot_general(
            left, right, ((dims[:1], dims[1:]), ((), ())), preferred_element_type=jnp.float32
        )

    queries, gradients = stacked(query_ref), stacked(grad_ref)
    keys, values = key_ref[...], value_ref[...]
    same = jnp.concatenate([row_ids[...] == column_ids[...]] * group, axis=0)
    scores = jnp.where(same, product(queries, keys, (1, 1)) * scale, -1e30)
    raised = jnp.exp(scores - jnp.max(scores, axis=-1, keepdims=True))
    probs = raised / jnp.sum(raised, axis=-1, keepdims=True)
    value_gradient = product(probs.astype(jnp.bfloat16), gradients, (0, 0)).astype(jnp.bfloat16)
    prob_grad = product(gradients, values, (1, 1))
    dots = jnp.sum(probs * prob_grad, axis=-1, keepdims=True)
    score_grad = (probs * (prob_grad - dots) * scale).astype(jnp.bfloat16)
    stacked_gradient = product(score_grad, keys, (1, 0)).astype(jnp.bfloat16)
    key_gradient = product(score_grad, queries, (0, 0)).astype(jnp.bfloat16)
    query_gradient = jnp.concatenate(
        [stacked_gradient[j * tokens : (j + 1) * tokens] for j in range(group)], axis=1
    )

    count = own_ref.shape[1] // ((group + 2) * HEAD_SIZE)

    def columns(start, width):
        return pl.ds(pl.multiple_of(start, HEAD_SIZE), width)

    own_ref[:, columns(head * group * HEAD_SIZE, group * HEAD_SIZE)] = query_gradient
    own_ref[:, columns((count * group + head) * HEAD_SIZE, HEAD_SIZE)] = key_gradient
    own_ref[:, columns((count * (group + 1) + head) * HEAD_SIZE, HEAD_SIZE)] = value_gradient

    @pl.when(head == 0)
    def _():
        middle_ref[...] = jnp.zeros_like(middle_ref)

    middle_ref[...] += adapter_scale * jnp.concatenate(
        [
            product(query_gradient, up_ref[...], (1, 1)),
            product(key_gradient, key_up_ref[0], (1, 1)),
            product(value_gradient, key_up_ref[1], (1, 1)),
        ],
        axis=1,
    )


def attention(queries, keys, values, gradients, ids, query_up_map, key_value_up_maps):
    tokens, key_width = keys.shape
    heads = key_width // HEAD_SIZE
    wide = queries.shape[1] // heads
    rank = query_up_map.shape[0]
    return pl.pallas_call(
        attention_kernel,
        out_shape=(
            jax.ShapeDtypeStruct((tokens, queries.shape[1] + 2 * key_width), jnp.bfloat16),
            jax.ShapeDtypeStruct((tokens, 3 * rank), jnp.float32),
        ),
        grid=(heads,),
        in_specs=[
            pl.BlockSpec((tokens, wide), lambda h: (0, h)),
            pl.BlockSpec((tokens, HEAD_SIZE), lambda h: (0, h)),
            pl.BlockSpec((tokens, HEAD_SIZE), lambda h: (0, h)),
            pl.BlockSpec((tokens, wide), lambda h: (0, h)),
            pl.BlockSpec((tokens, 1), lambda h: (0, 0)),
            pl.BlockSpec((1, tokens), lambda h: (0, 0)),
            pl.BlockSpec((rank, wide), lambda h: (0, h)),
            pl.BlockSpec((2, rank, HEAD_SIZE), lambda h: (0, 0, h)),
        ],
        out_specs=(
            pl.BlockSpec((tokens, queries.shape[1] + 2 * key_width), lambda h: (0, 0)),
            pl.BlockSpec((tokens, 3 * rank), lambda h: (0, 0)),
        ),
        compiler_params=pltpu.CompilerParams(vmem_limit_bytes=56 << 20),
        cost_estimate=pl.CostEstimate(
            flops=10 * tokens * tokens * queries.shape[1],
            bytes_accessed=6 * tokens * queries.shape[1],
            transcendentals=tokens * tokens * queries.shape[1] // HEAD_SIZE,
        ),
        name="attention",
    )(
        queries,
        keys,
        values,
        gradients,
        ids.reshape(tokens, 1),
        ids.reshape(1, tokens),
        query_up_map,
        key_value_up_maps,
    )


def term_kernel(place_ref, *refs):
    blocks, weights, (sent_ref, kept_ref, left, arrived) = refs[:7], refs[7:-4], refs[-4:]
    tokens = blocks[0].shape[0]
    hi = place_ref[1]

    @pl.when(pl.program_id(0) == 0)
    def _():
        for n in range(4):
            there = left.at[pl.ds(n * tokens, tokens), :]
            for step, block in zip((0, 1, 2, 3, -1, -2, -3), blocks):

                @pl.when(hi == n + step)
                def _(block=block, there=there, n=n):
                    pltpu.make_async_copy(block, there, arrived.at[n]).start()

        for n in range(4):
            there = left.at[pl.ds(n * tokens, tokens), :]
            pltpu.make_async_copy(blocks[0], there, arrived.at[n]).wait()

    for turn, out_ref in enumerate((sent_ref, kept_ref)):

        @pl.when(pl.program_id(0) == turn)
        def _(out_ref=out_ref):
            width = 2 * weights[0].shape[0]
            for n in range(len(weights) // 2):
                right = jnp.concatenate([weights[2 * n][...], weights[2 * n + 1][...]], axis=0)
                out_ref[:, n * width : (n + 1) * width] = lax.dot_general(
                    left[...], right, (((1,), (1,)), ((), ())), preferred_element_type=jnp.float32
                ).astype(jnp.bfloat16)


def term_halves(blocks, weights, core, hi):
    tokens, depth = blocks[0].shape
    rows = weights[0].shape[0] // 2
    count = len(weights)
    out = jax.ShapeDtypeStruct((4 * tokens, count * rows), jnp.bfloat16)
    return pl.pallas_call(
        term_kernel,
        out_shape=(out, out),
        grid_spec=pltpu.PrefetchScalarGridSpec(
            num_scalar_prefetch=1,
            grid=(2,),
            in_specs=[pl.BlockSpec(memory_space=pl.ANY)] * 7
            + [pl.BlockSpec((rows, depth), lambda i, place: (lax.rem(place[0] + 1 - i, 2), 0))]
            * count,
            out_specs=(pl.BlockSpec(out.shape, lambda i, place: (0, 0)),) * 2,
            scratch_shapes=[
                pltpu.VMEM((4 * tokens, depth), jnp.bfloat16),
                pltpu.SemaphoreType.DMA((4,)),
            ],
        ),
        compiler_params=pltpu.CompilerParams(vmem_limit_bytes=40 << 20),
        cost_estimate=pl.CostEstimate(
            flops=16 * tokens * depth * rows * count,
            bytes_accessed=8 * tokens * depth + (4 * rows * depth + 16 * tokens * rows) * count,
            transcendentals=0,
        ),
        name="term",
    )(jnp.stack([core, hi]), *blocks, *weights)


def finish_kernel(spot_ref, added_ref, *refs):
    pieces, out_ref = refs[:-1], refs[-1]
    width = sum(piece.shape[1] for piece in pieces) // spot_ref.shape[0]
    place = 0
    for piece in pieces:
        for start in range(0, piece.shape[1], width):
            there = pl.ds(pl.multiple_of(spot_ref[place] * width, width), width)
            out_ref[:, there] = (
                piece[:, start : start + width].astype(jnp.float32) + added_ref[:, there]
            ).astype(jnp.bfloat16)
            place += 1


def finish(pieces, spots, added):
    return pl.pallas_call(
        finish_kernel,
        out_shape=jax.ShapeDtypeStruct(added.shape, jnp.bfloat16),
        in_specs=[pl.BlockSpec(memory_space=pltpu.SMEM)]
        + [pl.BlockSpec(memory_space=pltpu.VMEM)] * (1 + len(pieces)),
        out_specs=pl.BlockSpec(memory_space=pltpu.VMEM),
        compiler_params=pltpu.CompilerParams(vmem_limit_bytes=24 << 20),
        cost_estimate=pl.CostEstimate(
            flops=added.size, bytes_accessed=8 * added.size, transcendentals=0
        ),
        name="finish",
    )(spots, added, *pieces)


def pieces_kernel(middle_ref, normed_ref, own_ref, out_ref):
    rank = middle_ref.shape[1] // 2
    width = out_ref.shape[3]
    each = (out_ref.shape[2] - rank) // 16
    heads = own_ref.shape[1] // 6

    def product(left, right):
        return lax.dot_general(
            left, right, (((0,), (0,)), ((), ())), preferred_element_type=jnp.float32
        )

    turned = middle_ref[:, rank:]
    for hi in range(4):
        for lo in range(4):
            start = (hi * 4 + lo) * width
            down = product(turned, normed_ref[:, start : start + width])
            out_ref[lo, hi, :rank, :] = down.astype(jnp.bfloat16)
    for column in range(own_ref.shape[1] // width):
        which = max(column * width // heads - 3, 0)
        part = middle_ref[:, which * ADAPTER_RANK : (which + 1) * ADAPTER_RANK]
        up = adapter_scale * product(part, own_ref[:, column * width : (column + 1) * width])
        for row in range(4):
            owner, n = divmod(column * 4 + row, each)
            lo, hi = divmod(owner, 4)
            out_ref[lo, hi, rank + n * 16 : rank + (n + 1) * 16, :] = up[
                row * 16 : (row + 1) * 16
            ].astype(jnp.bfloat16)


def dp_pieces(middle, normed, own):
    rank = middle.shape[1] // 2
    width = normed.shape[1] // 16
    rows = rank + ADAPTER_RANK * own.shape[1] // (16 * width)
    return pl.pallas_call(
        pieces_kernel,
        out_shape=jax.ShapeDtypeStruct((4, 4, rows, width), jnp.bfloat16),
        in_specs=[pl.BlockSpec(memory_space=pltpu.VMEM)] * 3,
        out_specs=pl.BlockSpec(memory_space=pltpu.VMEM),
        compiler_params=pltpu.CompilerParams(vmem_limit_bytes=24 << 20),
        cost_estimate=pl.CostEstimate(
            flops=2 * normed.size * rank + 2 * own.size * ADAPTER_RANK,
            bytes_accessed=2 * (normed.size + own.size) + 32 * rows * width,
            transcendentals=0,
        ),
        name="pieces",
    )(middle, normed, own)


def results_kernel(every_ref, down_ref, query_ref, key_value_ref):
    rank = down_ref.shape[0]
    width = every_ref.shape[3]
    each = (every_ref.shape[2] - rank) // 16
    for hi in range(4):
        for lo in range(4):
            piece = every_ref[lo, hi].astype(jnp.float32)
            start = (hi * 4 + lo) * width
            down_ref[:, start : start + width] = piece[:rank]
            for n in range(each):
                part = piece[rank + n * 16 : rank + (n + 1) * 16]
                column, row = divmod((lo * 4 + hi) * each + n, 4)
                rows = slice(row * 16, (row + 1) * 16)
                column = column * width
                if column < query_ref.shape[1]:
                    query_ref[rows, column : column + width] = part
                else:
                    which, column = divmod(column - query_ref.shape[1], key_value_ref.shape[2])
                    key_value_ref[which, rows, column : column + width] = part


def dp_results(every, rank, q_width, k_width):
    width = every.shape[3]
    down_turned, query, key_value = pl.pallas_call(
        results_kernel,
        out_shape=(
            jax.ShapeDtypeStruct((rank, 16 * width), jnp.float32),
            jax.ShapeDtypeStruct((ADAPTER_RANK, q_width), jnp.float32),
            jax.ShapeDtypeStruct((2, ADAPTER_RANK, k_width), jnp.float32),
        ),
        in_specs=[pl.BlockSpec(memory_space=pltpu.VMEM)],
        out_specs=(pl.BlockSpec(memory_space=pltpu.VMEM),) * 3,
        compiler_params=pltpu.CompilerParams(vmem_limit_bytes=24 << 20),
        cost_estimate=pl.CostEstimate(
            flops=every.size, bytes_accessed=6 * every.size, transcendentals=0
        ),
        name="results",
    )(every)
    return down_turned.T, query, key_value


def scatter_sum(value, axis):
    return jnp.sum(
        lax.all_to_all(value, axis, 0, 0), axis=0, dtype=jnp.float32
    ).astype(jnp.bfloat16)


def gather(value, axis):
    return lax.all_to_all(jnp.broadcast_to(value[None], (4, *value.shape)), axis, 0, 0)


def chain_hi(own, first):
    right, left = [own], [own]
    for step in range(1, 4):
        right.append(move_hi(right[-1], 1, step - 1, 2))
        left.append(move_hi(left[-1], -1, 1, 4 - step))
        if step == 1:
            right[1], left[1] = after((right[1], left[1]), first)
    return right[1:], left[1:]


def fast_shards():
    def shards(
        normed,
        stored_queries,
        stored_keys,
        stored_values,
        head_output_grad,
        document_index,
        query_projection_weight,
        key_projection_weight,
        value_projection_weight,
        adapter_down_maps,
        query_up_map,
        key_value_up_maps,
    ):
        hi, lo, core = (lax.axis_index(name) for name in AXES)
        parts = (query_projection_weight, key_projection_weight, value_projection_weight)
        cut = query_projection_weight.shape[0] // 2
        own_a = jnp.concatenate([w[:cut] for w in parts], axis=1)
        own_b = jnp.concatenate([w[cut:] for w in parts], axis=1)
        x_a, y_a = swap_lo(own_a, 1), swap_lo(own_a, 2)
        next_b = after(own_b, (x_a, y_a))
        x_b, y_b = swap_lo(next_b, 1), swap_lo(next_b, 2)
        document_index = after(document_index, own_a)

        own, middle_part = attention(
            stored_queries,
            stored_keys,
            stored_values,
            head_output_grad,
            document_index[0],
            query_up_map,
            key_value_up_maps,
        )
        q_width = stored_queries.shape[1]
        k_width = stored_keys.shape[1]
        query_gradient = own[:, :q_width]
        key_gradient = own[:, q_width : q_width + k_width]
        value_gradient = own[:, q_width + k_width :]
        middle_local = jnp.concatenate(
            [
                jnp.dot(normed, adapter_down_maps, preferred_element_type=jnp.float32),
                middle_part,
            ],
            axis=1,
        )
        middle = (middle_local + swap_core(middle_local)).astype(jnp.bfloat16)
        rank = adapter_down_maps.shape[1]
        adapter_middle, middle_gradient = middle[:, :rank], middle[:, rank:]
        laid = dp_pieces(middle, normed, own)
        right, left = chain_hi(own, (x_a, y_a, laid))
        blocks = (own, *right, *left)
        from_a, from_b = after((x_a, y_b), (x_b, right[1], left[1]))
        weights = (own_a, own_b, x_a, x_b, y_a, y_b, swap_lo(from_a, 2), swap_lo(from_b, 1))

        column = scatter_sum(laid, "lo")
        piece = scatter_sum(after(column, (right[1], left[1])), "hi")
        tokens = own.shape[0]
        source = (hi % 2) * 2 + core

        def owner(step):
            return lambda hi, lo, core: (((hi % 2) * 2 + core + step) % 4, lo, hi // 2)

        added = rows_product(middle_gradient, adapter_down_maps)
        line = after(gather(after(piece, (right[2], left[2])), "hi"), weights[-2:])
        sent, kept = term_halves(after(blocks, line), weights, core, hi)
        summed = kept.astype(jnp.float32) + swap_core(sent).astype(jnp.float32)
        summed = summed.astype(jnp.bfloat16).reshape(4, tokens, -1)
        received = [
            send(pick(summed, (source + step) % 4, 0), owner(step)) for step in range(4)
        ]
        every = after(gather(line, "lo"), received[0])
        down_total, query_total, key_value_total = dp_results(every, rank, q_width, k_width)

        spots = [
            (((hi - step) % 4) // 2) * 16 + (lo ^ block) * 4 + part * 2 + (hi - step) % 2
            for step in range(4)
            for block in range(4)
            for part in range(2)
        ]
        normed_input_grad = finish(received, jnp.stack(spots).astype(jnp.int32), added)
        return (normed_input_grad, down_total, query_total, key_value_total)

    return shards


def solution(mesh):
    ranks = mesh.shape["dp"]
    tensor = mesh.shape["tensor"]
    inner = math.gcd(ranks, 4)
    outer = ranks // inner
    split = Mesh(mesh.devices.reshape(outer, inner, tensor), AXES)
    rows = ("hi", "lo")
    in_specs = (
        P(rows, "tensor"),
        P(rows, "tensor"),
        P(rows, "tensor"),
        P(rows, "tensor"),
        P(rows, "tensor"),
        P(rows, None),
        P(rows, "tensor"),
        P(rows, "tensor"),
        P(rows, "tensor"),
        P("tensor", None),
        P(None, "tensor"),
        P(None, None, "tensor"),
    )
    out_specs = (P(rows, "tensor"), P("tensor", None), P(None, "tensor"), P(None, None, "tensor"))
    return jax.shard_map(
        fast_shards() if (outer, inner, tensor) == SIZES else general_shards(outer, inner, tensor),
        mesh=split,
        in_specs=in_specs,
        out_specs=out_specs,
        check_vma=False,
    )
```

```python
import math

import jax
import jax.numpy as jnp
from jax import lax
from jax.experimental import pallas as pl
from jax.experimental.pallas import tpu as pltpu
from jax.sharding import Mesh
from jax.sharding import PartitionSpec as P

QUERY_HEADS = 32
KEY_HEADS = 8
HEAD_SIZE = 128
ADAPTER_RANK = 64


adapter_scale = 0.5


def attention_backward(queries, keyrows, value_row_block, output_gradient, ids):
    token_count = queries.shape[0]
    key_value_heads = keyrows.shape[1] // HEAD_SIZE
    query_group = QUERY_HEADS // KEY_HEADS
    scale = 1.0 / math.sqrt(HEAD_SIZE)
    qmat = queries.reshape(token_count, key_value_heads, query_group, HEAD_SIZE)
    kmat = keyrows.reshape(token_count, key_value_heads, HEAD_SIZE)
    value_matrix = value_row_block.reshape(token_count, key_value_heads, HEAD_SIZE)
    output_matrix = output_gradient.reshape(token_count, key_value_heads, query_group, HEAD_SIZE)
    same = ids[:, None] == ids[None, :]
    scores = jnp.einsum("bmav,wmv->mabw", qmat, kmat, preferred_element_type=jnp.float32) * scale
    scores = jnp.where(same[None, None], scores, -1e30)
    probs = jax.nn.softmax(scores, axis=-1)
    probs_half = probs.astype(jnp.bfloat16)
    value_gradient = jnp.einsum(
        "kgtu,tkgd->ukd", probs_half, output_matrix, preferred_element_type=jnp.float32
    ).astype(jnp.bfloat16)
    probability_grad = jnp.einsum(
        "bmav,wmv->mabw", output_matrix, value_matrix, preferred_element_type=jnp.float32
    )
    row_dots = jnp.sum(probs * probability_grad, axis=-1, keepdims=True)
    score_grad = (probs * (probability_grad - row_dots) * scale).astype(jnp.bfloat16)
    query_gradient = jnp.einsum(
        "kgtu,ukd->tkgd", score_grad, kmat, preferred_element_type=jnp.float32
    ).astype(jnp.bfloat16)
    key_gradient = jnp.einsum(
        "kgtu,tkgd->ukd", score_grad, qmat, preferred_element_type=jnp.float32
    ).astype(jnp.bfloat16)
    return (
        query_gradient.reshape(token_count, -1),
        key_gradient.reshape(token_count, -1),
        value_gradient.reshape(token_count, -1),
    )


def rows_product(left, piece):
    return lax.dot_general(
        left, piece, (((1,), (1,)), ((), ())), preferred_element_type=jnp.float32
    )


def up_gradients(adapter_middle, query_gradient, key_gradient, value_gradient):
    rank = ADAPTER_RANK
    parts = []
    for place, gradient in enumerate((query_gradient, key_gradient, value_gradient)):
        parts.append(
            adapter_scale
            * lax.dot_general(
                adapter_middle[:, place * rank : (place + 1) * rank],
                gradient,
                (((0,), (0,)), ((), ())),
                preferred_element_type=jnp.float32,
            )
        )
    return parts


def general_shards(outer, inner, tensor):
    every = ("hi", "lo")

    def shards(
        normed,
        stored_queries,
        stored_keys,
        stored_values,
        head_output_grad,
        document_index,
        query_projection_weight,
        key_projection_weight,
        value_projection_weight,
        adapter_down_maps,
        query_up_map,
        key_value_up_maps,
    ):
        weights = lax.all_gather(
            jnp.concatenate(
                [query_projection_weight, key_projection_weight, value_projection_weight], axis=1
            ),
            "lo",
            axis=0,
            tiled=True,
        )
        query_gradient, key_gradient, value_gradient = attention_backward(
            stored_queries, stored_keys, stored_values, head_output_grad, document_index[0]
        )
        own = jnp.concatenate([query_gradient, key_gradient, value_gradient], axis=1)
        gathered = lax.all_gather(own, "hi", axis=0, tiled=True)
        local_middle = jnp.dot(normed, adapter_down_maps, preferred_element_type=jnp.float32)
        grad_local = jnp.concatenate(
            [
                adapter_scale * rows_product(query_gradient, query_up_map),
                adapter_scale * rows_product(key_gradient, key_value_up_maps[0]),
                adapter_scale * rows_product(value_gradient, key_value_up_maps[1]),
            ],
            axis=1,
        )
        middle_total, grad_sum = (
            lax.psum(local_middle.astype(jnp.bfloat16), "tensor").astype(jnp.float32),
            lax.psum(grad_local.astype(jnp.bfloat16), "tensor").astype(jnp.float32),
        )
        adapter_middle = middle_total.astype(jnp.bfloat16)
        middle_gradient = grad_sum.astype(jnp.bfloat16)

        down_local = lax.dot_general(
            normed, middle_gradient, (((0,), (0,)), ((), ())), preferred_element_type=jnp.float32
        )
        ups = up_gradients(adapter_middle, query_gradient, key_gradient, value_gradient)
        up_local = jnp.concatenate(ups, axis=1)
        down_piece = lax.psum_scatter(down_local, every, scatter_dimension=0, tiled=True)
        up_piece = lax.psum_scatter(up_local, every, scatter_dimension=1, tiled=True)
        down_total = lax.all_gather(down_piece, every, axis=0, tiled=True)
        up_total = lax.all_gather(up_piece, every, axis=1, tiled=True)
        q_width = query_gradient.shape[1]
        k_width = key_gradient.shape[1]
        query_total = up_total[:, :q_width]
        key_value_total = jnp.stack(
            [up_total[:, q_width : q_width + k_width], up_total[:, q_width + k_width :]]
        )

        term = rows_product(gathered, weights).astype(jnp.bfloat16)
        tokens = own.shape[0]
        block = weights.shape[0]
        summed = lax.psum_scatter(term, "tensor", scatter_dimension=1, tiled=True)
        piece = block // tensor
        moved = lax.all_to_all(
            summed.reshape(outer, tokens, piece), "hi", split_axis=0, concat_axis=0, tiled=True
        )
        moved = moved.reshape(tensor, outer // tensor, tokens, piece)
        moved = lax.all_to_all(moved, "tensor", split_axis=0, concat_axis=0, tiled=True)
        base = moved.transpose(2, 1, 0, 3).reshape(tokens, -1).astype(jnp.float32)
        normed_input_grad = (base + rows_product(middle_gradient, adapter_down_maps)).astype(
            jnp.bfloat16
        )
        return (normed_input_grad, down_total, query_total, key_value_total)

    return shards


SIZES = (4, 4, 2)
AXES = ("hi", "lo", "tensor")


def send(value, target):
    pairs = []
    for rank in range(32):
        hi, lo, core = rank // 8, rank // 2 % 4, rank % 2
        there = target(hi, lo, core)
        if there is not None:
            pairs.append((rank, there[0] * 8 + there[1] * 2 + there[2]))
    return lax.ppermute(value, AXES, pairs)


def after(value, first):
    return lax.optimization_barrier((value, first))[0]


def swap_lo(value, bit):
    return send(value, lambda hi, lo, core: (hi, lo ^ bit, core))


def swap_core(value):
    return send(value, lambda hi, lo, core: (hi, lo, 1 - core))


def move_hi(value, step, first, last):
    return send(
        value,
        lambda hi, lo, core: (hi + step, lo, core) if first <= hi <= last else None,
    )


def pick(value, index, axis):
    return lax.dynamic_index_in_dim(value, index, axis, keepdims=False)


def attention_kernel(
    query_ref, key_ref, value_ref, grad_ref, row_ids, column_ids, up_ref, key_up_ref, own_ref, middle_ref
):
    head = pl.program_id(0)
    group = query_ref.shape[1] // HEAD_SIZE
    scale = 1.0 / math.sqrt(HEAD_SIZE)
    tokens = query_ref.shape[0]

    def stacked(ref):
        return jnp.concatenate(
            [ref[:, j * HEAD_SIZE : (j + 1) * HEAD_SIZE] for j in range(group)], axis=0
        )

    def product(left, right, dims):
        return lax.dot_general(
            left, right, ((dims[:1], dims[1:]), ((), ())), preferred_element_type=jnp.float32
        )

    queries, gradients = stacked(query_ref), stacked(grad_ref)
    keys, values = key_ref[...], value_ref[...]
    same = jnp.concatenate([row_ids[...] == column_ids[...]] * group, axis=0)
    scores = jnp.where(same, product(queries, keys, (1, 1)) * scale, -1e30)
    raised = jnp.exp(scores - jnp.max(scores, axis=-1, keepdims=True))
    probs = raised / jnp.sum(raised, axis=-1, keepdims=True)
    value_gradient = product(probs.astype(jnp.bfloat16), gradients, (0, 0)).astype(jnp.bfloat16)
    prob_grad = product(gradients, values, (1, 1))
    dots = jnp.sum(probs * prob_grad, axis=-1, keepdims=True)
    score_grad = (probs * (prob_grad - dots) * scale).astype(jnp.bfloat16)
    stacked_gradient = product(score_grad, keys, (1, 0)).astype(jnp.bfloat16)
    key_gradient = product(score_grad, queries, (0, 0)).astype(jnp.bfloat16)
    query_gradient = jnp.concatenate(
        [stacked_gradient[j * tokens : (j + 1) * tokens] for j in range(group)], axis=1
    )

    count = own_ref.shape[1] // ((group + 2) * HEAD_SIZE)

    def columns(start, width):
        return pl.ds(pl.multiple_of(start, HEAD_SIZE), width)

    own_ref[:, columns(head * group * HEAD_SIZE, group * HEAD_SIZE)] = query_gradient
    own_ref[:, columns((count * group + head) * HEAD_SIZE, HEAD_SIZE)] = key_gradient
    own_ref[:, columns((count * (group + 1) + head) * HEAD_SIZE, HEAD_SIZE)] = value_gradient

    @pl.when(head == 0)
    def _():
        middle_ref[...] = jnp.zeros_like(middle_ref)

    middle_ref[...] += adapter_scale * jnp.concatenate(
        [
            product(query_gradient, up_ref[...], (1, 1)),
            product(key_gradient, key_up_ref[0], (1, 1)),
            product(value_gradient, key_up_ref[1], (1, 1)),
        ],
        axis=1,
    )


def attention(queries, keys, values, gradients, ids, query_up_map, key_value_up_maps):
    tokens, key_width = keys.shape
    heads = key_width // HEAD_SIZE
    wide = queries.shape[1] // heads
    rank = query_up_map.shape[0]
    return pl.pallas_call(
        attention_kernel,
        out_shape=(
            jax.ShapeDtypeStruct((tokens, queries.shape[1] + 2 * key_width), jnp.bfloat16),
            jax.ShapeDtypeStruct((tokens, 3 * rank), jnp.float32),
        ),
        grid=(heads,),
        in_specs=[
            pl.BlockSpec((tokens, wide), lambda h: (0, h)),
            pl.BlockSpec((tokens, HEAD_SIZE), lambda h: (0, h)),
            pl.BlockSpec((tokens, HEAD_SIZE), lambda h: (0, h)),
            pl.BlockSpec((tokens, wide), lambda h: (0, h)),
            pl.BlockSpec((tokens, 1), lambda h: (0, 0)),
            pl.BlockSpec((1, tokens), lambda h: (0, 0)),
            pl.BlockSpec((rank, wide), lambda h: (0, h)),
            pl.BlockSpec((2, rank, HEAD_SIZE), lambda h: (0, 0, h)),
        ],
        out_specs=(
            pl.BlockSpec((tokens, queries.shape[1] + 2 * key_width), lambda h: (0, 0)),
            pl.BlockSpec((tokens, 3 * rank), lambda h: (0, 0)),
        ),
        compiler_params=pltpu.CompilerParams(vmem_limit_bytes=56 << 20),
        cost_estimate=pl.CostEstimate(
            flops=10 * tokens * tokens * queries.shape[1],
            bytes_accessed=6 * tokens * queries.shape[1],
            transcendentals=tokens * tokens * queries.shape[1] // HEAD_SIZE,
        ),
        name="attention",
    )(
        queries,
        keys,
        values,
        gradients,
        ids.reshape(tokens, 1),
        ids.reshape(1, tokens),
        query_up_map,
        key_value_up_maps,
    )


def term_kernel(place_ref, *refs):
    blocks, weights, (sent_ref, kept_ref, left, arrived) = refs[:7], refs[7:-4], refs[-4:]
    tokens = blocks[0].shape[0]
    hi = place_ref[1]

    @pl.when(pl.program_id(0) == 0)
    def _():
        for n in range(4):
            there = left.at[pl.ds(n * tokens, tokens), :]
            for step, block in zip((0, 1, 2, 3, -1, -2, -3), blocks):

                @pl.when(hi == n + step)
                def _(block=block, there=there, n=n):
                    pltpu.make_async_copy(block, there, arrived.at[n]).start()

        for n in range(4):
            there = left.at[pl.ds(n * tokens, tokens), :]
            pltpu.make_async_copy(blocks[0], there, arrived.at[n]).wait()

    for turn, out_ref in enumerate((sent_ref, kept_ref)):

        @pl.when(pl.program_id(0) == turn)
        def _(out_ref=out_ref):
            width = 2 * weights[0].shape[0]
            for n in range(len(weights) // 2):
                right = jnp.concatenate([weights[2 * n][...], weights[2 * n + 1][...]], axis=0)
                out_ref[:, n * width : (n + 1) * width] = lax.dot_general(
                    left[...], right, (((1,), (1,)), ((), ())), preferred_element_type=jnp.float32
                ).astype(jnp.bfloat16)


def term_halves(blocks, weights, core, hi):
    tokens, depth = blocks[0].shape
    rows = weights[0].shape[0] // 2
    count = len(weights)
    out = jax.ShapeDtypeStruct((4 * tokens, count * rows), jnp.bfloat16)
    return pl.pallas_call(
        term_kernel,
        out_shape=(out, out),
        grid_spec=pltpu.PrefetchScalarGridSpec(
            num_scalar_prefetch=1,
            grid=(2,),
            in_specs=[pl.BlockSpec(memory_space=pl.ANY)] * 7
            + [pl.BlockSpec((rows, depth), lambda i, place: (lax.rem(place[0] + 1 - i, 2), 0))]
            * count,
            out_specs=(pl.BlockSpec(out.shape, lambda i, place: (0, 0)),) * 2,
            scratch_shapes=[
                pltpu.VMEM((4 * tokens, depth), jnp.bfloat16),
                pltpu.SemaphoreType.DMA((4,)),
            ],
        ),
        compiler_params=pltpu.CompilerParams(vmem_limit_bytes=56 << 20),
        cost_estimate=pl.CostEstimate(
            flops=16 * tokens * depth * rows * count,
            bytes_accessed=8 * tokens * depth + (4 * rows * depth + 16 * tokens * rows) * count,
            transcendentals=0,
        ),
        name="term",
    )(jnp.stack([core, hi]), *blocks, *weights)


def finish_kernel(spot_ref, added_ref, *refs):
    pieces, out_ref = refs[:-1], refs[-1]
    width = sum(piece.shape[1] for piece in pieces) // spot_ref.shape[0]
    place = 0
    for piece in pieces:
        for start in range(0, piece.shape[1], width):
            there = pl.ds(pl.multiple_of(spot_ref[place] * width, width), width)
            out_ref[:, there] = (
                piece[:, start : start + width].astype(jnp.float32) + added_ref[:, there]
            ).astype(jnp.bfloat16)
            place += 1


def finish(pieces, spots, added):
    return pl.pallas_call(
        finish_kernel,
        out_shape=jax.ShapeDtypeStruct(added.shape, jnp.bfloat16),
        in_specs=[pl.BlockSpec(memory_space=pltpu.SMEM)]
        + [pl.BlockSpec(memory_space=pltpu.VMEM)] * (1 + len(pieces)),
        out_specs=pl.BlockSpec(memory_space=pltpu.VMEM),
        compiler_params=pltpu.CompilerParams(vmem_limit_bytes=24 << 20),
        cost_estimate=pl.CostEstimate(
            flops=added.size, bytes_accessed=8 * added.size, transcendentals=0
        ),
        name="finish",
    )(spots, added, *pieces)


def pieces_kernel(middle_ref, normed_ref, own_ref, out_ref):
    rank = middle_ref.shape[1] // 2
    width = out_ref.shape[3]
    each = (out_ref.shape[2] - rank) // 16
    heads = own_ref.shape[1] // 6

    def product(left, right):
        return lax.dot_general(
            left, right, (((0,), (0,)), ((), ())), preferred_element_type=jnp.float32
        )

    turned = middle_ref[:, rank:]
    for hi in range(4):
        for lo in range(4):
            start = (hi * 4 + lo) * width
            down = product(turned, normed_ref[:, start : start + width])
            out_ref[lo, hi, :rank, :] = down.astype(jnp.bfloat16)
    for column in range(own_ref.shape[1] // width):
        which = max(column * width // heads - 3, 0)
        part = middle_ref[:, which * ADAPTER_RANK : (which + 1) * ADAPTER_RANK]
        up = adapter_scale * product(part, own_ref[:, column * width : (column + 1) * width])
        for row in range(4):
            owner, n = divmod(column * 4 + row, each)
            lo, hi = divmod(owner, 4)
            out_ref[lo, hi, rank + n * 16 : rank + (n + 1) * 16, :] = up[
                row * 16 : (row + 1) * 16
            ].astype(jnp.bfloat16)


def dp_pieces(middle, normed, own):
    rank = middle.shape[1] // 2
    width = normed.shape[1] // 16
    rows = rank + ADAPTER_RANK * own.shape[1] // (16 * width)
    return pl.pallas_call(
        pieces_kernel,
        out_shape=jax.ShapeDtypeStruct((4, 4, rows, width), jnp.bfloat16),
        in_specs=[pl.BlockSpec(memory_space=pltpu.VMEM)] * 3,
        out_specs=pl.BlockSpec(memory_space=pltpu.VMEM),
        compiler_params=pltpu.CompilerParams(vmem_limit_bytes=24 << 20),
        cost_estimate=pl.CostEstimate(
            flops=2 * normed.size * rank + 2 * own.size * ADAPTER_RANK,
            bytes_accessed=2 * (normed.size + own.size) + 32 * rows * width,
            transcendentals=0,
        ),
        name="pieces",
    )(middle, normed, own)


def results_kernel(every_ref, down_ref, query_ref, key_value_ref):
    rank = down_ref.shape[0]
    width = every_ref.shape[3]
    each = (every_ref.shape[2] - rank) // 16
    for hi in range(4):
        for lo in range(4):
            piece = every_ref[lo, hi].astype(jnp.float32)
            start = (hi * 4 + lo) * width
            down_ref[:, start : start + width] = piece[:rank]
            for n in range(each):
                part = piece[rank + n * 16 : rank + (n + 1) * 16]
                column, row = divmod((lo * 4 + hi) * each + n, 4)
                rows = slice(row * 16, (row + 1) * 16)
                column = column * width
                if column < query_ref.shape[1]:
                    query_ref[rows, column : column + width] = part
                else:
                    which, column = divmod(column - query_ref.shape[1], key_value_ref.shape[2])
                    key_value_ref[which, rows, column : column + width] = part


def dp_results(every, rank, q_width, k_width):
    width = every.shape[3]
    down_turned, query, key_value = pl.pallas_call(
        results_kernel,
        out_shape=(
            jax.ShapeDtypeStruct((rank, 16 * width), jnp.float32),
            jax.ShapeDtypeStruct((ADAPTER_RANK, q_width), jnp.float32),
            jax.ShapeDtypeStruct((2, ADAPTER_RANK, k_width), jnp.float32),
        ),
        in_specs=[pl.BlockSpec(memory_space=pltpu.VMEM)],
        out_specs=(pl.BlockSpec(memory_space=pltpu.VMEM),) * 3,
        compiler_params=pltpu.CompilerParams(vmem_limit_bytes=24 << 20),
        cost_estimate=pl.CostEstimate(
            flops=every.size, bytes_accessed=6 * every.size, transcendentals=0
        ),
        name="results",
    )(every)
    return down_turned.T, query, key_value


def scatter_sum(value, axis):
    return jnp.sum(
        lax.all_to_all(value, axis, 0, 0), axis=0, dtype=jnp.float32
    ).astype(jnp.bfloat16)


def gather(value, axis):
    return lax.all_to_all(jnp.broadcast_to(value[None], (4, *value.shape)), axis, 0, 0)


def chain_hi(own, first):
    right, left = [own], [own]
    for step in range(1, 4):
        right.append(move_hi(right[-1], 1, step - 1, 2))
        left.append(move_hi(left[-1], -1, 1, 4 - step))
        if step == 1:
            right[1], left[1] = after((right[1], left[1]), first)
    return right[1:], left[1:]


def fast_shards():
    def shards(
        normed,
        stored_queries,
        stored_keys,
        stored_values,
        head_output_grad,
        document_index,
        query_projection_weight,
        key_projection_weight,
        value_projection_weight,
        adapter_down_maps,
        query_up_map,
        key_value_up_maps,
    ):
        hi, lo, core = (lax.axis_index(name) for name in AXES)
        parts = (query_projection_weight, key_projection_weight, value_projection_weight)
        cut = query_projection_weight.shape[0] // 2
        own_a = jnp.concatenate([w[:cut] for w in parts], axis=1)
        own_b = jnp.concatenate([w[cut:] for w in parts], axis=1)
        x_a, y_a = swap_lo(own_a, 1), swap_lo(own_a, 2)
        next_b = after(own_b, (x_a, y_a))
        x_b, y_b = swap_lo(next_b, 1), swap_lo(next_b, 2)
        document_index = after(document_index, own_a)

        own, middle_part = attention(
            stored_queries,
            stored_keys,
            stored_values,
            head_output_grad,
            document_index[0],
            query_up_map,
            key_value_up_maps,
        )
        q_width = stored_queries.shape[1]
        k_width = stored_keys.shape[1]
        query_gradient = own[:, :q_width]
        key_gradient = own[:, q_width : q_width + k_width]
        value_gradient = own[:, q_width + k_width :]
        middle_local = jnp.concatenate(
            [
                jnp.dot(normed, adapter_down_maps, preferred_element_type=jnp.float32),
                middle_part,
            ],
            axis=1,
        )
        middle = (middle_local + swap_core(middle_local)).astype(jnp.bfloat16)
        rank = adapter_down_maps.shape[1]
        adapter_middle, middle_gradient = middle[:, :rank], middle[:, rank:]
        laid = dp_pieces(middle, normed, own)
        right, left = chain_hi(own, (x_a, y_a, laid))
        blocks = (own, *right, *left)
        from_a, from_b = after((x_a, y_b), (x_b, right[1], left[1]))
        weights = (own_a, own_b, x_a, x_b, y_a, y_b, swap_lo(from_a, 2), swap_lo(from_b, 1))

        column = scatter_sum(laid, "lo")
        piece = scatter_sum(after(column, (right[1], left[1])), "hi")
        tokens = own.shape[0]
        source = (hi % 2) * 2 + core

        def owner(step):
            return lambda hi, lo, core: (((hi % 2) * 2 + core + step) % 4, lo, hi // 2)

        added = rows_product(middle_gradient, adapter_down_maps)
        line = after(gather(after(piece, (right[2], left[2])), "hi"), weights[-2:])
        sent, kept = term_halves(after(blocks, line), weights, core, hi)
        summed = kept.astype(jnp.float32) + swap_core(sent).astype(jnp.float32)
        summed = summed.astype(jnp.bfloat16).reshape(4, tokens, -1)
        received = [
            send(pick(summed, (source + step) % 4, 0), owner(step)) for step in range(4)
        ]
        every = after(gather(line, "lo"), received[0])
        down_total, query_total, key_value_total = dp_results(every, rank, q_width, k_width)

        spots = [
            (((hi - step) % 4) // 2) * 16 + (lo ^ block) * 4 + part * 2 + (hi - step) % 2
            for step in range(4)
            for block in range(4)
            for part in range(2)
        ]
        normed_input_grad = finish(received, jnp.stack(spots).astype(jnp.int32), added)
        return (normed_input_grad, down_total, query_total, key_value_total)

    return shards


def solution(mesh):
    ranks = mesh.shape["dp"]
    tensor = mesh.shape["tensor"]
    inner = math.gcd(ranks, 4)
    outer = ranks // inner
    split = Mesh(mesh.devices.reshape(outer, inner, tensor), AXES)
    rows = ("hi", "lo")
    in_specs = (
        P(rows, "tensor"),
        P(rows, "tensor"),
        P(rows, "tensor"),
        P(rows, "tensor"),
        P(rows, "tensor"),
        P(rows, None),
        P(rows, "tensor"),
        P(rows, "tensor"),
        P(rows, "tensor"),
        P("tensor", None),
        P(None, "tensor"),
        P(None, None, "tensor"),
    )
    out_specs = (P(rows, "tensor"), P("tensor", None), P(None, "tensor"), P(None, None, "tensor"))
    return jax.shard_map(
        fast_shards() if (outer, inner, tensor) == SIZES else general_shards(outer, inner, tensor),
        mesh=split,
        in_specs=in_specs,
        out_specs=out_specs,
        check_vma=False,
    )
```

```python
import math

import jax
import jax.numpy as jnp
from jax import lax
from jax.experimental import pallas as pl
from jax.experimental.pallas import tpu as pltpu
from jax.sharding import Mesh
from jax.sharding import PartitionSpec as P

QUERY_HEADS = 32
KEY_HEADS = 8
HEAD_SIZE = 128
ADAPTER_RANK = 64


adapter_scale = 0.5


def attention_backward(queries, keyrows, value_row_block, output_gradient, ids):
    token_count = queries.shape[0]
    key_value_heads = keyrows.shape[1] // HEAD_SIZE
    query_group = QUERY_HEADS // KEY_HEADS
    scale = 1.0 / math.sqrt(HEAD_SIZE)
    qmat = queries.reshape(token_count, key_value_heads, query_group, HEAD_SIZE)
    kmat = keyrows.reshape(token_count, key_value_heads, HEAD_SIZE)
    value_matrix = value_row_block.reshape(token_count, key_value_heads, HEAD_SIZE)
    output_matrix = output_gradient.reshape(token_count, key_value_heads, query_group, HEAD_SIZE)
    same = ids[:, None] == ids[None, :]
    scores = jnp.einsum("bmav,wmv->mabw", qmat, kmat, preferred_element_type=jnp.float32) * scale
    scores = jnp.where(same[None, None], scores, -1e30)
    probs = jax.nn.softmax(scores, axis=-1)
    probs_half = probs.astype(jnp.bfloat16)
    value_gradient = jnp.einsum(
        "kgtu,tkgd->ukd", probs_half, output_matrix, preferred_element_type=jnp.float32
    ).astype(jnp.bfloat16)
    probability_grad = jnp.einsum(
        "bmav,wmv->mabw", output_matrix, value_matrix, preferred_element_type=jnp.float32
    )
    row_dots = jnp.sum(probs * probability_grad, axis=-1, keepdims=True)
    score_grad = (probs * (probability_grad - row_dots) * scale).astype(jnp.bfloat16)
    query_gradient = jnp.einsum(
        "kgtu,ukd->tkgd", score_grad, kmat, preferred_element_type=jnp.float32
    ).astype(jnp.bfloat16)
    key_gradient = jnp.einsum(
        "kgtu,tkgd->ukd", score_grad, qmat, preferred_element_type=jnp.float32
    ).astype(jnp.bfloat16)
    return (
        query_gradient.reshape(token_count, -1),
        key_gradient.reshape(token_count, -1),
        value_gradient.reshape(token_count, -1),
    )


def rows_product(left, piece):
    return lax.dot_general(
        left, piece, (((1,), (1,)), ((), ())), preferred_element_type=jnp.float32
    )


def up_gradients(adapter_middle, query_gradient, key_gradient, value_gradient):
    rank = ADAPTER_RANK
    parts = []
    for place, gradient in enumerate((query_gradient, key_gradient, value_gradient)):
        parts.append(
            adapter_scale
            * lax.dot_general(
                adapter_middle[:, place * rank : (place + 1) * rank],
                gradient,
                (((0,), (0,)), ((), ())),
                preferred_element_type=jnp.float32,
            )
        )
    return parts


def general_shards(outer, inner, tensor):
    every = ("hi", "lo")

    def shards(
        normed,
        stored_queries,
        stored_keys,
        stored_values,
        head_output_grad,
        document_index,
        query_projection_weight,
        key_projection_weight,
        value_projection_weight,
        adapter_down_maps,
        query_up_map,
        key_value_up_maps,
    ):
        weights = lax.all_gather(
            jnp.concatenate(
                [query_projection_weight, key_projection_weight, value_projection_weight], axis=1
            ),
            "lo",
            axis=0,
            tiled=True,
        )
        query_gradient, key_gradient, value_gradient = attention_backward(
            stored_queries, stored_keys, stored_values, head_output_grad, document_index[0]
        )
        own = jnp.concatenate([query_gradient, key_gradient, value_gradient], axis=1)
        gathered = lax.all_gather(own, "hi", axis=0, tiled=True)
        local_middle = jnp.dot(normed, adapter_down_maps, preferred_element_type=jnp.float32)
        grad_local = jnp.concatenate(
            [
                adapter_scale * rows_product(query_gradient, query_up_map),
                adapter_scale * rows_product(key_gradient, key_value_up_maps[0]),
                adapter_scale * rows_product(value_gradient, key_value_up_maps[1]),
            ],
            axis=1,
        )
        middle_total, grad_sum = (
            lax.psum(local_middle.astype(jnp.bfloat16), "tensor").astype(jnp.float32),
            lax.psum(grad_local.astype(jnp.bfloat16), "tensor").astype(jnp.float32),
        )
        adapter_middle = middle_total.astype(jnp.bfloat16)
        middle_gradient = grad_sum.astype(jnp.bfloat16)

        down_local = lax.dot_general(
            normed, middle_gradient, (((0,), (0,)), ((), ())), preferred_element_type=jnp.float32
        )
        ups = up_gradients(adapter_middle, query_gradient, key_gradient, value_gradient)
        up_local = jnp.concatenate(ups, axis=1)
        down_piece = lax.psum_scatter(down_local, every, scatter_dimension=0, tiled=True)
        up_piece = lax.psum_scatter(up_local, every, scatter_dimension=1, tiled=True)
        down_total = lax.all_gather(down_piece, every, axis=0, tiled=True)
        up_total = lax.all_gather(up_piece, every, axis=1, tiled=True)
        q_width = query_gradient.shape[1]
        k_width = key_gradient.shape[1]
        query_total = up_total[:, :q_width]
        key_value_total = jnp.stack(
            [up_total[:, q_width : q_width + k_width], up_total[:, q_width + k_width :]]
        )

        term = rows_product(gathered, weights).astype(jnp.bfloat16)
        tokens = own.shape[0]
        block = weights.shape[0]
        summed = lax.psum_scatter(term, "tensor", scatter_dimension=1, tiled=True)
        piece = block // tensor
        moved = lax.all_to_all(
            summed.reshape(outer, tokens, piece), "hi", split_axis=0, concat_axis=0, tiled=True
        )
        moved = moved.reshape(tensor, outer // tensor, tokens, piece)
        moved = lax.all_to_all(moved, "tensor", split_axis=0, concat_axis=0, tiled=True)
        base = moved.transpose(2, 1, 0, 3).reshape(tokens, -1).astype(jnp.float32)
        normed_input_grad = (base + rows_product(middle_gradient, adapter_down_maps)).astype(
            jnp.bfloat16
        )
        return (normed_input_grad, down_total, query_total, key_value_total)

    return shards


SIZES = (4, 4, 2)
AXES = ("hi", "lo", "tensor")


def send(value, target):
    pairs = []
    for rank in range(32):
        hi, lo, core = rank // 8, rank // 2 % 4, rank % 2
        there = target(hi, lo, core)
        if there is not None:
            pairs.append((rank, there[0] * 8 + there[1] * 2 + there[2]))
    return lax.ppermute(value, AXES, pairs)


def after(value, first):
    return lax.optimization_barrier((value, first))[0]


def swap_lo(value, bit):
    return send(value, lambda hi, lo, core: (hi, lo ^ bit, core))


def swap_core(value):
    return send(value, lambda hi, lo, core: (hi, lo, 1 - core))


def move_hi(value, step, first, last):
    return send(
        value,
        lambda hi, lo, core: (hi + step, lo, core) if first <= hi <= last else None,
    )


def pick(value, index, axis):
    return lax.dynamic_index_in_dim(value, index, axis, keepdims=False)


def attention_kernel(
    query_ref, key_ref, value_ref, grad_ref, row_ids, column_ids, up_ref, key_up_ref, own_ref, middle_ref
):
    head = pl.program_id(0)
    group = query_ref.shape[1] // HEAD_SIZE
    scale = 1.0 / math.sqrt(HEAD_SIZE)
    tokens = query_ref.shape[0]

    def stacked(ref):
        return jnp.concatenate(
            [ref[:, j * HEAD_SIZE : (j + 1) * HEAD_SIZE] for j in range(group)], axis=0
        )

    def product(left, right, dims):
        return lax.dot_general(
            left, right, ((dims[:1], dims[1:]), ((), ())), preferred_element_type=jnp.float32
        )

    queries, gradients = stacked(query_ref), stacked(grad_ref)
    keys, values = key_ref[...], value_ref[...]
    same = jnp.concatenate([row_ids[...] == column_ids[...]] * group, axis=0)
    scores = jnp.where(same, product(queries, keys, (1, 1)) * scale, -1e30)
    raised = jnp.exp(scores - jnp.max(scores, axis=-1, keepdims=True))
    probs = raised / jnp.sum(raised, axis=-1, keepdims=True)
    value_gradient = product(probs.astype(jnp.bfloat16), gradients, (0, 0)).astype(jnp.bfloat16)
    prob_grad = product(gradients, values, (1, 1))
    dots = jnp.sum(probs * prob_grad, axis=-1, keepdims=True)
    score_grad = (probs * (prob_grad - dots) * scale).astype(jnp.bfloat16)
    stacked_gradient = product(score_grad, keys, (1, 0)).astype(jnp.bfloat16)
    key_gradient = product(score_grad, queries, (0, 0)).astype(jnp.bfloat16)
    query_gradient = jnp.concatenate(
        [stacked_gradient[j * tokens : (j + 1) * tokens] for j in range(group)], axis=1
    )

    count = own_ref.shape[1] // ((group + 2) * HEAD_SIZE)

    def columns(start, width):
        return pl.ds(pl.multiple_of(start, HEAD_SIZE), width)

    own_ref[:, columns(head * group * HEAD_SIZE, group * HEAD_SIZE)] = query_gradient
    own_ref[:, columns((count * group + head) * HEAD_SIZE, HEAD_SIZE)] = key_gradient
    own_ref[:, columns((count * (group + 1) + head) * HEAD_SIZE, HEAD_SIZE)] = value_gradient

    @pl.when(head == 0)
    def _():
        middle_ref[...] = jnp.zeros_like(middle_ref)

    middle_ref[...] += adapter_scale * jnp.concatenate(
        [
            product(query_gradient, up_ref[...], (1, 1)),
            product(key_gradient, key_up_ref[0], (1, 1)),
            product(value_gradient, key_up_ref[1], (1, 1)),
        ],
        axis=1,
    )


def attention(queries, keys, values, gradients, ids, query_up_map, key_value_up_maps):
    tokens, key_width = keys.shape
    heads = key_width // HEAD_SIZE
    wide = queries.shape[1] // heads
    rank = query_up_map.shape[0]
    return pl.pallas_call(
        attention_kernel,
        out_shape=(
            jax.ShapeDtypeStruct((tokens, queries.shape[1] + 2 * key_width), jnp.bfloat16),
            jax.ShapeDtypeStruct((tokens, 3 * rank), jnp.float32),
        ),
        grid=(heads,),
        in_specs=[
            pl.BlockSpec((tokens, wide), lambda h: (0, h)),
            pl.BlockSpec((tokens, HEAD_SIZE), lambda h: (0, h)),
            pl.BlockSpec((tokens, HEAD_SIZE), lambda h: (0, h)),
            pl.BlockSpec((tokens, wide), lambda h: (0, h)),
            pl.BlockSpec((tokens, 1), lambda h: (0, 0)),
            pl.BlockSpec((1, tokens), lambda h: (0, 0)),
            pl.BlockSpec((rank, wide), lambda h: (0, h)),
            pl.BlockSpec((2, rank, HEAD_SIZE), lambda h: (0, 0, h)),
        ],
        out_specs=(
            pl.BlockSpec((tokens, queries.shape[1] + 2 * key_width), lambda h: (0, 0)),
            pl.BlockSpec((tokens, 3 * rank), lambda h: (0, 0)),
        ),
        compiler_params=pltpu.CompilerParams(vmem_limit_bytes=32 << 20),
        cost_estimate=pl.CostEstimate(
            flops=10 * tokens * tokens * queries.shape[1],
            bytes_accessed=6 * tokens * queries.shape[1],
            transcendentals=tokens * tokens * queries.shape[1] // HEAD_SIZE,
        ),
        name="attention",
    )(
        queries,
        keys,
        values,
        gradients,
        ids.reshape(tokens, 1),
        ids.reshape(1, tokens),
        query_up_map,
        key_value_up_maps,
    )


def term_kernel(place_ref, *refs):
    blocks, weights, (sent_ref, kept_ref, left, arrived) = refs[:7], refs[7:-4], refs[-4:]
    tokens = blocks[0].shape[0]
    hi = place_ref[1]

    @pl.when(pl.program_id(0) == 0)
    def _():
        for n in range(4):
            there = left.at[pl.ds(n * tokens, tokens), :]
            for step, block in zip((0, 1, 2, 3, -1, -2, -3), blocks):

                @pl.when(hi == n + step)
                def _(block=block, there=there, n=n):
                    pltpu.make_async_copy(block, there, arrived.at[n]).start()

        for n in range(4):
            there = left.at[pl.ds(n * tokens, tokens), :]
            pltpu.make_async_copy(blocks[0], there, arrived.at[n]).wait()

    for turn, out_ref in enumerate((sent_ref, kept_ref)):

        @pl.when(pl.program_id(0) == turn)
        def _(out_ref=out_ref):
            width = 2 * weights[0].shape[0]
            for n in range(len(weights) // 2):
                right = jnp.concatenate([weights[2 * n][...], weights[2 * n + 1][...]], axis=0)
                out_ref[:, n * width : (n + 1) * width] = lax.dot_general(
                    left[...], right, (((1,), (1,)), ((), ())), preferred_element_type=jnp.float32
                ).astype(jnp.bfloat16)


def term_halves(blocks, weights, core, hi):
    tokens, depth = blocks[0].shape
    rows = weights[0].shape[0] // 2
    count = len(weights)
    out = jax.ShapeDtypeStruct((4 * tokens, count * rows), jnp.bfloat16)
    return pl.pallas_call(
        term_kernel,
        out_shape=(out, out),
        grid_spec=pltpu.PrefetchScalarGridSpec(
            num_scalar_prefetch=1,
            grid=(2,),
            in_specs=[pl.BlockSpec(memory_space=pl.ANY)] * 7
            + [pl.BlockSpec((rows, depth), lambda i, place: (lax.rem(place[0] + 1 - i, 2), 0))]
            * count,
            out_specs=(pl.BlockSpec(out.shape, lambda i, place: (0, 0)),) * 2,
            scratch_shapes=[
                pltpu.VMEM((4 * tokens, depth), jnp.bfloat16),
                pltpu.SemaphoreType.DMA((4,)),
            ],
        ),
        compiler_params=pltpu.CompilerParams(vmem_limit_bytes=56 << 20),
        cost_estimate=pl.CostEstimate(
            flops=16 * tokens * depth * rows * count,
            bytes_accessed=8 * tokens * depth + (4 * rows * depth + 16 * tokens * rows) * count,
            transcendentals=0,
        ),
        name="term",
    )(jnp.stack([core, hi]), *blocks, *weights)


def finish_kernel(spot_ref, added_ref, *refs):
    pieces, out_ref = refs[:-1], refs[-1]
    width = sum(piece.shape[1] for piece in pieces) // spot_ref.shape[0]
    place = 0
    for piece in pieces:
        for start in range(0, piece.shape[1], width):
            there = pl.ds(pl.multiple_of(spot_ref[place] * width, width), width)
            out_ref[:, there] = (
                piece[:, start : start + width].astype(jnp.float32) + added_ref[:, there]
            ).astype(jnp.bfloat16)
            place += 1


def finish(pieces, spots, added):
    return pl.pallas_call(
        finish_kernel,
        out_shape=jax.ShapeDtypeStruct(added.shape, jnp.bfloat16),
        in_specs=[pl.BlockSpec(memory_space=pltpu.SMEM)]
        + [pl.BlockSpec(memory_space=pltpu.VMEM)] * (1 + len(pieces)),
        out_specs=pl.BlockSpec(memory_space=pltpu.VMEM),
        compiler_params=pltpu.CompilerParams(vmem_limit_bytes=24 << 20),
        cost_estimate=pl.CostEstimate(
            flops=added.size, bytes_accessed=8 * added.size, transcendentals=0
        ),
        name="finish",
    )(spots, added, *pieces)


def pieces_kernel(middle_ref, normed_ref, own_ref, out_ref):
    rank = middle_ref.shape[1] // 2
    width = out_ref.shape[3]
    each = (out_ref.shape[2] - rank) // 16
    heads = own_ref.shape[1] // 6

    def product(left, right):
        return lax.dot_general(
            left, right, (((0,), (0,)), ((), ())), preferred_element_type=jnp.float32
        )

    turned = middle_ref[:, rank:]
    for hi in range(4):
        for lo in range(4):
            start = (hi * 4 + lo) * width
            down = product(turned, normed_ref[:, start : start + width])
            out_ref[lo, hi, :rank, :] = down.astype(jnp.bfloat16)
    for column in range(own_ref.shape[1] // width):
        which = max(column * width // heads - 3, 0)
        part = middle_ref[:, which * ADAPTER_RANK : (which + 1) * ADAPTER_RANK]
        up = adapter_scale * product(part, own_ref[:, column * width : (column + 1) * width])
        for row in range(4):
            owner, n = divmod(column * 4 + row, each)
            lo, hi = divmod(owner, 4)
            out_ref[lo, hi, rank + n * 16 : rank + (n + 1) * 16, :] = up[
                row * 16 : (row + 1) * 16
            ].astype(jnp.bfloat16)


def dp_pieces(middle, normed, own):
    rank = middle.shape[1] // 2
    width = normed.shape[1] // 16
    rows = rank + ADAPTER_RANK * own.shape[1] // (16 * width)
    return pl.pallas_call(
        pieces_kernel,
        out_shape=jax.ShapeDtypeStruct((4, 4, rows, width), jnp.bfloat16),
        in_specs=[pl.BlockSpec(memory_space=pltpu.VMEM)] * 3,
        out_specs=pl.BlockSpec(memory_space=pltpu.VMEM),
        compiler_params=pltpu.CompilerParams(vmem_limit_bytes=24 << 20),
        cost_estimate=pl.CostEstimate(
            flops=2 * normed.size * rank + 2 * own.size * ADAPTER_RANK,
            bytes_accessed=2 * (normed.size + own.size) + 32 * rows * width,
            transcendentals=0,
        ),
        name="pieces",
    )(middle, normed, own)


def results_kernel(every_ref, down_ref, query_ref, key_value_ref):
    rank = down_ref.shape[0]
    width = every_ref.shape[3]
    each = (every_ref.shape[2] - rank) // 16
    for hi in range(4):
        for lo in range(4):
            piece = every_ref[lo, hi].astype(jnp.float32)
            start = (hi * 4 + lo) * width
            down_ref[:, start : start + width] = piece[:rank]
            for n in range(each):
                part = piece[rank + n * 16 : rank + (n + 1) * 16]
                column, row = divmod((lo * 4 + hi) * each + n, 4)
                rows = slice(row * 16, (row + 1) * 16)
                column = column * width
                if column < query_ref.shape[1]:
                    query_ref[rows, column : column + width] = part
                else:
                    which, column = divmod(column - query_ref.shape[1], key_value_ref.shape[2])
                    key_value_ref[which, rows, column : column + width] = part


def dp_results(every, rank, q_width, k_width):
    width = every.shape[3]
    down_turned, query, key_value = pl.pallas_call(
        results_kernel,
        out_shape=(
            jax.ShapeDtypeStruct((rank, 16 * width), jnp.float32),
            jax.ShapeDtypeStruct((ADAPTER_RANK, q_width), jnp.float32),
            jax.ShapeDtypeStruct((2, ADAPTER_RANK, k_width), jnp.float32),
        ),
        in_specs=[pl.BlockSpec(memory_space=pltpu.VMEM)],
        out_specs=(pl.BlockSpec(memory_space=pltpu.VMEM),) * 3,
        compiler_params=pltpu.CompilerParams(vmem_limit_bytes=24 << 20),
        cost_estimate=pl.CostEstimate(
            flops=every.size, bytes_accessed=6 * every.size, transcendentals=0
        ),
        name="results",
    )(every)
    return down_turned.T, query, key_value


def scatter_sum(value, axis):
    return jnp.sum(
        lax.all_to_all(value, axis, 0, 0), axis=0, dtype=jnp.float32
    ).astype(jnp.bfloat16)


def gather(value, axis):
    return lax.all_to_all(jnp.broadcast_to(value[None], (4, *value.shape)), axis, 0, 0)


def chain_hi(own, first):
    right, left = [own], [own]
    for step in range(1, 4):
        right.append(move_hi(right[-1], 1, step - 1, 2))
        left.append(move_hi(left[-1], -1, 1, 4 - step))
        if step == 1:
            right[1], left[1] = after((right[1], left[1]), first)
    return right[1:], left[1:]


def fast_shards():
    def shards(
        normed,
        stored_queries,
        stored_keys,
        stored_values,
        head_output_grad,
        document_index,
        query_projection_weight,
        key_projection_weight,
        value_projection_weight,
        adapter_down_maps,
        query_up_map,
        key_value_up_maps,
    ):
        hi, lo, core = (lax.axis_index(name) for name in AXES)
        parts = (query_projection_weight, key_projection_weight, value_projection_weight)
        cut = query_projection_weight.shape[0] // 2
        own_a = jnp.concatenate([w[:cut] for w in parts], axis=1)
        own_b = jnp.concatenate([w[cut:] for w in parts], axis=1)
        x_a, y_a = swap_lo(own_a, 1), swap_lo(own_a, 2)
        next_b = after(own_b, (x_a, y_a))
        x_b, y_b = swap_lo(next_b, 1), swap_lo(next_b, 2)
        document_index = after(document_index, own_a)

        own, middle_part = attention(
            stored_queries,
            stored_keys,
            stored_values,
            head_output_grad,
            document_index[0],
            query_up_map,
            key_value_up_maps,
        )
        q_width = stored_queries.shape[1]
        k_width = stored_keys.shape[1]
        query_gradient = own[:, :q_width]
        key_gradient = own[:, q_width : q_width + k_width]
        value_gradient = own[:, q_width + k_width :]
        middle_local = jnp.concatenate(
            [
                jnp.dot(normed, adapter_down_maps, preferred_element_type=jnp.float32),
                middle_part,
            ],
            axis=1,
        )
        middle = (middle_local + swap_core(middle_local)).astype(jnp.bfloat16)
        rank = adapter_down_maps.shape[1]
        adapter_middle, middle_gradient = middle[:, :rank], middle[:, rank:]
        laid = dp_pieces(middle, normed, own)
        right, left = chain_hi(own, (x_a, y_a, laid))
        blocks = (own, *right, *left)
        from_a, from_b = after((x_a, y_b), (x_b, right[1], left[1]))
        weights = (own_a, own_b, x_a, x_b, y_a, y_b, swap_lo(from_a, 2), swap_lo(from_b, 1))

        column = scatter_sum(laid, "lo")
        piece = scatter_sum(after(column, (right[1], left[1])), "hi")
        tokens = own.shape[0]
        source = (hi % 2) * 2 + core

        def owner(step):
            return lambda hi, lo, core: (((hi % 2) * 2 + core + step) % 4, lo, hi // 2)

        added = rows_product(middle_gradient, adapter_down_maps)
        line = after(gather(after(piece, (right[2], left[2])), "hi"), weights[-2:])
        sent, kept = term_halves(after(blocks, line), weights, core, hi)
        summed = kept.astype(jnp.float32) + swap_core(sent).astype(jnp.float32)
        summed = summed.astype(jnp.bfloat16).reshape(4, tokens, -1)
        received = [
            send(pick(summed, (source + step) % 4, 0), owner(step)) for step in range(4)
        ]
        every = after(gather(line, "lo"), received[0])
        down_total, query_total, key_value_total = dp_results(every, rank, q_width, k_width)

        spots = [
            (((hi - step) % 4) // 2) * 16 + (lo ^ block) * 4 + part * 2 + (hi - step) % 2
            for step in range(4)
            for block in range(4)
            for part in range(2)
        ]
        normed_input_grad = finish(received, jnp.stack(spots).astype(jnp.int32), added)
        return (normed_input_grad, down_total, query_total, key_value_total)

    return shards


def solution(mesh):
    ranks = mesh.shape["dp"]
    tensor = mesh.shape["tensor"]
    inner = math.gcd(ranks, 4)
    outer = ranks // inner
    split = Mesh(mesh.devices.reshape(outer, inner, tensor), AXES)
    rows = ("hi", "lo")
    in_specs = (
        P(rows, "tensor"),
        P(rows, "tensor"),
        P(rows, "tensor"),
        P(rows, "tensor"),
        P(rows, "tensor"),
        P(rows, None),
        P(rows, "tensor"),
        P(rows, "tensor"),
        P(rows, "tensor"),
        P("tensor", None),
        P(None, "tensor"),
        P(None, None, "tensor"),
    )
    out_specs = (P(rows, "tensor"), P("tensor", None), P(None, "tensor"), P(None, None, "tensor"))
    return jax.shard_map(
        fast_shards() if (outer, inner, tensor) == SIZES else general_shards(outer, inner, tensor),
        mesh=split,
        in_specs=in_specs,
        out_specs=out_specs,
        check_vma=False,
    )
```
